32 devices in a mesh: groups: 2 (over y), rows: 4 (over z), blocks: 2 (over x), cols: 2 (over core).
Axes of the slice: x: 2, y: 2, z: 4, core: 2. Of those that a mesh axis runs over, the one named last changes fastest.
Arguments:
- inputs: bfloat16 [4096, 1024], P(('groups', 'rows')), parts along dimension 0, may hold values from -6 to 6
- projection: bfloat16 [1024, 8192], P(None, ('groups', 'blocks', 'cols')), parts along dimension 1, may hold values from -0.1875 to 0.1875
- phases: bfloat16 [8192], P(('groups', 'blocks', 'cols')), parts along dimension 0, may hold values from -3.140625 to 3.140625
- inverse_blocks: float32 [4, 2048, 2048], P(('groups', 'blocks'), 'rows'), parts along dimension 0, as said below
- labels: int32 [4096], P(('groups', 'rows')), parts along dimension 0, may hold values from 0 to 999
- predictions: float32 [4096, 1000], P(('groups', 'rows'), 'cols'), parts along dimension 0, may hold values from -4 to 4
- coefficients: float32 [8192, 1000], P(('groups', 'blocks', 'rows'), 'cols'), parts along dimension 0, may hold values from -3 to 3
Outputs:
- new_coefficients: float32 [8192, 1000], P(('groups', 'blocks', 'rows'), 'cols'), parts along dimension 0
- new_predictions: float32 [4096, 1000], P(('groups', 'rows'), 'cols'), parts along dimension 0
The draws below stay inside these ranges and needn't reach their ends.
There are 2 independent parts, one for each index of `groups`. The reference program is written for one: setup_inputs(seed, part) draws one part's arguments, and reference() takes and returns one part's arrays. A program takes and returns all parts, laid end to end along the dimension named above; each array names one. Nothing has to cross between parts.
Inputs may be any that keep to these rules, and one draw needn't show every extreme that they name: `inverse_blocks`: one dense preconditioner for each feature block.
All inputs are finite; a program needn't handle non-finite values.
Results may differ from the reference program's by a relative error of at most 0.0029.
Values may be sent and summed in bfloat16 or wider, within the bound.
No kernel may reach another device: no remote copies, remote signals or barrier semaphores. Data moves between devices by JAX's collectives and lax.ppermute only.
A program may use at most 64 MiB of HBM per device.

```python
import math
import jax
import jax.numpy as jnp
from jax import lax

DIN = 1024
FB = 2048
OUT = 1000
NBLK = 2
ROWS = 2048
FEATS = 4096


def draw_inverse_blocks(key, part):
    key_diag, key_off = jax.random.split(jax.random.fold_in(key, 17))
    diagonal = jnp.exp(jax.random.uniform(key_diag, (NBLK, FB), jnp.float32, 0.0, math.log(4.0)))
    offdiag = jax.random.normal(key_off, (NBLK, FB, FB), jnp.float32)
    places = jnp.arange(FB, dtype=jnp.int32)
    identity_mat = (places[:, None] == places[None, :]).astype(jnp.float32)
    matrix = identity_mat[None, :, :] * diagonal[:, :, None] + offdiag * (0.6 / math.sqrt(FB))
    return matrix * (4.0 / ROWS)


def place_ends(result, rng, smallest, largest):
    spot = [jax.random.randint(jax.random.fold_in(rng, axis), (), 0, length) for axis, length in enumerate(result.shape)]
    longest = result.shape.index(max(result.shape))
    neighbour = spot[:longest] + [(spot[longest] + 1) % result.shape[longest]] + spot[longest + 1:]
    return result.at[tuple(spot)].set(smallest).at[tuple(neighbour)].set(largest)


def block_levels(rng, shape, pieces, low, largest):
    factor_of, own = 1.0, jax.random.fold_in(rng, 6)
    for dim, shards_of in pieces:
        draws = jnp.exp(jax.random.uniform(jax.random.fold_in(own, dim), (shards_of,), jnp.float32, low / len(pieces), largest / len(pieces)))
        factor_of = factor_of * jnp.repeat(draws, shape[dim] // shards_of).reshape([-1 if axis == dim else 1 for axis in range(len(shape))])
    return factor_of


def gaussian(own_key, extent, deviation, bound, cuts=(), kind=jnp.bfloat16):
    drawn = deviation * jax.random.normal(own_key, extent, jnp.float32)
    if cuts:
        drawn = drawn * block_levels(own_key, extent, cuts, -0.22, 0.18)
    return jnp.clip(drawn, -bound, bound).astype(kind)


def setup_inputs(seed: int = 0, part: int = 0) -> dict:
    key_of = jax.random.split(jax.random.key(seed), 8)
    part_splits = jax.random.split(jax.random.fold_in(key_of[7], part), 8)
    return {
        "inputs": gaussian(part_splits[0], (ROWS, DIN), 1.0, 6.0, ((0, 4),)),
        "projection": gaussian(part_splits[1], (DIN, FEATS), DIN ** -0.5, 0.1875, ((1, 4),)),
        "phases": jnp.clip(jax.random.uniform(part_splits[2], (FEATS,), jnp.float32, -3.140625, 3.140625), -3.140625, 3.140625).astype(jnp.bfloat16),
        "inverse_blocks": draw_inverse_blocks(jax.random.fold_in(jax.random.fold_in(key_of[7], part), 71), part),
        "labels": place_ends(jax.random.randint(part_splits[4], (ROWS,), 0, OUT), jax.random.fold_in(part_splits[4], 1), 0, OUT - 1).astype(jnp.int32),
        "predictions": gaussian(part_splits[5], (ROWS, OUT), 0.5, 4.0, ((0, 4), (1, 2)), jnp.float32),
        "coefficients": gaussian(part_splits[6], (FEATS, OUT), 0.3, 3.0, ((0, 8), (1, 2)), jnp.float32),
    }


DAMPING = 0.5


def reference(inputs, projection, phases, inverse_blocks, labels, predictions, coefficients):
    onehot = (labels[:, None] == jnp.arange(OUT, dtype=jnp.int32)[None, :]).astype(jnp.float32)
    residual = (onehot - predictions).astype(jnp.bfloat16)

    def sweep_block(running, block_index):
        offset = (block_index * FB).astype(jnp.int32)
        proj_block = lax.dynamic_slice_in_dim(projection, offset, FB, 1)
        phase_block = lax.dynamic_slice_in_dim(phases, offset, FB, 0).astype(jnp.float32)
        angles = jnp.dot(inputs, proj_block, preferred_element_type=jnp.float32) + phase_block[None, :]
        features = jnp.cos(angles).astype(jnp.bfloat16)
        gradient = lax.dot_general(features, residual, (((0,), (0,)), ((), ())), preferred_element_type=jnp.float32)
        update = DAMPING * jnp.dot(inverse_blocks[block_index], gradient, precision=lax.Precision.HIGHEST)
        change = jnp.dot(features, update.astype(jnp.bfloat16), preferred_element_type=jnp.float32)
        return running + change, update

    accumulated, updates = lax.scan(sweep_block, jnp.zeros((ROWS, OUT), jnp.float32), jnp.arange(NBLK, dtype=jnp.int32))
    new_coefficients = coefficients + updates.reshape(NBLK * FB, OUT)
    new_predictions = predictions + accumulated
    return (new_coefficients, new_predictions)
```

```python
import functools

import jax
import jax.numpy as jnp
from jax import lax
from jax.experimental import pallas as pl
from jax.experimental.pallas import tpu as pltpu
from jax.sharding import PartitionSpec as P

DAMPING = 0.5
F32, BF16 = jnp.float32, jnp.bfloat16
LANES = 128

COS_TERMS = (
    0.9999999887556631, -0.49999988843399, 0.04166648574334225, -0.001388778673619495,
    2.4769518189949842e-05, -2.7075418374484127e-07, 1.7231808612122658e-09,
)
INV_TWO_PI = 0.15915494309189535
TWO_PI_HIGH = 6.28125
TWO_PI_LOW = 0.0019353071795864769


def cosine(angles):
    turns = jnp.round(angles * INV_TWO_PI)
    rest = (angles - turns * TWO_PI_HIGH) - turns * TWO_PI_LOW
    square = rest * rest
    result = jnp.full_like(square, COS_TERMS[-1])
    for term in COS_TERMS[-2::-1]:
        result = result * square + term
    return result


def dot(a, b):
    return jnp.dot(a, b, preferred_element_type=F32)


def dot_nt(a, b):
    return lax.dot_general(a, b, (((1,), (1,)), ((), ())), preferred_element_type=F32)


def params(n_grid, vmem_mib=48):
    return pltpu.CompilerParams(
        dimension_semantics=("arbitrary",) * n_grid, vmem_limit_bytes=vmem_mib << 20
    )


def residual_kernel(place, labels, predictions, out, wide):
    width = predictions.shape[1]
    wide[...] = jnp.zeros_like(wide)
    wide[:, :width] = predictions[...]
    flipped = wide[...].T
    classes = lax.broadcasted_iota(jnp.int32, flipped.shape, 0)
    hit = (classes + place[2] * width == labels[0]).astype(F32)
    out[...] = jnp.where(classes < width, hit - flipped, 0.0).astype(BF16)


def residual_block(place, labels, predictions, padded, rows):
    width = predictions.shape[1]
    part = rows // 2
    pick = lambda j, p: 2 * p[1] + (j ^ p[2])
    return pl.pallas_call(
        residual_kernel,
        out_shape=jax.ShapeDtypeStruct((padded, rows), BF16),
        grid_spec=pltpu.PrefetchScalarGridSpec(
            num_scalar_prefetch=1,
            grid=(2,),
            in_specs=[
                pl.BlockSpec((1, 1, part), lambda j, p: (pick(j, p), 0, 0)),
                pl.BlockSpec((part, width), lambda j, p: (pick(j, p), 0)),
            ],
            out_specs=pl.BlockSpec((padded, part), lambda j, p: (0, j)),
            scratch_shapes=[pltpu.VMEM((part, padded), F32)],
        ),
        compiler_params=params(1),
        name="residual",
    )(place, labels.reshape(-1, 1, part), predictions)


def features_kernel(n_rows, tiles, place, *refs):
    rows, (w_own, w_other, p_own, p_other, out) = refs[:n_rows], refs[n_rows:]
    step = pl.program_id(0)

    def body(weights, phases):
        start = 0
        for ref in rows:
            angles = dot(ref[...], weights[...]) + phases[...].astype(F32)
            out[start:start + ref.shape[0], :] = cosine(angles).astype(BF16)
            start += ref.shape[0]

    @pl.when(step < tiles)
    def _():
        body(w_own, p_own)

    @pl.when(step >= tiles)
    def _():
        body(w_other, p_other)


def features(place, rows, weights, phases, tile=512):
    depth, half = weights[0].shape
    tiles = half // tile
    total = sum(r.shape[0] for r in rows)
    own = lambda i, p: (0, jnp.minimum(i, tiles - 1))
    other = lambda i, p: (0, jnp.maximum(i - tiles, 0))

    def where(i, p):
        second = (i >= tiles).astype(jnp.int32)
        return (0, (p[2] ^ second) * tiles + (i - second * tiles))

    return pl.pallas_call(
        functools.partial(features_kernel, len(rows), tiles),
        out_shape=jax.ShapeDtypeStruct((total, 2 * half), BF16),
        grid_spec=pltpu.PrefetchScalarGridSpec(
            num_scalar_prefetch=1,
            grid=(2 * tiles,),
            in_specs=[pl.BlockSpec(r.shape, lambda i, p: (0, 0)) for r in rows]
            + [
                pl.BlockSpec((depth, tile), own),
                pl.BlockSpec((depth, tile), other),
                pl.BlockSpec((1, tile), own),
                pl.BlockSpec((1, tile), other),
            ],
            out_specs=pl.BlockSpec((total, tile), where),
        ),
        compiler_params=params(1),
        name="features",
    )(place, *rows, *weights, *phases)


def joined(pieces, part):
    sides = [[r[:, i * part:(i + 1) * part] for r in pieces] for i in (0, 1)]
    return [s[0] if len(s) == 1 else jnp.concatenate(s, axis=1) for s in sides]


def gradient_of(groups, refs, part):
    total, at = None, 0
    for count, stacked in groups:
        pieces = [refs[at + i][...] for i in range(count)]
        if stacked:
            pieces = [jnp.concatenate(pieces, axis=0)]
        first, second = joined(pieces, part)
        mine, theirs = refs[at + count][...], refs[at + count + 1][...]
        at += count + 2
        if first.shape[1] < 256:
            products = [dot(jnp.concatenate([first, second], axis=1), jnp.concatenate([mine, theirs], axis=0))]
        else:
            products = [dot(first, mine), dot(second, theirs)]
        for product in products:
            total = product if total is None else total + product
    return total


def flat(groups):
    return [a for pieces, mine, theirs in groups for a in (*pieces, mine, theirs)]


def shape_of(groups, stacked):
    return [(len(g[0]), s) for g, s in zip(groups, stacked)]


def group_specs(groups, tile):
    specs = []
    for pieces, mine, theirs in groups:
        specs += [pl.BlockSpec(r.shape, lambda k: (0, 0)) for r in pieces]
        specs += [pl.BlockSpec((f.shape[0], tile), lambda k: (0, k)) for f in (mine, theirs)]
    return specs


def gradient_kernel(form, part, *refs):
    refs[-1][...] = gradient_of(form, refs[:-1], part)


def gradient(groups, stacked, part, padded, tile=512):
    n_feat = groups[0][1].shape[1]
    return pl.pallas_call(
        functools.partial(gradient_kernel, shape_of(groups, stacked), part),
        out_shape=jax.ShapeDtypeStruct((padded, n_feat), F32),
        grid=(n_feat // tile,),
        in_specs=group_specs(groups, tile),
        out_specs=pl.BlockSpec((padded, tile), lambda k: (0, k)),
        compiler_params=params(1),
        name="gradient",
    )(*flat(groups))


def high_low(x):
    high = x.astype(BF16)
    return high, (x - high.astype(F32)).astype(BF16)


def solve_kernel(form, part, *refs):
    *pieces, partial_gradient, inverse, coefficients, new, sent, total = refs
    k = pl.program_id(0)
    g_high, g_low = high_low(partial_gradient[...] + gradient_of(form, pieces, part))
    p_high, p_low = high_low(inverse[...])
    product = dot_nt(p_high, g_high) + (dot_nt(p_low, g_high) + dot_nt(p_high, g_low))

    @pl.when(k == 0)
    def _():
        total[...] = product

    @pl.when(k > 0)
    def _():
        total[...] += product

    @pl.when(k == pl.num_programs(0) - 1)
    def _():
        update = DAMPING * total[...]
        new[...] = coefficients[...] + update[:, :new.shape[1]]
        sent[...] = update.astype(BF16)


def solve(groups, stacked, part, partial_gradient, inverse, coefficients, tile=512):
    padded, n_feat = partial_gradient.shape
    slice_rows, width = coefficients.shape
    return pl.pallas_call(
        functools.partial(solve_kernel, shape_of(groups, stacked), part),
        out_shape=(
            jax.ShapeDtypeStruct((slice_rows, width), F32),
            jax.ShapeDtypeStruct((slice_rows, padded), BF16),
        ),
        grid=(n_feat // tile,),
        in_specs=group_specs(groups, tile)
        + [
            pl.BlockSpec((padded, tile), lambda k: (0, k)),
            pl.BlockSpec((slice_rows, tile), lambda k: (0, k)),
            pl.BlockSpec((slice_rows, width), lambda k: (0, 0)),
        ],
        out_specs=(
            pl.BlockSpec((slice_rows, width), lambda k: (0, 0)),
            pl.BlockSpec((slice_rows, padded), lambda k: (0, 0)),
        ),
        scratch_shapes=[pltpu.VMEM((slice_rows, padded), F32)],
        compiler_params=params(1),
        name="solve",
    )(*flat(groups), partial_gradient, inverse, coefficients)


def change(body, place, mine, theirs, sent, received, out_shapes, name):
    depth = sent.shape[0]
    own_slice = lambda i, p: (0, p[0])
    whole = lambda i, p: (0, 0)

    def kernel(place, *refs):
        body(*refs)

    return pl.pallas_call(
        kernel,
        out_shape=tuple(jax.ShapeDtypeStruct(s, BF16) for s in out_shapes),
        grid_spec=pltpu.PrefetchScalarGridSpec(
            num_scalar_prefetch=1,
            grid=(1,),
            in_specs=[pl.BlockSpec((f.shape[0], depth), own_slice) for f in (mine, theirs)]
            + [pl.BlockSpec(a.shape, whole) for a in (sent, *received)],
            out_specs=tuple(pl.BlockSpec(s, whole) for s in out_shapes),
        ),
        compiler_params=params(1),
        name=name,
    )(place, mine, theirs, sent, *received)


def far_body(mine, theirs, sent, a, b):
    a[...] = dot(mine[...], sent[...]).astype(BF16)
    b[...] = dot(theirs[...], sent[...]).astype(BF16)


def third_body(mine, theirs, sent, in_e, in_o, out_e, out_o):
    part = in_e.shape[0]
    mine, theirs = dot(mine[...], sent[...]), dot(theirs[...], sent[...])
    out_e[:part] = mine[:part].astype(BF16)
    out_e[part:] = (theirs[:part] + in_o[...].astype(F32)).astype(BF16)
    out_o[:part] = (mine[part:] + in_e[...].astype(F32)).astype(BF16)
    out_o[part:] = theirs[part:].astype(BF16)


def middle_body(mine, theirs, sent, in_e, in_o, out_e, out_o):
    part = in_e.shape[0] // 2
    mine, theirs = dot(mine[...], sent[...]), dot(theirs[...], sent[...])
    came_e, came_o = in_e[...].astype(F32), in_o[...].astype(F32)
    out_e[:part] = (mine[:part] + came_e[:part]).astype(BF16)
    out_e[part:] = (theirs[:part] + came_e[part:]).astype(BF16)
    out_o[:part] = (mine[part:] + came_o[:part]).astype(BF16)
    out_o[part:] = (theirs[part:] + came_o[part:]).astype(BF16)


def last_body(mine, theirs, sent, in_e, in_o, out):
    part = mine.shape[0]
    came = in_e[...].astype(F32) + in_o[...].astype(F32)
    out[:part] = (dot(mine[...], sent[...]) + came[:part]).astype(BF16)
    out[part:] = (dot(theirs[...], sent[...]) + came[part:]).astype(BF16)


def apply_kernel(place, predictions, own, other, new):
    width = new.shape[1]
    mine = pl.program_id(0) // 2 == place[1]

    @pl.when(mine)
    def _():
        new[...] = predictions[...] + own[:, :width].astype(F32)

    @pl.when(jnp.logical_not(mine))
    def _():
        new[...] = predictions[...] + other[:, :width].astype(F32)


def apply_change(place, predictions, own, other):
    rows, width = predictions.shape
    part = rows // 4
    whole = lambda i, p: (i, 0)
    source = lambda i, p: ((i % 2) ^ p[2], 0)
    return pl.pallas_call(
        apply_kernel,
        out_shape=jax.ShapeDtypeStruct((rows, width), F32),
        grid_spec=pltpu.PrefetchScalarGridSpec(
            num_scalar_prefetch=1,
            grid=(4,),
            in_specs=[
                pl.BlockSpec((part, width), whole),
                pl.BlockSpec((part, own.shape[1]), source),
                pl.BlockSpec((part, own.shape[1]), source),
            ],
            out_specs=pl.BlockSpec((part, width), whole),
        ),
        compiler_params=params(1),
        name="apply",
    )(place, predictions, own, other)


def swap(x, axes, pairs):
    return lax.ppermute(x, axes, [p for a, b in pairs for p in ((a, b), (b, a))])


def ring_shards(n_rows, inputs, projection, phases, inverse_blocks, labels, predictions, coefficients):
    ring = [2 * z for z in range(n_rows)] + [2 * z + 1 for z in reversed(range(n_rows))]
    size = len(ring)
    even = [(ring[i], ring[i + 1]) for i in range(0, size, 2)]
    odd = [(ring[i], ring[(i + 1) % size]) for i in range(1, size, 2)]
    E = lambda x: swap(x, ("rows", "blocks"), even)
    O = lambda x: swap(x, ("rows", "blocks"), odd)
    C = lambda x: swap(x, "cols", [(0, 1)])

    z, x, c = (lax.axis_index(a) for a in ("rows", "blocks", "cols"))
    place = jnp.stack([z, x, c]).astype(jnp.int32)
    local_rows, width = predictions.shape
    part = local_rows // 4
    padded = -(-width // LANES) * LANES

    weights = (projection, C(projection))
    phases = phases[None, :]
    phases = (phases, C(phases))

    x0 = lax.dynamic_slice_in_dim(inputs, (2 * x + c) * part, part, 0)
    r0 = residual_block(place, labels, predictions, padded, 2 * part)

    def around(own):
        half = own.shape[0] // 2
        e1, o1 = E(own), O(own)
        e2, o2 = E(o1), O(e1)
        e3, o3 = E(o2), O(e2)
        e4, o4 = E(o3[:half]), O(e3[half:])
        return (e1, o1), (e2, o2), (e3, o3), (e4, o4)

    xs = ((x0,),) + around(x0)
    rs = ((r0,),) + around(r0)
    groups = []
    for rows_in, residual_in in zip(xs, rs):
        mine = features(place, rows_in, weights, phases)
        groups.append((residual_in, mine, C(mine)))
    partial_gradient = gradient(groups[:3], (False,) * 3, part, padded)
    new_coefficients, sent = solve(
        groups[3:], (False, True), part, partial_gradient, inverse_blocks[0], coefficients
    )

    step = lambda body, k, received, shapes, name: change(
        body, place, groups[k][1], groups[k][2], sent, received, shapes, name
    )
    piece, block = (part, padded), (2 * part, padded)
    a4, b4 = step(far_body, 4, (), (piece, piece), "far")
    e3, o3 = step(third_body, 3, (E(a4), O(b4)), (block, block), "third")
    e2, o2 = step(middle_body, 2, (O(o3), E(e3)), (block, block), "second")
    e1, o1 = step(middle_body, 1, (O(o2), E(e2)), (block, block), "first")
    (own,) = step(last_body, 0, (E(e1), O(o1)), (block,), "last")
    other = swap(own, "blocks", [(0, 1)])
    return new_coefficients, apply_change(place, predictions, own, other)


def plain_shards(inputs, projection, phases, inverse_blocks, labels, predictions, coefficients):
    out_width = predictions.shape[1]
    classes = lax.axis_index("cols") * out_width + jnp.arange(out_width, dtype=jnp.int32)
    onehot = (labels[:, None] == classes[None, :]).astype(F32)
    residual = (onehot - predictions).astype(BF16)
    angles = dot(inputs, projection) + phases.astype(F32)[None, :]
    half_features = jnp.cos(angles).astype(BF16)
    features_full = lax.all_gather(half_features, "cols", axis=1, tiled=True)
    own_gradient = lax.psum_scatter(
        lax.dot_general(features_full, residual, (((0,), (0,)), ((), ())), preferred_element_type=F32),
        "rows", scatter_dimension=0, tiled=True,
    )
    gradient_full = lax.all_gather(own_gradient, "rows", axis=0, tiled=True)
    update = DAMPING * jnp.dot(inverse_blocks[0], gradient_full, precision=lax.Precision.HIGHEST)
    sent = lax.all_gather(update.astype(BF16), "rows", axis=0, tiled=True)
    summed = lax.psum(dot(features_full, sent), "blocks")
    return coefficients + update, predictions + summed


def solution(mesh):
    n_rows, n_blocks = mesh.shape["rows"], mesh.shape["blocks"]
    small_ring = n_blocks == 2 and n_rows == 4 and mesh.shape["cols"] == 2
    shards = functools.partial(ring_shards, n_rows) if small_ring else plain_shards
    return jax.shard_map(
        shards,
        mesh=mesh,
        in_specs=(
            P(("groups", "rows"), None),
            P(None, ("groups", "blocks", "cols")),
            P(("groups", "blocks", "cols")),
            P(("groups", "blocks"), "rows", None),
            P(("groups", "rows")),
            P(("groups", "rows"), "cols"),
            P(("groups", "blocks", "rows"), "cols"),
        ),
        out_specs=(P(("groups", "blocks", "rows"), "cols"), P(("groups", "rows"), "cols")),
        check_vma=False,
    )
```

```python
import functools

import jax
import jax.numpy as jnp
from jax import lax
from jax.experimental import pallas as pl
from jax.experimental.pallas import tpu as pltpu
from jax.sharding import PartitionSpec as P

DAMPING = 0.5
F32, BF16 = jnp.float32, jnp.bfloat16
LANES = 128

COS_TERMS = (
    0.9999999887556631, -0.49999988843399, 0.04166648574334225, -0.001388778673619495,
    2.4769518189949842e-05, -2.7075418374484127e-07, 1.7231808612122658e-09,
)
INV_TWO_PI = 0.15915494309189535
TWO_PI_HIGH = 6.28125
TWO_PI_LOW = 0.0019353071795864769


def cosine(angles):
    turns = jnp.round(angles * INV_TWO_PI)
    rest = (angles - turns * TWO_PI_HIGH) - turns * TWO_PI_LOW
    square = rest * rest
    result = jnp.full_like(square, COS_TERMS[-1])
    for term in COS_TERMS[-2::-1]:
        result = result * square + term
    return result


def dot(a, b):
    return jnp.dot(a, b, preferred_element_type=F32)


def dot_nt(a, b):
    return lax.dot_general(a, b, (((1,), (1,)), ((), ())), preferred_element_type=F32)


def call(kernel, out_shapes, place, args, name, vmem_mib=56):
    vmem = pl.BlockSpec(memory_space=pltpu.VMEM)
    single = isinstance(out_shapes, jax.ShapeDtypeStruct)
    return pl.pallas_call(
        kernel,
        out_shape=out_shapes,
        in_specs=[pl.BlockSpec(memory_space=pltpu.SMEM)] + [vmem] * len(args),
        out_specs=vmem if single else (vmem,) * len(out_shapes),
        compiler_params=pltpu.CompilerParams(vmem_limit_bytes=vmem_mib << 20),
        name=name,
    )(place, *args)


def like(shape, dtype=BF16):
    return jax.ShapeDtypeStruct(tuple(shape), dtype)


def lanes(index, size):
    return pl.ds(pl.multiple_of(index * size, size), size)


def residual_kernel(place, labels, predictions, out):
    width = predictions.shape[0]
    part = out.shape[1] // 2
    out[...] = jnp.zeros_like(out)
    for j in (0, 1):
        own = lanes(2 * place[1] + (place[2] ^ j), part)
        classes = lax.broadcasted_iota(jnp.int32, (width, part), 0) + place[2] * width
        hit = (classes == labels[:, own]).astype(F32)
        out[:width, j * part:(j + 1) * part] = (hit - predictions[:, own]).astype(BF16)


def features_kernel(n_rows, place, *refs):
    rows, (w_own, w_other, p_own, p_other, out) = refs[:n_rows], refs[n_rows:]
    inputs = rows[0][...] if n_rows == 1 else jnp.concatenate([r[...] for r in rows], axis=0)
    half = w_own.shape[1]
    for i, (weights, phases) in enumerate(((w_own, p_own), (w_other, p_other))):
        angles = dot(inputs, weights[...]) + phases[...].astype(F32)
        out[:, lanes(place[2] ^ i, half)] = cosine(angles).astype(BF16)


def features(place, rows, weights, phases):
    total = sum(r.shape[0] for r in rows)
    return call(
        functools.partial(features_kernel, len(rows)),
        like((total, 2 * weights[0].shape[1])), place, (*rows, *weights, *phases), "features",
    )


def joined(pieces, part):
    sides = [[r[:, i * part:(i + 1) * part] for r in pieces] for i in (0, 1)]
    return [s[0] if len(s) == 1 else jnp.concatenate(s, axis=1) for s in sides]


def gradient_of(groups, refs, part, at_features):
    total, at = None, 0
    for count, stacked in groups:
        pieces = [refs[at + i][...] for i in range(count)]
        if stacked:
            pieces = [jnp.concatenate(pieces, axis=0)]
        first, second = joined(pieces, part)
        mine, theirs = refs[at + count][:, at_features], refs[at + count + 1][:, at_features]
        at += count + 2
        if first.shape[1] < 256:
            products = [dot(jnp.concatenate([first, second], axis=1), jnp.concatenate([mine, theirs], axis=0))]
        else:
            products = [dot(first, mine), dot(second, theirs)]
        for product in products:
            total = product if total is None else total + product
    return total


def flat(groups):
    return [a for pieces, mine, theirs in groups for a in (*pieces, mine, theirs)]


def shape_of(groups, stacked):
    return [(len(g[0]), s) for g, s in zip(groups, stacked)]


TILE = 512


def gradient_kernel(form, part, earlier, place, *refs):
    *pieces, out = refs
    for k in range(0, out.shape[1], TILE):
        at = slice(k, k + TILE)
        total = gradient_of(form, pieces[earlier:], part, at)
        out[:, at] = pieces[0][:, at] + total if earlier else total


def gradient(place, groups, stacked, part, padded, earlier=()):
    n_feat = groups[0][1].shape[1]
    return call(
        functools.partial(gradient_kernel, shape_of(groups, stacked), part, len(earlier)),
        like((padded, n_feat), F32), place, (*earlier, *flat(groups)), "gradient",
    )


def high_low(x):
    high = x.astype(BF16)
    return high, (x - high.astype(F32)).astype(BF16)


def solve_kernel(form, part, place, *refs):
    *pieces, partial_gradient, inverse, coefficients, new, sent = refs
    total = None
    for k in range(0, inverse.shape[1], TILE):
        at = slice(k, k + TILE)
        g_high, g_low = high_low(partial_gradient[:, at] + gradient_of(form, pieces, part, at))
        p_high, p_low = high_low(inverse[:, at])
        product = dot_nt(g_high, p_high) + (dot_nt(g_high, p_low) + dot_nt(g_low, p_high))
        total = product if total is None else total + product
    update = DAMPING * total
    new[...] = coefficients[...] + update[:new.shape[0]]
    sent[...] = update.astype(BF16)


def solve(place, groups, stacked, part, partial_gradient, inverse, coefficients):
    outs = (like(coefficients.shape, F32), like((partial_gradient.shape[0], coefficients.shape[1])))
    return call(
        functools.partial(solve_kernel, shape_of(groups, stacked), part),
        outs, place, (*flat(groups), partial_gradient, inverse, coefficients), "solve",
    )


def own_change(place, sent, features_ref):
    depth = sent.shape[1]
    return dot_nt(sent[...], features_ref[:, lanes(place[0], depth)])


def far_kernel(place, sent, mine, theirs, a, b):
    a[...] = own_change(place, sent, mine).astype(BF16)
    b[...] = own_change(place, sent, theirs).astype(BF16)


def third_kernel(place, sent, mine, theirs, in_e, in_o, out_e, out_o):
    part = in_e.shape[1]
    mine, theirs = own_change(place, sent, mine), own_change(place, sent, theirs)
    out_e[:, :part] = mine[:, :part].astype(BF16)
    out_e[:, part:] = (theirs[:, :part] + in_o[...].astype(F32)).astype(BF16)
    out_o[:, :part] = (mine[:, part:] + in_e[...].astype(F32)).astype(BF16)
    out_o[:, part:] = theirs[:, part:].astype(BF16)


def middle_kernel(place, sent, mine, theirs, in_e, in_o, out_e, out_o):
    part = in_e.shape[1] // 2
    for i, own in enumerate((mine, theirs)):
        own = own_change(place, sent, own)
        at = slice(i * part, (i + 1) * part)
        out_e[:, at] = (own[:, :part] + in_e[:, at].astype(F32)).astype(BF16)
        out_o[:, at] = (own[:, part:] + in_o[:, at].astype(F32)).astype(BF16)


def last_kernel(place, sent, mine, theirs, in_e, in_o, out):
    part = in_e.shape[1] // 2
    for i, own in enumerate((mine, theirs)):
        at = slice(i * part, (i + 1) * part)
        came = in_e[:, at].astype(F32) + in_o[:, at].astype(F32)
        out[:, at] = (own_change(place, sent, own) + came).astype(BF16)


def apply_kernel(place, predictions, own, other, new):
    width, part = new.shape[0], own.shape[1] // 2
    for i, source in enumerate((own, other)):
        for j in (0, 1):
            at = lanes(2 * (place[1] ^ i) + (place[2] ^ j), part)
            new[:, at] = predictions[:, at] + source[:width, j * part:(j + 1) * part].astype(F32)


def swap(x, axes, pairs):
    return lax.ppermute(x, axes, [p for a, b in pairs for p in ((a, b), (b, a))])


def ring_shards(n_rows, inputs, projection, phases, inverse_blocks, labels, predictions, coefficients):
    ring = [2 * z for z in range(n_rows)] + [2 * z + 1 for z in reversed(range(n_rows))]
    size = len(ring)
    even = [(ring[i], ring[i + 1]) for i in range(0, size, 2)]
    odd = [(ring[i], ring[(i + 1) % size]) for i in range(1, size, 2)]
    E = lambda x: swap(x, ("rows", "blocks"), even)
    O = lambda x: swap(x, ("rows", "blocks"), odd)
    C = lambda x: swap(x, "cols", [(0, 1)])

    z, x, c = (lax.axis_index(a) for a in ("rows", "blocks", "cols"))
    place = jnp.stack([z, x, c]).astype(jnp.int32)
    local_rows, width = predictions.shape
    part = local_rows // 4
    padded = -(-width // LANES) * LANES

    weights = (projection, C(projection))
    phases = phases[None, :]
    phases = (phases, C(phases))
    predictions, coefficients = predictions.T, coefficients.T

    x0 = lax.dynamic_slice_in_dim(inputs, (2 * x + c) * part, part, 0)
    r0 = call(
        residual_kernel, like((padded, 2 * part)), place, (labels[None, :], predictions), "residual"
    )

    def around(own):
        half = own.shape[0] // 2
        e1, o1 = E(own), O(own)
        e2, o2 = E(o1), O(e1)
        e3, o3 = E(o2), O(e2)
        e4, o4 = E(o3[:half]), O(e3[half:])
        return (e1, o1), (e2, o2), (e3, o3), (e4, o4)

    xs = ((x0,),) + around(x0)
    rs = ((r0,),) + around(r0)
    groups = []
    for rows_in, residual_in in zip(xs, rs):
        mine = features(place, rows_in, weights, phases)
        groups.append((residual_in, mine, C(mine)))
    first = gradient(place, groups[:3], (False,) * 3, part, padded)
    first = gradient(place, groups[3:4], (False,), part, padded, (first,))
    new_coefficients, sent = solve(place, groups[4:], (True,), part, first, inverse_blocks[0], coefficients)

    def step(kernel, k, received, shapes, name):
        return call(kernel, tuple(like(s) for s in shapes), place, (sent, *groups[k][1:], *received), name)

    piece, block = (padded, part), (padded, 2 * part)
    a4, b4 = step(far_kernel, 4, (), (piece, piece), "far")
    e3, o3 = step(third_kernel, 3, (E(a4), O(b4)), (block, block), "third")
    e2, o2 = step(middle_kernel, 2, (O(o3), E(e3)), (block, block), "second")
    e1, o1 = step(middle_kernel, 1, (O(o2), E(e2)), (block, block), "first")
    (own,) = step(last_kernel, 0, (E(e1), O(o1)), (block,), "last")
    other = swap(own, "blocks", [(0, 1)])
    new = call(apply_kernel, like(predictions.shape, F32), place, (predictions, own, other), "apply")
    return new_coefficients.T, new.T


def plain_shards(inputs, projection, phases, inverse_blocks, labels, predictions, coefficients):
    out_width = predictions.shape[1]
    classes = lax.axis_index("cols") * out_width + jnp.arange(out_width, dtype=jnp.int32)
    onehot = (labels[:, None] == classes[None, :]).astype(F32)
    residual = (onehot - predictions).astype(BF16)
    angles = dot(inputs, projection) + phases.astype(F32)[None, :]
    half_features = jnp.cos(angles).astype(BF16)
    features_full = lax.all_gather(half_features, "cols", axis=1, tiled=True)
    own_gradient = lax.psum_scatter(
        lax.dot_general(features_full, residual, (((0,), (0,)), ((), ())), preferred_element_type=F32),
        "rows", scatter_dimension=0, tiled=True,
    )
    gradient_full = lax.all_gather(own_gradient, "rows", axis=0, tiled=True)
    update = DAMPING * jnp.dot(inverse_blocks[0], gradient_full, precision=lax.Precision.HIGHEST)
    sent = lax.all_gather(update.astype(BF16), "rows", axis=0, tiled=True)
    summed = lax.psum(dot(features_full, sent), "blocks")
    return coefficients + update, predictions + summed


def solution(mesh):
    n_rows, n_blocks = mesh.shape["rows"], mesh.shape["blocks"]
    small_ring = n_blocks == 2 and n_rows == 4 and mesh.shape["cols"] == 2
    shards = functools.partial(ring_shards, n_rows) if small_ring else plain_shards
    return jax.shard_map(
        shards,
        mesh=mesh,
        in_specs=(
            P(("groups", "rows"), None),
            P(None, ("groups", "blocks", "cols")),
            P(("groups", "blocks", "cols")),
            P(("groups", "blocks"), "rows", None),
            P(("groups", "rows")),
            P(("groups", "rows"), "cols"),
            P(("groups", "blocks", "rows"), "cols"),
        ),
        out_specs=(P(("groups", "blocks", "rows"), "cols"), P(("groups", "rows"), "cols")),
        check_vma=False,
    )
```

```python
import functools

import jax
import jax.numpy as jnp
from jax import lax
from jax.experimental import pallas as pl
from jax.experimental.pallas import tpu as pltpu
from jax.sharding import PartitionSpec as P

DAMPING = 0.5
F32, BF16 = jnp.float32, jnp.bfloat16
LANES = 128

COS_TERMS = (
    0.9999999887556631, -0.49999988843399, 0.04166648574334225, -0.001388778673619495,
    2.4769518189949842e-05, -2.7075418374484127e-07, 1.7231808612122658e-09,
)
INV_TWO_PI = 0.15915494309189535
TWO_PI_HIGH = 6.28125
TWO_PI_LOW = 0.0019353071795864769


def cosine(angles):
    turns = jnp.round(angles * INV_TWO_PI)
    rest = (angles - turns * TWO_PI_HIGH) - turns * TWO_PI_LOW
    square = rest * rest
    result = jnp.full_like(square, COS_TERMS[-1])
    for term in COS_TERMS[-2::-1]:
        result = result * square + term
    return result


def dot(a, b):
    return jnp.dot(a, b, preferred_element_type=F32)


def dot_nt(a, b):
    return lax.dot_general(a, b, (((1,), (1,)), ((), ())), preferred_element_type=F32)


def call(kernel, out_shapes, place, args, name, vmem_mib):
    vmem = pl.BlockSpec(memory_space=pltpu.VMEM)
    single = isinstance(out_shapes, jax.ShapeDtypeStruct)
    return pl.pallas_call(
        kernel,
        out_shape=out_shapes,
        in_specs=[pl.BlockSpec(memory_space=pltpu.SMEM)] + [vmem] * len(args),
        out_specs=vmem if single else (vmem,) * len(out_shapes),
        compiler_params=pltpu.CompilerParams(vmem_limit_bytes=vmem_mib << 20),
        name=name,
    )(place, *args)


def like(shape, dtype=BF16):
    return jax.ShapeDtypeStruct(tuple(shape), dtype)


def lanes(index, size):
    return pl.ds(pl.multiple_of(index * size, size), size)


def residual_kernel(place, labels, predictions, out):
    width = predictions.shape[0]
    part = out.shape[1] // 2
    out[...] = jnp.zeros_like(out)
    for j in (0, 1):
        own = lanes(2 * place[1] + (place[2] ^ j), part)
        classes = lax.broadcasted_iota(jnp.int32, (width, part), 0) + place[2] * width
        hit = (classes == labels[:, own]).astype(F32)
        out[:width, j * part:(j + 1) * part] = (hit - predictions[:, own]).astype(BF16)


def features_kernel(n_rows, place, *refs):
    rows, (w_own, w_other, p_own, p_other, out) = refs[:n_rows], refs[n_rows:]
    inputs = rows[0][...] if n_rows == 1 else jnp.concatenate([r[...] for r in rows], axis=0)
    half = w_own.shape[1]
    for i, (weights, phases) in enumerate(((w_own, p_own), (w_other, p_other))):
        angles = dot(inputs, weights[...]) + phases[...].astype(F32)
        out[:, lanes(place[2] ^ i, half)] = cosine(angles).astype(BF16)


def features(place, rows, weights, phases):
    total = sum(r.shape[0] for r in rows)
    return call(
        functools.partial(features_kernel, len(rows)),
        like((total, 2 * weights[0].shape[1])), place, (*rows, *weights, *phases), "features", 14,
    )


def joined(pieces, part):
    sides = [[r[:, i * part:(i + 1) * part] for r in pieces] for i in (0, 1)]
    return [s[0] if len(s) == 1 else jnp.concatenate(s, axis=1) for s in sides]


def gradient_of(groups, refs, part, at_features):
    total, at = None, 0
    for count, stacked in groups:
        pieces = [refs[at + i][...] for i in range(count)]
        if stacked:
            pieces = [jnp.concatenate(pieces, axis=0)]
        first, second = joined(pieces, part)
        mine, theirs = refs[at + count][:, at_features], refs[at + count + 1][:, at_features]
        at += count + 2
        if first.shape[1] < 256:
            products = [dot(jnp.concatenate([first, second], axis=1), jnp.concatenate([mine, theirs], axis=0))]
        else:
            products = [dot(first, mine), dot(second, theirs)]
        for product in products:
            total = product if total is None else total + product
    return total


def flat(groups):
    return [a for pieces, mine, theirs in groups for a in (*pieces, mine, theirs)]


def shape_of(groups, stacked):
    return [(len(g[0]), s) for g, s in zip(groups, stacked)]


TILE = 512


def gradient_kernel(form, part, earlier, place, *refs):
    *pieces, out = refs
    for k in range(0, out.shape[1], TILE):
        at = slice(k, k + TILE)
        total = gradient_of(form, pieces[earlier:], part, at)
        out[:, at] = pieces[0][:, at] + total if earlier else total


def gradient(place, groups, stacked, part, padded, earlier=()):
    n_feat = groups[0][1].shape[1]
    return call(
        functools.partial(gradient_kernel, shape_of(groups, stacked), part, len(earlier)),
        like((padded, n_feat), F32), place, (*earlier, *flat(groups)), "gradient", 20,
    )


def high_low(x):
    high = x.astype(BF16)
    return high, (x - high.astype(F32)).astype(BF16)


def solve_kernel(form, part, place, *refs):
    *pieces, partial_gradient, inverse, coefficients, new, sent = refs
    total = None
    for k in range(0, inverse.shape[1], TILE):
        at = slice(k, k + TILE)
        g_high, g_low = high_low(partial_gradient[:, at] + gradient_of(form, pieces, part, at))
        p_high, p_low = high_low(inverse[:, at])
        product = dot_nt(g_high, p_high) + (dot_nt(g_high, p_low) + dot_nt(g_low, p_high))
        total = product if total is None else total + product
    update = DAMPING * total
    new[...] = coefficients[...] + update[:new.shape[0]]
    sent[...] = update.astype(BF16)


def solve(place, groups, stacked, part, partial_gradient, inverse, coefficients):
    outs = (like(coefficients.shape, F32), like((partial_gradient.shape[0], coefficients.shape[1])))
    return call(
        functools.partial(solve_kernel, shape_of(groups, stacked), part),
        outs, place, (*flat(groups), partial_gradient, inverse, coefficients), "solve", 24,
    )


def own_change(place, sent, features_ref):
    depth = sent.shape[1]
    return dot_nt(sent[...], features_ref[:, lanes(place[0], depth)])


def far_kernel(place, sent, mine, theirs, a, b):
    a[...] = own_change(place, sent, mine).astype(BF16)
    b[...] = own_change(place, sent, theirs).astype(BF16)


def third_kernel(place, sent, mine, theirs, in_e, in_o, out_e, out_o):
    part = in_e.shape[1]
    mine, theirs = own_change(place, sent, mine), own_change(place, sent, theirs)
    out_e[:, :part] = mine[:, :part].astype(BF16)
    out_e[:, part:] = (theirs[:, :part] + in_o[...].astype(F32)).astype(BF16)
    out_o[:, :part] = (mine[:, part:] + in_e[...].astype(F32)).astype(BF16)
    out_o[:, part:] = theirs[:, part:].astype(BF16)


def middle_kernel(place, sent, mine, theirs, in_e, in_o, out_e, out_o):
    part = in_e.shape[1] // 2
    for i, own in enumerate((mine, theirs)):
        own = own_change(place, sent, own)
        at = slice(i * part, (i + 1) * part)
        out_e[:, at] = (own[:, :part] + in_e[:, at].astype(F32)).astype(BF16)
        out_o[:, at] = (own[:, part:] + in_o[:, at].astype(F32)).astype(BF16)


def last_kernel(place, sent, mine, theirs, in_e, in_o, out):
    part = in_e.shape[1] // 2
    for i, own in enumerate((mine, theirs)):
        at = slice(i * part, (i + 1) * part)
        came = in_e[:, at].astype(F32) + in_o[:, at].astype(F32)
        out[:, at] = (own_change(place, sent, own) + came).astype(BF16)


def apply_kernel(place, predictions, own, other, new):
    width, part = new.shape[0], own.shape[1] // 2
    for i, source in enumerate((own, other)):
        for j in (0, 1):
            at = lanes(2 * (place[1] ^ i) + (place[2] ^ j), part)
            new[:, at] = predictions[:, at] + source[:width, j * part:(j + 1) * part].astype(F32)


def swap(x, axes, pairs):
    return lax.ppermute(x, axes, [p for a, b in pairs for p in ((a, b), (b, a))])


def ring_shards(n_rows, inputs, projection, phases, inverse_blocks, labels, predictions, coefficients):
    ring = [2 * z for z in range(n_rows)] + [2 * z + 1 for z in reversed(range(n_rows))]
    size = len(ring)
    even = [(ring[i], ring[i + 1]) for i in range(0, size, 2)]
    odd = [(ring[i], ring[(i + 1) % size]) for i in range(1, size, 2)]
    E = lambda x: swap(x, ("rows", "blocks"), even)
    O = lambda x: swap(x, ("rows", "blocks"), odd)
    C = lambda x: swap(x, "cols", [(0, 1)])

    z, x, c = (lax.axis_index(a) for a in ("rows", "blocks", "cols"))
    place = jnp.stack([z, x, c]).astype(jnp.int32)
    local_rows, width = predictions.shape
    part = local_rows // 4
    padded = -(-width // LANES) * LANES

    weights = (projection, C(projection))
    phases = phases[None, :]
    phases = (phases, C(phases))
    predictions, coefficients = predictions.T, coefficients.T

    x0 = lax.dynamic_slice_in_dim(inputs, (2 * x + c) * part, part, 0)
    r0 = call(
        residual_kernel, like((padded, 2 * part)), place, (labels[None, :], predictions), "residual", 6
    )

    def around(own):
        half = own.shape[0] // 2
        e1, o1 = E(own), O(own)
        e2, o2 = E(o1), O(e1)
        e3, o3 = E(o2), O(e2)
        e4, o4 = E(o3[:half]), O(e3[half:])
        return (e1, o1), (e2, o2), (e3, o3), (e4, o4)

    xs = ((x0,),) + around(x0)
    rs = ((r0,),) + around(r0)
    groups = []
    for rows_in, residual_in in zip(xs, rs):
        mine = features(place, rows_in, weights, phases)
        groups.append((residual_in, mine, C(mine)))
    first = gradient(place, groups[:3], (False,) * 3, part, padded)
    first = gradient(place, groups[3:4], (False,), part, padded, (first,))
    new_coefficients, sent = solve(place, groups[4:], (True,), part, first, inverse_blocks[0], coefficients)

    def step(kernel, k, received, shapes, name):
        return call(kernel, tuple(like(s) for s in shapes), place, (sent, *groups[k][1:], *received), name, 8)

    piece, block = (padded, part), (padded, 2 * part)
    a4, b4 = step(far_kernel, 4, (), (piece, piece), "far")
    e3, o3 = step(third_kernel, 3, (E(a4), O(b4)), (block, block), "third")
    e2, o2 = step(middle_kernel, 2, (O(o3), E(e3)), (block, block), "second")
    e1, o1 = step(middle_kernel, 1, (O(o2), E(e2)), (block, block), "first")
    (own,) = step(last_kernel, 0, (E(e1), O(o1)), (block,), "last")
    other = swap(own, "blocks", [(0, 1)])
    new = call(apply_kernel, like(predictions.shape, F32), place, (predictions, own, other), "apply", 6)
    return new_coefficients.T, new.T


def plain_shards(inputs, projection, phases, inverse_blocks, labels, predictions, coefficients):
    out_width = predictions.shape[1]
    classes = lax.axis_index("cols") * out_width + jnp.arange(out_width, dtype=jnp.int32)
    onehot = (labels[:, None] == classes[None, :]).astype(F32)
    residual = (onehot - predictions).astype(BF16)
    angles = dot(inputs, projection) + phases.astype(F32)[None, :]
    half_features = jnp.cos(angles).astype(BF16)
    features_full = lax.all_gather(half_features, "cols", axis=1, tiled=True)
    own_gradient = lax.psum_scatter(
        lax.dot_general(features_full, residual, (((0,), (0,)), ((), ())), preferred_element_type=F32),
        "rows", scatter_dimension=0, tiled=True,
    )
    gradient_full = lax.all_gather(own_gradient, "rows", axis=0, tiled=True)
    update = DAMPING * jnp.dot(inverse_blocks[0], gradient_full, precision=lax.Precision.HIGHEST)
    sent = lax.all_gather(update.astype(BF16), "rows", axis=0, tiled=True)
    summed = lax.psum(dot(features_full, sent), "blocks")
    return coefficients + update, predictions + summed


def solution(mesh):
    n_rows, n_blocks = mesh.shape["rows"], mesh.shape["blocks"]
    small_ring = n_blocks == 2 and n_rows == 4 and mesh.shape["cols"] == 2
    shards = functools.partial(ring_shards, n_rows) if small_ring else plain_shards
    return jax.shard_map(
        shards,
        mesh=mesh,
        in_specs=(
            P(("groups", "rows"), None),
            P(None, ("groups", "blocks", "cols")),
            P(("groups", "blocks", "cols")),
            P(("groups", "blocks"), "rows", None),
            P(("groups", "rows")),
            P(("groups", "rows"), "cols"),
            P(("groups", "blocks", "rows"), "cols"),
        ),
        out_specs=(P(("groups", "blocks", "rows"), "cols"), P(("groups", "rows"), "cols")),
        check_vma=False,
    )
```

```python
import functools

import jax
import jax.numpy as jnp
from jax import lax
from jax.experimental import pallas as pl
from jax.experimental.pallas import tpu as pltpu
from jax.sharding import PartitionSpec as P

DAMPING = 0.5
F32, BF16 = jnp.float32, jnp.bfloat16
LANES = 128

COS_TERMS = (
    0.9999999887556631, -0.49999988843399, 0.04166648574334225, -0.001388778673619495,
    2.4769518189949842e-05, -2.7075418374484127e-07, 1.7231808612122658e-09,
)
INV_TWO_PI = 0.15915494309189535
TWO_PI_HIGH = 6.28125
TWO_PI_LOW = 0.0019353071795864769


def cosine(angles):
    turns = jnp.round(angles * INV_TWO_PI)
    rest = (angles - turns * TWO_PI_HIGH) - turns * TWO_PI_LOW
    square = rest * rest
    result = jnp.full_like(square, COS_TERMS[-1])
    for term in COS_TERMS[-2::-1]:
        result = result * square + term
    return result


def dot(a, b):
    return jnp.dot(a, b, preferred_element_type=F32)


def dot_nt(a, b):
    return lax.dot_general(a, b, (((1,), (1,)), ((), ())), preferred_element_type=F32)


def call(kernel, out_shapes, place, args, name, vmem_mib, scratch=()):
    vmem = pl.BlockSpec(memory_space=pltpu.VMEM)
    single = isinstance(out_shapes, jax.ShapeDtypeStruct)
    return pl.pallas_call(
        kernel,
        out_shape=out_shapes,
        in_specs=[pl.BlockSpec(memory_space=pltpu.SMEM)] + [vmem] * len(args),
        out_specs=vmem if single else (vmem,) * len(out_shapes),
        scratch_shapes=scratch,
        compiler_params=pltpu.CompilerParams(vmem_limit_bytes=vmem_mib << 20),
        name=name,
    )(place, *args)


def like(shape, dtype=BF16):
    return jax.ShapeDtypeStruct(tuple(shape), dtype)


def lanes(index, size):
    return pl.ds(pl.multiple_of(index * size, size), size)


def message_kernel(place, inputs, labels, predictions, out):
    width = predictions.shape[0]
    part = out.shape[0] - LANES
    start = pl.multiple_of((2 * place[1] + place[2]) * part, part)
    out[:part] = inputs[pl.ds(start, part)]
    for i, k in enumerate(range(0, width, LANES)):
        size = min(LANES, width - k)
        if size < LANES:
            out[part:, 2 * part * i:2 * part * (i + 1)] = jnp.zeros((LANES, 2 * part), BF16)
        for j in (0, 1):
            own = lanes(2 * place[1] + (place[2] ^ j), part)
            classes = lax.broadcasted_iota(jnp.int32, (size, part), 0) + (place[2] * width + k)
            hit = (classes == labels[:, own]).astype(F32)
            at = slice(part * (2 * i + j), part * (2 * i + j + 1))
            out[part:part + size, at] = (hit - predictions[k:k + size, own]).astype(BF16)


def high_low(x):
    high = x.astype(BF16)
    return high, (x - high.astype(F32)).astype(BF16)


def split_kernel(place, x, high, low):
    high[...], low[...] = high_low(x[...])


TILE = 512


def block_kernel(n_rows, place, *refs):
    rows, (w_own, w_other, p_own, p_other, high, low, out, feats) = refs[:n_rows], refs[n_rows:]
    part = feats.shape[0] // n_rows
    inputs = [r[:part] for r in rows]
    inputs = inputs[0] if n_rows == 1 else jnp.concatenate(inputs, axis=0)
    half, depth = w_own.shape[1], high.shape[0]
    total = None
    for i, (weights, phases) in enumerate(((w_own, p_own), (w_other, p_other))):
        for k in range(0, half, TILE):
            at = pl.ds(pl.multiple_of((place[2] ^ i) * half + k, TILE), TILE)
            angles = dot(inputs, weights[:, k:k + TILE]) + phases[:, k:k + TILE].astype(F32)
            tile = cosine(angles).astype(BF16)
            feats[:, at] = tile
            product = dot_nt(tile, high[:, at]) + dot_nt(tile, low[:, at])
            total = product if total is None else total + product
    out[:, :depth], out[:, depth:2 * depth] = high_low(total)
    out[:, 2 * depth:] = feats[:, lanes(place[0], depth)]


def residual_of(ref, part):
    pieces = ref[ref.shape[0] - LANES:]
    pieces = [pieces[:, k:k + 2 * part] for k in range(0, pieces.shape[1], 2 * part)]
    return jnp.concatenate(pieces, axis=0)


def product_of(counts, refs, depth):
    total, at = None, 0
    for count in counts:
        mine, theirs = refs[at + count], refs[at + count + 1]
        part = mine.shape[0] // count
        pieces = [residual_of(refs[at + i], part) for i in range(count)]
        at += count + 2
        if count == 1:
            products = [dot(pieces[0], jnp.concatenate([mine[:, :2 * depth], theirs[:, :2 * depth]], axis=0))]
        else:
            sides = [jnp.concatenate([p[:, i * part:(i + 1) * part] for p in pieces], axis=1) for i in (0, 1)]
            products = [dot(side, q[:, :2 * depth]) for side, q in zip(sides, (mine, theirs))]
        for product in products:
            product = product[:, :depth] + product[:, depth:]
            total = product if total is None else total + product
    return total


def flat(groups):
    return [a for pieces, mine, theirs in groups for a in (*pieces, mine, theirs)]


def begin_kernel(counts, place, *refs):
    *pieces, out = refs
    out[...] = product_of(counts, pieces, out.shape[1])


def update_kernel(counts, place, *refs):
    *pieces, begun, coefficients, new, sent = refs
    update = DAMPING * (begun[...] + product_of(counts, pieces, begun.shape[1]))
    new[...] = coefficients[...] + update[:new.shape[0]]
    sent[...] = update.astype(BF16)


def own_change(sent, mine, theirs, rows=slice(None)):
    depth = sent.shape[1]
    pieces = [f[rows, 2 * depth:] for f in (mine, theirs)]
    return dot_nt(sent[...], jnp.concatenate(pieces, axis=0))


def far_kernel(place, sent, mine, out):
    out[...] = dot_nt(sent[...], mine[:, 2 * sent.shape[1]:]).astype(BF16)


def third_kernel(which, place, sent, mine, theirs, came, out):
    part = came.shape[1]
    own = own_change(sent, mine, theirs, slice(which * part, (which + 1) * part))
    for i in (0, 1):
        at = slice(i * part, (i + 1) * part)
        total = own[:, at] + came[...].astype(F32) if i != which else own[:, at]
        out[:, at] = total.astype(BF16)


def middle_kernel(which, place, sent, mine, theirs, came, out):
    part = came.shape[1] // 2
    own = own_change(sent, mine, theirs, slice(which * part, (which + 1) * part))
    out[...] = (own + came[...].astype(F32)).astype(BF16)


def last_kernel(place, sent, mine, theirs, in_a, in_b, out):
    came = in_a[...].astype(F32) + in_b[...].astype(F32)
    out[...] = (own_change(sent, mine, theirs) + came).astype(BF16)


def apply_kernel(place, predictions, own, other, new):
    width, part = new.shape[0], own.shape[1] // 2
    for i, source in enumerate((own, other)):
        for j in (0, 1):
            at = lanes(2 * (place[1] ^ i) + (place[2] ^ j), part)
            new[:, at] = predictions[:, at] + source[:width, j * part:(j + 1) * part].astype(F32)


def swap(x, axes, pairs):
    return lax.ppermute(x, axes, [p for a, b in pairs for p in ((a, b), (b, a))])


def ring_shards(n_rows, inputs, projection, phases, inverse_blocks, labels, predictions, coefficients):
    ring = [2 * z for z in range(n_rows)] + [2 * z + 1 for z in reversed(range(n_rows))]
    size = len(ring)
    even = [(ring[i], ring[i + 1]) for i in range(0, size, 2)]
    odd = [(ring[i], ring[(i + 1) % size]) for i in range(1, size, 2)]
    E = lambda x: swap(x, ("rows", "blocks"), even)
    O = lambda x: swap(x, ("rows", "blocks"), odd)
    C = lambda x: swap(x, "cols", [(0, 1)])

    z, x, c = (lax.axis_index(a) for a in ("rows", "blocks", "cols"))
    place = jnp.stack([z, x, c]).astype(jnp.int32)
    local_rows, width = predictions.shape
    part = local_rows // 4
    padded = -(-width // LANES) * LANES

    weights = (projection, C(projection))
    phases = phases[None, :]
    phases = (phases, C(phases))
    predictions, coefficients = predictions.T, coefficients.T
    depth = coefficients.shape[1]

    sent0 = call(
        message_kernel, like((part + LANES, inputs.shape[1])), place,
        (inputs, labels[None, :], predictions), "message", 8,
    )
    e1, o1 = E(sent0), O(sent0)
    e2, o2 = E(o1), O(e1)
    e3, o3 = E(o2), O(e2)
    e4, o4 = E(o3[:part]), O(e3[part:])
    inverse = call(
        split_kernel, (like(inverse_blocks.shape[1:]),) * 2, place, (inverse_blocks[0],), "split", 14
    )

    def block(*rows):
        out = like((len(rows) * part, 3 * depth))
        scratch = (pltpu.VMEM((len(rows) * part, 2 * projection.shape[1]), BF16),)
        args = (*rows, *weights, *phases, *inverse)
        mine = call(functools.partial(block_kernel, len(rows)), out, place, args, "block", 16, scratch)
        return mine, C(mine)

    b0, b1, b2, b3, b4 = block(sent0), block(e1, o1), block(e2, o2), block(e3, o3), block(e4)
    begun = call(
        functools.partial(begin_kernel, (1, 2, 2)), like((padded, depth), F32), place,
        flat([((sent0,), *b0), ((e1, o1), *b1), ((e2, o2), *b2)]), "begin", 14,
    )
    new_coefficients, sent = call(
        functools.partial(update_kernel, (2, 1)),
        (like(coefficients.shape, F32), like((padded, depth))), place,
        (*flat([((e3, o3), *b3), ((o4,), *b4)]), begun, coefficients), "update", 14,
    )

    piece, whole = like((padded, part)), like((padded, 2 * part))

    def hop(kernel, which, k, came, name):
        return call(functools.partial(kernel, which), whole, place, (sent, *k, came), name, 6)

    far_a = call(far_kernel, piece, place, (sent, b4[0]), "far", 6)
    far_b = call(far_kernel, piece, place, (sent, b4[1]), "far", 6)
    way_a, way_b = E(far_a), O(far_b)
    way_a, way_b = O(hop(third_kernel, 1, b3, way_a, "third")), E(hop(third_kernel, 0, b3, way_b, "third"))
    way_a, way_b = E(hop(middle_kernel, 0, b2, way_a, "second")), O(hop(middle_kernel, 1, b2, way_b, "second"))
    way_a, way_b = O(hop(middle_kernel, 1, b1, way_a, "first")), E(hop(middle_kernel, 0, b1, way_b, "first"))
    own = call(last_kernel, whole, place, (sent, *b0, way_a, way_b), "last", 6)
    other = swap(own, "blocks", [(0, 1)])
    new = call(apply_kernel, like(predictions.shape, F32), place, (predictions, own, other), "apply", 6)
    return new_coefficients.T, new.T


def plain_shards(inputs, projection, phases, inverse_blocks, labels, predictions, coefficients):
    out_width = predictions.shape[1]
    classes = lax.axis_index("cols") * out_width + jnp.arange(out_width, dtype=jnp.int32)
    onehot = (labels[:, None] == classes[None, :]).astype(F32)
    residual = (onehot - predictions).astype(BF16)
    angles = dot(inputs, projection) + phases.astype(F32)[None, :]
    half_features = jnp.cos(angles).astype(BF16)
    features_full = lax.all_gather(half_features, "cols", axis=1, tiled=True)
    own_gradient = lax.psum_scatter(
        lax.dot_general(features_full, residual, (((0,), (0,)), ((), ())), preferred_element_type=F32),
        "rows", scatter_dimension=0, tiled=True,
    )
    gradient_full = lax.all_gather(own_gradient, "rows", axis=0, tiled=True)
    update = DAMPING * jnp.dot(inverse_blocks[0], gradient_full, precision=lax.Precision.HIGHEST)
    sent = lax.all_gather(update.astype(BF16), "rows", axis=0, tiled=True)
    summed = lax.psum(dot(features_full, sent), "blocks")
    return coefficients + update, predictions + summed


def solution(mesh):
    n_rows, n_blocks = mesh.shape["rows"], mesh.shape["blocks"]
    small_ring = n_blocks == 2 and n_rows == 4 and mesh.shape["cols"] == 2
    shards = functools.partial(ring_shards, n_rows) if small_ring else plain_shards
    return jax.shard_map(
        shards,
        mesh=mesh,
        in_specs=(
            P(("groups", "rows"), None),
            P(None, ("groups", "blocks", "cols")),
            P(("groups", "blocks", "cols")),
            P(("groups", "blocks"), "rows", None),
            P(("groups", "rows")),
            P(("groups", "rows"), "cols"),
            P(("groups", "blocks", "rows"), "cols"),
        ),
        out_specs=(P(("groups", "blocks", "rows"), "cols"), P(("groups", "rows"), "cols")),
        check_vma=False,
    )
```

```python
import functools

import jax
import jax.numpy as jnp
from jax import lax
from jax.experimental import pallas as pl
from jax.experimental.pallas import tpu as pltpu
from jax.sharding import PartitionSpec as P

DAMPING = 0.5
F32, BF16 = jnp.float32, jnp.bfloat16
LANES = 128

COS_TERMS = (
    0.9999999887556631, -0.49999988843399, 0.04166648574334225, -0.001388778673619495,
    2.4769518189949842e-05, -2.7075418374484127e-07, 1.7231808612122658e-09,
)
INV_TWO_PI = 0.15915494309189535
TWO_PI_HIGH = 6.28125
TWO_PI_LOW = 0.0019353071795864769


def cosine(angles):
    turns = jnp.round(angles * INV_TWO_PI)
    rest = (angles - turns * TWO_PI_HIGH) - turns * TWO_PI_LOW
    square = rest * rest
    result = jnp.full_like(square, COS_TERMS[-1])
    for term in COS_TERMS[-2::-1]:
        result = result * square + term
    return result


def dot(a, b):
    return jnp.dot(a, b, preferred_element_type=F32)


def dot_nt(a, b):
    return lax.dot_general(a, b, (((1,), (1,)), ((), ())), preferred_element_type=F32)


def call(kernel, out_shapes, place, args, name, vmem_mib, mflops, scratch=()):
    vmem = pl.BlockSpec(memory_space=pltpu.VMEM)
    single = isinstance(out_shapes, jax.ShapeDtypeStruct)
    return pl.pallas_call(
        kernel,
        out_shape=out_shapes,
        in_specs=[pl.BlockSpec(memory_space=pltpu.SMEM)] + [vmem] * len(args),
        out_specs=vmem if single else (vmem,) * len(out_shapes),
        scratch_shapes=scratch,
        cost_estimate=pl.CostEstimate(
            flops=mflops * 10**6, transcendentals=0, bytes_accessed=sum(a.size * a.dtype.itemsize for a in args)
        ),
        compiler_params=pltpu.CompilerParams(vmem_limit_bytes=vmem_mib << 20),
        name=name,
    )(place, *args)


def like(shape, dtype=BF16):
    return jax.ShapeDtypeStruct(tuple(shape), dtype)


def lanes(index, size):
    return pl.ds(pl.multiple_of(index * size, size), size)


def message_kernel(place, inputs, labels, predictions, out):
    width = predictions.shape[0]
    part = out.shape[0] - LANES
    start = pl.multiple_of((2 * place[1] + place[2]) * part, part)
    out[:part] = inputs[pl.ds(start, part)]
    for i, k in enumerate(range(0, width, LANES)):
        size = min(LANES, width - k)
        if size < LANES:
            out[part:, 2 * part * i:2 * part * (i + 1)] = jnp.zeros((LANES, 2 * part), BF16)
        for j in (0, 1):
            own = lanes(2 * place[1] + (place[2] ^ j), part)
            classes = lax.broadcasted_iota(jnp.int32, (size, part), 0) + (place[2] * width + k)
            hit = (classes == labels[:, own]).astype(F32)
            at = slice(part * (2 * i + j), part * (2 * i + j + 1))
            out[part:part + size, at] = (hit - predictions[k:k + size, own]).astype(BF16)


def high_low(x):
    high = x.astype(BF16)
    return high, (x - high.astype(F32)).astype(BF16)


def split_kernel(place, x, high, low):
    high[...], low[...] = high_low(x[...])


TILE = 512


def block_kernel(n_rows, place, *refs):
    rows, (w_own, w_other, p_own, p_other, high, low, out, feats) = refs[:n_rows], refs[n_rows:]
    part = feats.shape[0] // n_rows
    inputs = [r[:part] for r in rows]
    inputs = inputs[0] if n_rows == 1 else jnp.concatenate(inputs, axis=0)
    half, depth = w_own.shape[1], high.shape[0]
    total = None
    for i, (weights, phases) in enumerate(((w_own, p_own), (w_other, p_other))):
        for k in range(0, half, TILE):
            at = pl.ds(pl.multiple_of((place[2] ^ i) * half + k, TILE), TILE)
            angles = dot(inputs, weights[:, k:k + TILE]) + phases[:, k:k + TILE].astype(F32)
            tile = cosine(angles).astype(BF16)
            feats[:, at] = tile
            product = dot_nt(tile, high[:, at]) + dot_nt(tile, low[:, at])
            total = product if total is None else total + product
    out[:, :depth], out[:, depth:2 * depth] = high_low(total)
    out[:, 2 * depth:] = feats[:, lanes(place[0], depth)]


def residual_of(ref, part):
    pieces = ref[ref.shape[0] - LANES:]
    pieces = [pieces[:, k:k + 2 * part] for k in range(0, pieces.shape[1], 2 * part)]
    return jnp.concatenate(pieces, axis=0)


def product_of(counts, refs, depth):
    total, at = None, 0
    for count in counts:
        mine, theirs = refs[at + count], refs[at + count + 1]
        part = mine.shape[0] // count
        pieces = [residual_of(refs[at + i], part) for i in range(count)]
        at += count + 2
        if count == 1:
            products = [dot(pieces[0], jnp.concatenate([mine[:, :2 * depth], theirs[:, :2 * depth]], axis=0))]
        else:
            sides = [jnp.concatenate([p[:, i * part:(i + 1) * part] for p in pieces], axis=1) for i in (0, 1)]
            products = [dot(side, q[:, :2 * depth]) for side, q in zip(sides, (mine, theirs))]
        for product in products:
            product = product[:, :depth] + product[:, depth:]
            total = product if total is None else total + product
    return total


def flat(groups):
    return [a for pieces, mine, theirs in groups for a in (*pieces, mine, theirs)]


def begin_kernel(counts, earlier, place, *refs):
    *pieces, out = refs
    total = product_of(counts, pieces[earlier:], out.shape[1])
    out[...] = pieces[0][...] + total if earlier else total


def update_kernel(counts, place, *refs):
    *pieces, begun, coefficients, new, sent = refs
    update = DAMPING * (begun[...] + product_of(counts, pieces, begun.shape[1]))
    new[...] = coefficients[...] + update[:new.shape[0]]
    sent[...] = update.astype(BF16)


def own_change(sent, mine, theirs, rows=slice(None)):
    depth = sent.shape[1]
    pieces = [f[rows, 2 * depth:] for f in (mine, theirs)]
    return dot_nt(sent[...], jnp.concatenate(pieces, axis=0))


def far_kernel(place, sent, mine, out):
    out[...] = dot_nt(sent[...], mine[:, 2 * sent.shape[1]:]).astype(BF16)


def third_kernel(which, place, sent, mine, theirs, came, out):
    part = came.shape[1]
    own = own_change(sent, mine, theirs, slice(which * part, (which + 1) * part))
    for i in (0, 1):
        at = slice(i * part, (i + 1) * part)
        total = own[:, at] + came[...].astype(F32) if i != which else own[:, at]
        out[:, at] = total.astype(BF16)


def middle_kernel(which, place, sent, mine, theirs, came, out):
    part = came.shape[1] // 2
    own = own_change(sent, mine, theirs, slice(which * part, (which + 1) * part))
    out[...] = (own + came[...].astype(F32)).astype(BF16)


def last_kernel(place, sent, mine, theirs, in_a, in_b, out):
    came = in_a[...].astype(F32) + in_b[...].astype(F32)
    out[...] = (own_change(sent, mine, theirs) + came).astype(BF16)


def apply_kernel(place, predictions, own, other, new):
    width, part = new.shape[0], own.shape[1] // 2
    for i, source in enumerate((own, other)):
        for j in (0, 1):
            at = lanes(2 * (place[1] ^ i) + (place[2] ^ j), part)
            new[:, at] = predictions[:, at] + source[:width, j * part:(j + 1) * part].astype(F32)


def swap(x, axes, pairs):
    return lax.ppermute(x, axes, [p for a, b in pairs for p in ((a, b), (b, a))])


def after(arrays, *others):
    return lax.optimization_barrier((*arrays, *others))[:len(arrays)]


def ring_shards(n_rows, inputs, projection, phases, inverse_blocks, labels, predictions, coefficients):
    ring = [2 * z for z in range(n_rows)] + [2 * z + 1 for z in reversed(range(n_rows))]
    size = len(ring)
    even = [(ring[i], ring[i + 1]) for i in range(0, size, 2)]
    odd = [(ring[i], ring[(i + 1) % size]) for i in range(1, size, 2)]
    E = lambda x: swap(x, ("rows", "blocks"), even)
    O = lambda x: swap(x, ("rows", "blocks"), odd)
    C = lambda x: swap(x, "cols", [(0, 1)])

    z, x, c = (lax.axis_index(a) for a in ("rows", "blocks", "cols"))
    place = jnp.stack([z, x, c]).astype(jnp.int32)
    local_rows, width = predictions.shape
    part = local_rows // 4
    padded = -(-width // LANES) * LANES

    weights = (projection, C(projection))
    phases = phases[None, :]
    phases = (phases, C(phases))
    predictions, coefficients = predictions.T, coefficients.T
    depth = coefficients.shape[1]

    sent0 = call(
        message_kernel, like((part + LANES, inputs.shape[1])), place,
        (inputs, labels[None, :], predictions), "message", 8, 300,
    )
    inverse = call(
        split_kernel, (like(inverse_blocks.shape[1:]),) * 2, place, (inverse_blocks[0],), "split", 14, 500
    )

    def block(*rows):
        out = like((len(rows) * part, 3 * depth))
        scratch = (pltpu.VMEM((len(rows) * part, 2 * projection.shape[1]), BF16),)
        args = (*rows, *weights, *phases, *inverse)
        mine = call(
            functools.partial(block_kernel, len(rows)), out, place, args, "block", 16, 2000 * len(rows), scratch
        )
        return mine, C(mine)

    def begin(groups, *earlier):
        counts = tuple(len(g[0]) for g in groups)
        return call(
            functools.partial(begin_kernel, counts, len(earlier)), like((padded, depth), F32), place,
            (*earlier, *flat(groups)), "begin", 14, 1400,
        )

    e1, o1 = E(sent0), O(sent0)
    b0 = block(sent0)
    e1, o1 = after((e1, o1), b0[0])
    e2, o2 = E(o1), O(e1)
    b1 = block(e1, o1)
    e2, o2 = after((e2, o2), b1[0])
    e3, o3 = E(o2), O(e2)
    b2 = block(e2, o2)
    begun = begin([((sent0,), *b0), ((e1, o1), *b1)])
    e3, o3 = after((e3, o3), b2[0], begun)
    rows4, residual4 = o3[:part], e3[part:]
    e4, o4 = E(rows4), O(residual4)
    e3, o3 = after((e3, o3), rows4, residual4)
    b3 = block(e3, o3)
    begun = begin([((e2, o2), *b2), ((e3, o3), *b3)], begun)
    e4, o4 = after((e4, o4), begun)
    b4 = block(e4)
    new_coefficients, sent = call(
        functools.partial(update_kernel, (1,)),
        (like(coefficients.shape, F32), like((padded, depth))), place,
        (*flat([((o4,), *b4)]), begun, coefficients), "update", 14, 800,
    )

    piece, whole = like((padded, part)), like((padded, 2 * part))

    def hop(kernel, which, k, came, name):
        return call(functools.partial(kernel, which), whole, place, (sent, *k, came), name, 6, 150)

    far_a = call(far_kernel, piece, place, (sent, b4[0]), "far", 6, 70)
    far_b = call(far_kernel, piece, place, (sent, b4[1]), "far", 6, 70)
    way_a, way_b = E(far_a), O(far_b)
    way_a, way_b = O(hop(third_kernel, 1, b3, way_a, "third")), E(hop(third_kernel, 0, b3, way_b, "third"))
    way_a, way_b = E(hop(middle_kernel, 0, b2, way_a, "second")), O(hop(middle_kernel, 1, b2, way_b, "second"))
    way_a, way_b = O(hop(middle_kernel, 1, b1, way_a, "first")), E(hop(middle_kernel, 0, b1, way_b, "first"))
    own = call(last_kernel, whole, place, (sent, *b0, way_a, way_b), "last", 6, 150)
    other = swap(own, "blocks", [(0, 1)])
    new = call(apply_kernel, like(predictions.shape, F32), place, (predictions, own, other), "apply", 6, 100)
    return new_coefficients.T, new.T


def plain_shards(inputs, projection, phases, inverse_blocks, labels, predictions, coefficients):
    out_width = predictions.shape[1]
    classes = lax.axis_index("cols") * out_width + jnp.arange(out_width, dtype=jnp.int32)
    onehot = (labels[:, None] == classes[None, :]).astype(F32)
    residual = (onehot - predictions).astype(BF16)
    angles = dot(inputs, projection) + phases.astype(F32)[None, :]
    half_features = jnp.cos(angles).astype(BF16)
    features_full = lax.all_gather(half_features, "cols", axis=1, tiled=True)
    own_gradient = lax.psum_scatter(
        lax.dot_general(features_full, residual, (((0,), (0,)), ((), ())), preferred_element_type=F32),
        "rows", scatter_dimension=0, tiled=True,
    )
    gradient_full = lax.all_gather(own_gradient, "rows", axis=0, tiled=True)
    update = DAMPING * jnp.dot(inverse_blocks[0], gradient_full, precision=lax.Precision.HIGHEST)
    sent = lax.all_gather(update.astype(BF16), "rows", axis=0, tiled=True)
    summed = lax.psum(dot(features_full, sent), "blocks")
    return coefficients + update, predictions + summed


def solution(mesh):
    n_rows, n_blocks = mesh.shape["rows"], mesh.shape["blocks"]
    small_ring = n_blocks == 2 and n_rows == 4 and mesh.shape["cols"] == 2
    shards = functools.partial(ring_shards, n_rows) if small_ring else plain_shards
    return jax.shard_map(
        shards,
        mesh=mesh,
        in_specs=(
            P(("groups", "rows"), None),
            P(None, ("groups", "blocks", "cols")),
            P(("groups", "blocks", "cols")),
            P(("groups", "blocks"), "rows", None),
            P(("groups", "rows")),
            P(("groups", "rows"), "cols"),
            P(("groups", "blocks", "rows"), "cols"),
        ),
        out_specs=(P(("groups", "blocks", "rows"), "cols"), P(("groups", "rows"), "cols")),
        check_vma=False,
    )
```

```python
import functools

import jax
import jax.numpy as jnp
from jax import lax
from jax.experimental import pallas as pl
from jax.experimental.pallas import tpu as pltpu
from jax.sharding import PartitionSpec as P

DAMPING = 0.5
F32, BF16 = jnp.float32, jnp.bfloat16
LANES = 128

COS_TERMS = (
    0.9999999887556631, -0.49999988843399, 0.04166648574334225, -0.001388778673619495,
    2.4769518189949842e-05, -2.7075418374484127e-07, 1.7231808612122658e-09,
)
INV_TWO_PI = 0.15915494309189535
TWO_PI_HIGH = 6.28125
TWO_PI_LOW = 0.0019353071795864769


def cosine(angles):
    turns = jnp.round(angles * INV_TWO_PI)
    rest = (angles - turns * TWO_PI_HIGH) - turns * TWO_PI_LOW
    square = rest * rest
    result = jnp.full_like(square, COS_TERMS[-1])
    for term in COS_TERMS[-2::-1]:
        result = result * square + term
    return result


def dot(a, b):
    return jnp.dot(a, b, preferred_element_type=F32)


def dot_nt(a, b):
    return lax.dot_general(a, b, (((1,), (1,)), ((), ())), preferred_element_type=F32)


def call(kernel, out_shapes, place, args, name, vmem_mib, mflops, scratch=()):
    vmem = pl.BlockSpec(memory_space=pltpu.VMEM)
    single = isinstance(out_shapes, jax.ShapeDtypeStruct)
    return pl.pallas_call(
        kernel,
        out_shape=out_shapes,
        in_specs=[pl.BlockSpec(memory_space=pltpu.SMEM)] + [vmem] * len(args),
        out_specs=vmem if single else (vmem,) * len(out_shapes),
        scratch_shapes=scratch,
        cost_estimate=pl.CostEstimate(
            flops=mflops * 10**6, transcendentals=0, bytes_accessed=sum(a.size * a.dtype.itemsize for a in args)
        ),
        compiler_params=pltpu.CompilerParams(vmem_limit_bytes=vmem_mib << 20),
        name=name,
    )(place, *args)


def like(shape, dtype=BF16):
    return jax.ShapeDtypeStruct(tuple(shape), dtype)


def lanes(index, size):
    return pl.ds(pl.multiple_of(index * size, size), size)


def inputs_kernel(place, inputs, out):
    part = out.shape[0] // 2
    for j in (0, 1):
        start = pl.multiple_of((2 * place[1] + (place[2] ^ j)) * part, part)
        out[j * part:(j + 1) * part] = inputs[pl.ds(start, part)]


def residual_kernel(place, labels, predictions, own, given):
    width = predictions.shape[0]
    part = own.shape[1] // 2
    tail = own.shape[0] - width
    own[width:], given[width:] = (jnp.zeros((tail, 2 * part), BF16),) * 2
    for j in (0, 1):
        at = lanes(2 * place[1] + (place[2] ^ j), part)
        classes = lax.broadcasted_iota(jnp.int32, (width, part), 0) + place[2] * width
        residual = ((classes == labels[:, at]).astype(F32) - predictions[:, at]).astype(BF16)
        own[:width, j * part:(j + 1) * part] = residual
        given[:width, (1 - j) * part:(2 - j) * part] = residual


def high_low(x):
    high = x.astype(BF16)
    return high, (x - high.astype(F32)).astype(BF16)


def split_kernel(place, x, high, low):
    high[...], low[...] = high_low(x[...])


TILE = 512


def block_kernel(place, rows, w_own, w_other, p_own, p_other, high, low, out, own_slice, feats):
    inputs = rows[:feats.shape[0]]
    half, depth = w_own.shape[1], high.shape[0]
    total = None
    for i, (weights, phases) in enumerate(((w_own, p_own), (w_other, p_other))):
        for k in range(0, half, TILE):
            at = pl.ds(pl.multiple_of((place[2] ^ i) * half + k, TILE), TILE)
            angles = dot(inputs, weights[:, k:k + TILE]) + phases[:, k:k + TILE].astype(F32)
            tile = cosine(angles).astype(BF16)
            feats[:, at] = tile
            product = dot_nt(tile, high[:, at]) + dot_nt(tile, low[:, at])
            total = product if total is None else total + product
    out[:, :depth], out[:, depth:] = high_low(total)
    own_slice[...] = feats[:, lanes(place[0], depth)]


def product_of(refs, classes):
    total, short = None, None
    for residual, q in zip(refs[::2], refs[1::2]):
        left, right = residual[:classes], q[...]
        if right.shape[0] < 256:
            if short is None:
                short = left[:, :right.shape[0]], right
                continue
            at = slice(0, right.shape[0]) if left.shape[1] == right.shape[0] else slice(right.shape[0], None)
            left = jnp.concatenate([short[0], left[:, at]], axis=1)
            right = jnp.concatenate([short[1], right], axis=0)
            short = None
        product = dot(left, right)
        depth = product.shape[1] // 2
        product = product[:, :depth] + product[:, depth:]
        total = product if total is None else total + product
    return total


def begin_kernel(earlier, place, *refs):
    *pieces, out = refs
    total = product_of(pieces[earlier:], out.shape[0])
    out[...] = pieces[0][...] + total if earlier else total


def update_kernel(place, begun, coefficients, *refs):
    *pieces, new, sent = refs
    update = DAMPING * (begun[...] + product_of(pieces, begun.shape[0]))
    new[...] = coefficients[...] + update[:new.shape[0]]
    sent[...] = update.astype(BF16)


def far_kernel(place, sent, feats, out):
    out[...] = dot_nt(sent[...], feats[...]).astype(BF16)


def hop_kernel(place, sent, feats, came, out):
    total = dot_nt(sent[...], feats[...])
    size = came.shape[1]
    out[:, :size] = (total[:, :size] + came[...].astype(F32)).astype(BF16)
    if size < out.shape[1]:
        out[:, size:] = total[:, size:].astype(BF16)


def last_kernel(place, sent, mine, theirs, came, given, out):
    part = mine.shape[0]
    total = dot_nt(sent[...], jnp.concatenate([mine[...], theirs[...]], axis=0)) + came[...].astype(F32)
    for i in (0, 1):
        at, there = slice(i * part, (i + 1) * part), slice((1 - i) * part, (2 - i) * part)
        out[:, at] = (total[:, at] + given[:, there].astype(F32)).astype(BF16)


def apply_kernel(place, predictions, own, other, new):
    width, part = new.shape[0], own.shape[1] // 2
    for i, source in enumerate((own, other)):
        for j in (0, 1):
            at = lanes(2 * (place[1] ^ i) + (place[2] ^ j), part)
            new[:, at] = predictions[:, at] + source[:width, j * part:(j + 1) * part].astype(F32)


def swap(x, axes, pairs):
    return lax.ppermute(x, axes, [p for a, b in pairs for p in ((a, b), (b, a))])


def after(arrays, *others):
    return lax.optimization_barrier((*arrays, *others))[:len(arrays)]


def ring_shards(n_rows, inputs, projection, phases, inverse_blocks, labels, predictions, coefficients):
    ring = [2 * z for z in range(n_rows)] + [2 * z + 1 for z in reversed(range(n_rows))]
    size = len(ring)
    even = [(ring[i], ring[i + 1]) for i in range(0, size, 2)]
    odd = [(ring[i], ring[(i + 1) % size]) for i in range(1, size, 2)]
    ways = [[(2 * a + c, 2 * b + c) for c, pairs in enumerate(way) for a, b in pairs]
            for way in ((even, odd), (odd, even))]
    S = lambda x: swap(x, ("rows", "blocks", "cols"), ways[0])
    T = lambda x: swap(x, ("rows", "blocks", "cols"), ways[1])
    C = lambda x: swap(x, "cols", [(0, 1)])

    place = jnp.stack([lax.axis_index(a) for a in ("rows", "blocks", "cols")]).astype(jnp.int32)
    local_rows, width = predictions.shape
    part = local_rows // 4
    padded = -(-width // LANES) * LANES
    predictions, coefficients = predictions.T, coefficients.T
    depth = coefficients.shape[1]

    x0 = call(inputs_kernel, like((2 * part, inputs.shape[1])), place, (inputs,), "inputs", 6, 100)
    own, given = call(
        residual_kernel, (like((padded, 2 * part)),) * 2, place, (labels[None, :], predictions), "residual", 6, 300
    )
    r0 = jnp.concatenate([own, C(given)], axis=0)
    weights = (projection, C(projection))
    phases = phases[None, :]
    phases = (phases, C(phases))
    inverse = call(
        split_kernel, (like(inverse_blocks.shape[1:]),) * 2, place, (inverse_blocks[0],), "split", 14, 500
    )

    def block(rows, size):
        scratch = (pltpu.VMEM((size, 2 * projection.shape[1]), BF16),)
        return call(
            block_kernel, (like((size, 2 * depth)), like((size, depth))), place,
            (rows, *weights, *phases, *inverse), "block", 16, size, scratch,
        )

    def begin(pairs, *earlier):
        return call(
            functools.partial(begin_kernel, len(earlier)), like((padded, depth), F32), place,
            (*earlier, *[a for pair in pairs for a in pair]), "begin", 14, 200,
        )

    x1, r1 = S(x0), S(r0)
    q0, f0 = block(x0, part)
    (x1,) = after((x1,), q0)
    x2 = T(x1)
    q1, f1 = block(x1, 2 * part)
    (r1,) = after((r1,), q1)
    r2 = T(r1)
    (x2,) = after((x2,), q1)
    x3 = S(x2)
    q2, f2 = block(x2, 2 * part)
    (r2,) = after((r2,), q2)
    r3 = S(r2)
    theirs = lambda r: C(r[padded:])
    q0_other, f0_other = C(q0), C(f0)
    begun = begin([(r0, q0), (r0, q0_other), (r1, q1), (theirs(r1), C(q1))])
    (x3,) = after((x3,), begun, f0_other)
    x4 = T(x3[:part])
    q3, f3 = block(x3, 2 * part)
    (r3,) = after((r3,), q3)
    r4 = T(r3[:, :part])
    begun = begin([(r2, q2), (theirs(r2), C(q2)), (r3, q3), (theirs(r3), C(q3))], begun)
    (x4,) = after((x4,), begun)
    q4, f4 = block(x4, part)
    new_coefficients, sent = call(
        update_kernel, (like(coefficients.shape, F32), like((padded, depth))), place,
        (begun, coefficients, r4, q4, theirs(r4), C(q4)), "update", 14, 800,
    )

    piece, whole = like((padded, part)), like((padded, 2 * part))
    far = lambda u: call(far_kernel, piece, place, (u, f4), "far", 6, 70)
    first = far(sent)
    updates = (sent, *after((C(sent),), first))
    moving = [T(first), T(far(updates[1]))]
    for way, feats in ((S, f3), (T, f2), (S, f1)):
        moving = [
            way(call(hop_kernel, whole, place, (u, feats, m), "hop", 6, 150)) for u, m in zip(updates, moving)
        ]
    own = call(last_kernel, whole, place, (sent, f0, f0_other, moving[0], C(moving[1])), "last", 6, 150)
    other = swap(own, "blocks", [(0, 1)])
    new = call(apply_kernel, like(predictions.shape, F32), place, (predictions, own, other), "apply", 6, 100)
    return new_coefficients.T, new.T


def plain_shards(inputs, projection, phases, inverse_blocks, labels, predictions, coefficients):
    out_width = predictions.shape[1]
    classes = lax.axis_index("cols") * out_width + jnp.arange(out_width, dtype=jnp.int32)
    onehot = (labels[:, None] == classes[None, :]).astype(F32)
    residual = (onehot - predictions).astype(BF16)
    angles = dot(inputs, projection) + phases.astype(F32)[None, :]
    half_features = jnp.cos(angles).astype(BF16)
    features_full = lax.all_gather(half_features, "cols", axis=1, tiled=True)
    own_gradient = lax.psum_scatter(
        lax.dot_general(features_full, residual, (((0,), (0,)), ((), ())), preferred_element_type=F32),
        "rows", scatter_dimension=0, tiled=True,
    )
    gradient_full = lax.all_gather(own_gradient, "rows", axis=0, tiled=True)
    update = DAMPING * jnp.dot(inverse_blocks[0], gradient_full, precision=lax.Precision.HIGHEST)
    sent = lax.all_gather(update.astype(BF16), "rows", axis=0, tiled=True)
    summed = lax.psum(dot(features_full, sent), "blocks")
    return coefficients + update, predictions + summed


def solution(mesh):
    n_rows, n_blocks = mesh.shape["rows"], mesh.shape["blocks"]
    small_ring = n_blocks == 2 and n_rows == 4 and mesh.shape["cols"] == 2
    shards = functools.partial(ring_shards, n_rows) if small_ring else plain_shards
    return jax.shard_map(
        shards,
        mesh=mesh,
        in_specs=(
            P(("groups", "rows"), None),
            P(None, ("groups", "blocks", "cols")),
            P(("groups", "blocks", "cols")),
            P(("groups", "blocks"), "rows", None),
            P(("groups", "rows")),
            P(("groups", "rows"), "cols"),
            P(("groups", "blocks", "rows"), "cols"),
        ),
        out_specs=(P(("groups", "blocks", "rows"), "cols"), P(("groups", "rows"), "cols")),
        check_vma=False,
    )
```

```python
import functools

import jax
import jax.numpy as jnp
from jax import lax
from jax.experimental import pallas as pl
from jax.experimental.pallas import tpu as pltpu
from jax.sharding import PartitionSpec as P

DAMPING = 0.5
F32, BF16 = jnp.float32, jnp.bfloat16
LANES = 128

SINE_TERMS = (
    6.283185280127733, -41.341680582549685, 81.60247253767959, -76.5810396203459, 39.75848375303386
)
TURNS = 0.15915494309189535


def cosine(angles, phases):
    turns = angles * TURNS + phases.astype(F32) * TURNS
    quarter = 0.25 - jnp.abs(turns - jnp.round(turns))
    square = quarter * quarter
    result = square * SINE_TERMS[-1] + SINE_TERMS[-2]
    for term in SINE_TERMS[-3::-1]:
        result = result * square + term
    return result * quarter


def dot(a, b):
    return jnp.dot(a, b, preferred_element_type=F32)


def dot_nt(a, b):
    return lax.dot_general(a, b, (((1,), (1,)), ((), ())), preferred_element_type=F32)


def call(kernel, out_shapes, place, args, name, vmem_mib, scratch=(), in_place=None, out_place=pltpu.VMEM, aliases={}):
    spaces = in_place or (pltpu.VMEM,) * len(args)
    vmem = pl.BlockSpec(memory_space=out_place)
    single = isinstance(out_shapes, jax.ShapeDtypeStruct)
    return pl.pallas_call(
        kernel,
        out_shape=out_shapes,
        in_specs=[pl.BlockSpec(memory_space=m) for m in (pltpu.SMEM, *spaces)],
        out_specs=vmem if single else (vmem,) * len(out_shapes),
        scratch_shapes=scratch,
        input_output_aliases=aliases,
        compiler_params=pltpu.CompilerParams(vmem_limit_bytes=vmem_mib << 20),
        name=name,
    )(place, *args)


def like(shape, dtype=BF16):
    return jax.ShapeDtypeStruct(tuple(shape), dtype)


def lanes(index, size):
    return pl.ds(pl.multiple_of(index * size, size), size)


def prepare_kernel(place, inputs, labels, predictions, rows, own, given, wide, tags, sems):
    width = predictions.shape[0]
    part = own.shape[1] // 2
    copies = []
    for j in (0, 1):
        block = 2 * place[1] + (place[2] ^ j)
        at, there = lanes(block, part), slice(j * part, (j + 1) * part)
        copies += [
            pltpu.make_async_copy(predictions.at[:, at], wide.at[:, there], sems.at[3 * j]),
            pltpu.make_async_copy(labels.at[:, at], tags.at[:, there], sems.at[3 * j + 1]),
            pltpu.make_async_copy(inputs.at[at], rows.at[there], sems.at[3 * j + 2]),
        ]
    for copy in copies:
        copy.start()
    tail = own.shape[0] - width
    own[width:], given[width:] = (jnp.zeros((tail, 2 * part), BF16),) * 2
    for j in (0, 1):
        copies[3 * j].wait()
        copies[3 * j + 1].wait()
        there = slice(j * part, (j + 1) * part)
        classes = lax.broadcasted_iota(jnp.int32, (width, part), 0) + place[2] * width
        residual = ((classes == tags[:, there]).astype(F32) - wide[:, there]).astype(BF16)
        own[:width, there] = residual
        given[:width, (1 - j) * part:(2 - j) * part] = residual
    for j in (0, 1):
        copies[3 * j + 2].wait()


def high_low(x):
    high = x.astype(BF16)
    return high, (x - high.astype(F32)).astype(BF16)


def split_kernel(place, x, high, low):
    high[...], low[...] = high_low(x[...])


TILE = 512


def block_kernel(place, rows, w_own, w_other, p_own, p_other, high, low, out, own_slice, feats):
    inputs = rows[:feats.shape[0]]
    half, depth = w_own.shape[1], high.shape[0]
    total = None
    for i, (weights, phases) in enumerate(((w_own, p_own), (w_other, p_other))):
        for k in range(0, half, TILE):
            at = pl.ds(pl.multiple_of((place[2] ^ i) * half + k, TILE), TILE)
            tile = cosine(dot(inputs, weights[:, k:k + TILE]), phases[:, k:k + TILE]).astype(BF16)
            feats[:, at] = tile
            product = dot_nt(tile, high[:, at]) + dot_nt(tile, low[:, at])
            total = product if total is None else total + product
    out[:, :depth], out[:, depth:] = high_low(total)
    own_slice[...] = feats[:, lanes(place[0], depth)]


def product_of(refs, classes):
    total, short = None, None
    for residual, q in zip(refs[::2], refs[1::2]):
        left, right = residual[:classes], q[...]
        if right.shape[0] < 256:
            if short is None:
                short = left[:, :right.shape[0]], right
                continue
            at = slice(0, right.shape[0]) if left.shape[1] == right.shape[0] else slice(right.shape[0], None)
            left = jnp.concatenate([short[0], left[:, at]], axis=1)
            right = jnp.concatenate([short[1], right], axis=0)
            short = None
        product = dot(left, right)
        depth = product.shape[1] // 2
        product = product[:, :depth] + product[:, depth:]
        total = product if total is None else total + product
    return total


def begin_kernel(earlier, place, *refs):
    *pieces, out = refs
    total = product_of(pieces[earlier:], out.shape[0])
    out[...] = pieces[0][...] + total if earlier else total


def update_kernel(place, begun, *refs):
    *pieces, update, sent = refs
    total = DAMPING * (begun[...] + product_of(pieces, begun.shape[0]))
    update[...] = total
    sent[...] = total.astype(BF16)


def far_kernel(place, sent, feats, out):
    out[...] = dot_nt(sent[...], feats[...]).astype(BF16)


def hop_kernel(place, sent, feats, came, out):
    total = dot_nt(sent[...], feats[...])
    size = came.shape[1]
    out[:, :size] = (total[:, :size] + came[...].astype(F32)).astype(BF16)
    if size < out.shape[1]:
        out[:, size:] = total[:, size:].astype(BF16)


def last_kernel(place, sent, mine, theirs, came, given, out):
    part = mine.shape[0]
    total = dot_nt(sent[...], jnp.concatenate([mine[...], theirs[...]], axis=0)) + came[...].astype(F32)
    for i in (0, 1):
        at, there = slice(i * part, (i + 1) * part), slice((1 - i) * part, (2 - i) * part)
        out[:, at] = (total[:, at] + given[:, there].astype(F32)).astype(BF16)


def apply_kernel(which, place, predictions, change, *refs):
    new, total, sems = refs[-3:]
    width, part = total.shape[0], total.shape[1] // 2
    copies = []
    for j in (0, 1):
        at, there = lanes(2 * (place[1] ^ which) + (place[2] ^ j), part), slice(j * part, (j + 1) * part)
        total[:, there] = predictions[:, at] + change[:width, there].astype(F32)
        copies.append(pltpu.make_async_copy(total.at[:, there], new.at[:, at], sems.at[j]))
        copies[j].start()
    for copy in copies:
        copy.wait()


def swap(x, axes, pairs):
    return lax.ppermute(x, axes, [p for a, b in pairs for p in ((a, b), (b, a))])


def after(arrays, *others):
    return lax.optimization_barrier((*arrays, *others))[:len(arrays)]


def ring_shards(n_rows, inputs, projection, phases, inverse_blocks, labels, predictions, coefficients):
    ring = [2 * z for z in range(n_rows)] + [2 * z + 1 for z in reversed(range(n_rows))]
    size = len(ring)
    even = [(ring[i], ring[i + 1]) for i in range(0, size, 2)]
    odd = [(ring[i], ring[(i + 1) % size]) for i in range(1, size, 2)]
    ways = [[(2 * a + c, 2 * b + c) for c, pairs in enumerate(way) for a, b in pairs]
            for way in ((even, odd), (odd, even))]
    S = lambda x: swap(x, ("rows", "blocks", "cols"), ways[0])
    T = lambda x: swap(x, ("rows", "blocks", "cols"), ways[1])
    C = lambda x: swap(x, "cols", [(0, 1)])

    place = jnp.stack([lax.axis_index(a) for a in ("rows", "blocks", "cols")]).astype(jnp.int32)
    local_rows, width = predictions.shape
    part = local_rows // 4
    padded = -(-width // LANES) * LANES
    predictions, coefficients = predictions.T, coefficients.T
    depth = coefficients.shape[1]

    dma = pltpu.SemaphoreType.DMA
    block_rows = like((2 * part, inputs.shape[1]))
    x0, own, given = call(
        prepare_kernel, (block_rows, *(like((padded, 2 * part)),) * 2), place,
        tuple(pltpu.with_memory_space_constraint(a, pltpu.HBM) for a in (inputs, labels[None, :], predictions)),
        "prepare", 6,
        (pltpu.VMEM((width, 2 * part), F32), pltpu.VMEM((1, 2 * part), jnp.int32), dma((6,))), (pltpu.HBM,) * 3,
    )
    given = C(given)
    (x0,) = after((x0,), given)
    r0 = jnp.concatenate([own, given], axis=0)
    weights = (projection, C(projection))
    phases = phases[None, :]
    phases = (phases, C(phases))
    inverse = call(
        split_kernel, (like(inverse_blocks.shape[1:]),) * 2, place, (inverse_blocks[0],), "split", 14
    )

    def block(rows, size):
        scratch = (pltpu.VMEM((size, 2 * projection.shape[1]), BF16),)
        return call(
            block_kernel, (like((size, 2 * depth)), like((size, depth))), place,
            (rows, *weights, *phases, *inverse), "block", 16, scratch,
        )

    def begin(pairs, *earlier):
        return call(
            functools.partial(begin_kernel, len(earlier)), like((padded, depth), F32), place,
            (*earlier, *[a for pair in pairs for a in pair]), "begin", 14,
        )

    x1, r1 = S(x0), S(r0)
    q0, f0 = block(x0, part)
    (x1,) = after((x1,), q0)
    x2 = T(x1)
    q1, f1 = block(x1, 2 * part)
    (r1,) = after((r1,), q1)
    r2 = T(r1)
    (x2,) = after((x2,), q1)
    x3 = S(x2)
    q2, f2 = block(x2, 2 * part)
    (r2,) = after((r2,), q2)
    r3 = S(r2)
    theirs = lambda r: C(r[padded:])
    q0_other, f0_other = C(q0), C(f0)
    begun = begin([(r0, q0), (r0, q0_other), (r1, q1), (theirs(r1), C(q1))])
    (x3,) = after((x3,), begun, f0_other)
    x4 = T(x3[:part])
    q3, f3 = block(x3, 2 * part)
    (r3,) = after((r3,), q3)
    r4 = T(r3[:, :part])
    begun = begin([(r2, q2), (theirs(r2), C(q2)), (r3, q3), (theirs(r3), C(q3))], begun)
    (x4,) = after((x4,), begun)
    q4, f4 = block(x4, part)
    update, sent = call(
        update_kernel, (like((padded, depth), F32), like((padded, depth))), place,
        (begun, r4, q4, theirs(r4), C(q4)), "update", 14,
    )

    piece, whole = like((padded, part)), like((padded, 2 * part))
    far = lambda u: call(far_kernel, piece, place, (u, f4), "far", 6)
    hop = lambda u, feats, came: call(hop_kernel, whole, place, (u, feats, came), "hop", 6)
    first = far(sent)
    sent_other, first = after((C(sent), first), first)
    first, second = T(first), T(far(sent_other))
    (second,) = after((second,), first)
    for way, feats in ((S, f3), (T, f2), (S, f1)):
        second_sum = hop(sent_other, feats, second)
        (first,) = after((first,), second_sum)
        first_sum = hop(sent, feats, first)
        second, first = way(second_sum), way(first_sum)
        (second,) = after((second,), first_sum)
    own = call(last_kernel, whole, place, (sent, f0, f0_other, first, C(second)), "last", 6)
    new = None
    for i in (0, 1):
        change = swap(own, "blocks", [(0, 1)]) if i else own
        earlier = (new,) if i else ()
        new = call(
            functools.partial(apply_kernel, i), like(predictions.shape, F32), place,
            (predictions, change, *earlier), "apply", 6, (pltpu.VMEM((width, 2 * part), F32), dma((2,))),
            (pltpu.VMEM, pltpu.VMEM, *(pl.ANY,) * i), pl.ANY, {3: 0} if i else {},
        )
    return (coefficients + update[:width]).T, new.T


def plain_shards(inputs, projection, phases, inverse_blocks, labels, predictions, coefficients):
    out_width = predictions.shape[1]
    classes = lax.axis_index("cols") * out_width + jnp.arange(out_width, dtype=jnp.int32)
    onehot = (labels[:, None] == classes[None, :]).astype(F32)
    residual = (onehot - predictions).astype(BF16)
    angles = dot(inputs, projection) + phases.astype(F32)[None, :]
    half_features = jnp.cos(angles).astype(BF16)
    features_full = lax.all_gather(half_features, "cols", axis=1, tiled=True)
    own_gradient = lax.psum_scatter(
        lax.dot_general(features_full, residual, (((0,), (0,)), ((), ())), preferred_element_type=F32),
        "rows", scatter_dimension=0, tiled=True,
    )
    gradient_full = lax.all_gather(own_gradient, "rows", axis=0, tiled=True)
    update = DAMPING * jnp.dot(inverse_blocks[0], gradient_full, precision=lax.Precision.HIGHEST)
    sent = lax.all_gather(update.astype(BF16), "rows", axis=0, tiled=True)
    summed = lax.psum(dot(features_full, sent), "blocks")
    return coefficients + update, predictions + summed


def solution(mesh):
    n_rows, n_blocks = mesh.shape["rows"], mesh.shape["blocks"]
    small_ring = n_blocks == 2 and n_rows == 4 and mesh.shape["cols"] == 2
    shards = functools.partial(ring_shards, n_rows) if small_ring else plain_shards
    return jax.shard_map(
        shards,
        mesh=mesh,
        in_specs=(
            P(("groups", "rows"), None),
            P(None, ("groups", "blocks", "cols")),
            P(("groups", "blocks", "cols")),
            P(("groups", "blocks"), "rows", None),
            P(("groups", "rows")),
            P(("groups", "rows"), "cols"),
            P(("groups", "blocks", "rows"), "cols"),
        ),
        out_specs=(P(("groups", "blocks", "rows"), "cols"), P(("groups", "rows"), "cols")),
        check_vma=False,
    )
```

```python
import functools

import jax
import jax.numpy as jnp
from jax import lax
from jax.experimental import pallas as pl
from jax.experimental.pallas import tpu as pltpu
from jax.sharding import PartitionSpec as P

DAMPING = 0.5
F32, BF16 = jnp.float32, jnp.bfloat16
LANES = 128

SINE_TERMS = (
    6.283185280127733, -41.341680582549685, 81.60247253767959, -76.5810396203459, 39.75848375303386
)
TURNS = 0.15915494309189535


def cosine(angles, phases):
    turns = angles * TURNS + phases.astype(F32) * TURNS
    quarter = 0.25 - jnp.abs(turns - jnp.round(turns))
    square = quarter * quarter
    result = square * SINE_TERMS[-1] + SINE_TERMS[-2]
    for term in SINE_TERMS[-3::-1]:
        result = result * square + term
    return result * quarter


def dot(a, b):
    return jnp.dot(a, b, preferred_element_type=F32)


def dot_nt(a, b):
    return lax.dot_general(a, b, (((1,), (1,)), ((), ())), preferred_element_type=F32)


def call(kernel, out_shapes, place, args, name, vmem_mib, scratch=(), in_place=None, out_place=pltpu.VMEM, aliases={}):
    spaces = in_place or (pltpu.VMEM,) * len(args)
    vmem = pl.BlockSpec(memory_space=out_place)
    single = isinstance(out_shapes, jax.ShapeDtypeStruct)
    return pl.pallas_call(
        kernel,
        out_shape=out_shapes,
        in_specs=[pl.BlockSpec(memory_space=m) for m in (pltpu.SMEM, *spaces)],
        out_specs=vmem if single else (vmem,) * len(out_shapes),
        scratch_shapes=scratch,
        input_output_aliases=aliases,
        compiler_params=pltpu.CompilerParams(vmem_limit_bytes=vmem_mib << 20),
        name=name,
    )(place, *args)


def like(shape, dtype=BF16):
    return jax.ShapeDtypeStruct(tuple(shape), dtype)


def lanes(index, size):
    return pl.ds(pl.multiple_of(index * size, size), size)


def prepare_kernel(place, inputs, labels, predictions, rows, own, given, wide, tags, sems):
    width = predictions.shape[0]
    part = own.shape[1] // 2
    copies = []
    for j in (0, 1):
        block = 2 * place[1] + (place[2] ^ j)
        at, there = lanes(block, part), slice(j * part, (j + 1) * part)
        copies += [
            pltpu.make_async_copy(predictions.at[:, at], wide.at[:, there], sems.at[3 * j]),
            pltpu.make_async_copy(labels.at[:, at], tags.at[:, there], sems.at[3 * j + 1]),
            pltpu.make_async_copy(inputs.at[at], rows.at[there], sems.at[3 * j + 2]),
        ]
    for copy in copies:
        copy.start()
    tail = own.shape[0] - width
    own[width:], given[width:] = (jnp.zeros((tail, 2 * part), BF16),) * 2
    for j in (0, 1):
        copies[3 * j].wait()
        copies[3 * j + 1].wait()
        there = slice(j * part, (j + 1) * part)
        classes = lax.broadcasted_iota(jnp.int32, (width, part), 0) + place[2] * width
        residual = ((classes == tags[:, there]).astype(F32) - wide[:, there]).astype(BF16)
        own[:width, there] = residual
        given[:width, (1 - j) * part:(2 - j) * part] = residual
    for j in (0, 1):
        copies[3 * j + 2].wait()


def high_low(x):
    high = x.astype(BF16)
    return high, (x - high.astype(F32)).astype(BF16)


def split_kernel(place, x, high, low):
    high[...], low[...] = high_low(x[...])


TILE = 512


def block_kernel(place, rows, w_own, w_other, p_own, p_other, high, low, out, own_slice, feats):
    inputs = rows[:feats.shape[0]]
    half, depth = w_own.shape[1], high.shape[0]
    total = None
    for i, (weights, phases) in enumerate(((w_own, p_own), (w_other, p_other))):
        for k in range(0, half, TILE):
            at = pl.ds(pl.multiple_of((place[2] ^ i) * half + k, TILE), TILE)
            tile = cosine(dot(inputs, weights[:, k:k + TILE]), phases[:, k:k + TILE]).astype(BF16)
            feats[:, at] = tile
            product = dot_nt(tile, high[:, at]) + dot_nt(tile, low[:, at])
            total = product if total is None else total + product
    out[:, :depth], out[:, depth:] = high_low(total)
    own_slice[...] = feats[:, lanes(place[0], depth)]


def product_of(refs, classes):
    total, short = None, None
    for residual, q in zip(refs[::2], refs[1::2]):
        left, right = residual[:classes], q[...]
        if right.shape[0] < 256:
            if short is None:
                short = left[:, :right.shape[0]], right
                continue
            at = slice(0, right.shape[0]) if left.shape[1] == right.shape[0] else slice(right.shape[0], None)
            left = jnp.concatenate([short[0], left[:, at]], axis=1)
            right = jnp.concatenate([short[1], right], axis=0)
            short = None
        product = dot(left, right)
        depth = product.shape[1] // 2
        product = product[:, :depth] + product[:, depth:]
        total = product if total is None else total + product
    return total


def begin_kernel(earlier, place, *refs):
    *pieces, out = refs
    total = product_of(pieces[earlier:], out.shape[0])
    out[...] = pieces[0][...] + total if earlier else total


def update_kernel(place, begun, *refs):
    *pieces, update, sent = refs
    total = DAMPING * (begun[...] + product_of(pieces, begun.shape[0]))
    update[...] = total
    sent[...] = total.astype(BF16)


def far_kernel(place, sent, feats, out):
    out[...] = dot_nt(sent[...], feats[...]).astype(BF16)


def hop_kernel(place, sent, feats, came, out):
    total = dot_nt(sent[...], feats[...])
    size = came.shape[1]
    out[:, :size] = (total[:, :size] + came[...].astype(F32)).astype(BF16)
    if size < out.shape[1]:
        out[:, size:] = total[:, size:].astype(BF16)


def last_kernel(place, sent, mine, theirs, came, given, out):
    part = mine.shape[0]
    total = dot_nt(sent[...], jnp.concatenate([mine[...], theirs[...]], axis=0)) + came[...].astype(F32)
    for i in (0, 1):
        at, there = slice(i * part, (i + 1) * part), slice((1 - i) * part, (2 - i) * part)
        out[:, at] = (total[:, at] + given[:, there].astype(F32)).astype(BF16)


def apply_kernel(which, place, predictions, change, *refs):
    new, total, sems = refs[-3:]
    width, part = total.shape[0], total.shape[1] // 2
    copies = []
    for j in (0, 1):
        at, there = lanes(2 * (place[1] ^ which) + (place[2] ^ j), part), slice(j * part, (j + 1) * part)
        total[:, there] = predictions[:, at] + change[:width, there].astype(F32)
        copies.append(pltpu.make_async_copy(total.at[:, there], new.at[:, at], sems.at[j]))
        copies[j].start()
    for copy in copies:
        copy.wait()


def swap(x, axes, pairs):
    return lax.ppermute(x, axes, [p for a, b in pairs for p in ((a, b), (b, a))])


def after(arrays, *others):
    return lax.optimization_barrier((*arrays, *others))[:len(arrays)]


def ring_shards(n_rows, inputs, projection, phases, inverse_blocks, labels, predictions, coefficients):
    ring = [2 * z for z in range(n_rows)] + [2 * z + 1 for z in reversed(range(n_rows))]
    size = len(ring)
    even = [(ring[i], ring[i + 1]) for i in range(0, size, 2)]
    odd = [(ring[i], ring[(i + 1) % size]) for i in range(1, size, 2)]
    ways = [[(2 * a + c, 2 * b + c) for c, pairs in enumerate(way) for a, b in pairs]
            for way in ((even, odd), (odd, even))]
    S = lambda x: swap(x, ("rows", "blocks", "cols"), ways[0])
    T = lambda x: swap(x, ("rows", "blocks", "cols"), ways[1])
    C = lambda x: swap(x, "cols", [(0, 1)])

    place = jnp.stack([lax.axis_index(a) for a in ("rows", "blocks", "cols")]).astype(jnp.int32)
    local_rows, width = predictions.shape
    part = local_rows // 4
    padded = -(-width // LANES) * LANES
    predictions, coefficients = predictions.T, coefficients.T
    depth = coefficients.shape[1]

    dma = pltpu.SemaphoreType.DMA
    block_rows = like((2 * part, inputs.shape[1]))
    x0, own, given = call(
        prepare_kernel, (block_rows, *(like((padded, 2 * part)),) * 2), place,
        tuple(pltpu.with_memory_space_constraint(a, pltpu.HBM) for a in (inputs, labels[None, :], predictions)),
        "prepare", 6,
        (pltpu.VMEM((width, 2 * part), F32), pltpu.VMEM((1, 2 * part), jnp.int32), dma((6,))), (pltpu.HBM,) * 3,
    )
    given = C(given)
    (x0,) = after((x0,), given)
    r0 = jnp.concatenate([own, given], axis=0)
    weights = (projection, C(projection))
    phases = phases[None, :]
    phases = (phases, C(phases))
    inverse = call(
        split_kernel, (like(inverse_blocks.shape[1:]),) * 2, place, (inverse_blocks[0],), "split", 14
    )

    def block(rows, size):
        scratch = (pltpu.VMEM((size, 2 * projection.shape[1]), BF16),)
        return call(
            block_kernel, (like((size, 2 * depth)), like((size, depth))), place,
            (rows, *weights, *phases, *inverse), "block", 16, scratch,
        )

    def begin(pairs, *earlier):
        return call(
            functools.partial(begin_kernel, len(earlier)), like((padded, depth), F32), place,
            (*earlier, *[a for pair in pairs for a in pair]), "begin", 14,
        )

    x1, r1 = S(x0), S(r0)
    q0, f0 = block(x0, part)
    (x1,) = after((x1,), q0)
    x2 = T(x1)
    q1, f1 = block(x1, 2 * part)
    (r1,) = after((r1,), q1)
    r2 = T(r1)
    (x2,) = after((x2,), q1)
    x3 = S(x2)
    q2, f2 = block(x2, 2 * part)
    (r2,) = after((r2,), q2)
    r3 = S(r2)
    theirs = lambda r: C(r[padded:])
    q0_other, f0_other = C(q0), C(f0)
    begun = begin([(r0, q0), (r0, q0_other), (r1, q1), (theirs(r1), C(q1))])
    (x3,) = after((x3,), begun, f0_other)
    x4 = T(x3[:part])
    q3, f3 = block(x3, 2 * part)
    (r3,) = after((r3,), q3)
    r4 = T(r3[:, :part])
    (x4,) = after((x4,), q3)
    q4, f4 = block(x4, part)
    begun = begin([(r2, q2), (theirs(r2), C(q2)), (r3, q3), (theirs(r3), C(q3))], begun)
    update, sent = call(
        update_kernel, (like((padded, depth), F32), like((padded, depth))), place,
        (begun, r4, q4, theirs(r4), C(q4)), "update", 14,
    )

    piece, whole = like((padded, part)), like((padded, 2 * part))
    far = lambda u: call(far_kernel, piece, place, (u, f4), "far", 6)
    hop = lambda u, feats, came: call(hop_kernel, whole, place, (u, feats, came), "hop", 6)
    first = far(sent)
    sent_other, first = after((C(sent), first), first)
    first, second = T(first), T(far(sent_other))
    (second,) = after((second,), first)
    for way, feats in ((S, f3), (T, f2), (S, f1)):
        second_sum = hop(sent_other, feats, second)
        (first,) = after((first,), second_sum)
        first_sum = hop(sent, feats, first)
        second, first = way(second_sum), way(first_sum)
        (second,) = after((second,), first_sum)
    own = call(last_kernel, whole, place, (sent, f0, f0_other, first, C(second)), "last", 6)
    new = None
    for i in (0, 1):
        change = swap(own, "blocks", [(0, 1)]) if i else own
        earlier = (new,) if i else ()
        new = call(
            functools.partial(apply_kernel, i), like(predictions.shape, F32), place,
            (predictions, change, *earlier), "apply", 6, (pltpu.VMEM((width, 2 * part), F32), dma((2,))),
            (pltpu.VMEM, pltpu.VMEM, *(pl.ANY,) * i), pl.ANY, {3: 0} if i else {},
        )
    return (coefficients + update[:width]).T, new.T


def plain_shards(inputs, projection, phases, inverse_blocks, labels, predictions, coefficients):
    out_width = predictions.shape[1]
    classes = lax.axis_index("cols") * out_width + jnp.arange(out_width, dtype=jnp.int32)
    onehot = (labels[:, None] == classes[None, :]).astype(F32)
    residual = (onehot - predictions).astype(BF16)
    angles = dot(inputs, projection) + phases.astype(F32)[None, :]
    half_features = jnp.cos(angles).astype(BF16)
    features_full = lax.all_gather(half_features, "cols", axis=1, tiled=True)
    own_gradient = lax.psum_scatter(
        lax.dot_general(features_full, residual, (((0,), (0,)), ((), ())), preferred_element_type=F32),
        "rows", scatter_dimension=0, tiled=True,
    )
    gradient_full = lax.all_gather(own_gradient, "rows", axis=0, tiled=True)
    update = DAMPING * jnp.dot(inverse_blocks[0], gradient_full, precision=lax.Precision.HIGHEST)
    sent = lax.all_gather(update.astype(BF16), "rows", axis=0, tiled=True)
    summed = lax.psum(dot(features_full, sent), "blocks")
    return coefficients + update, predictions + summed


def solution(mesh):
    n_rows, n_blocks = mesh.shape["rows"], mesh.shape["blocks"]
    small_ring = n_blocks == 2 and n_rows == 4 and mesh.shape["cols"] == 2
    shards = functools.partial(ring_shards, n_rows) if small_ring else plain_shards
    return jax.shard_map(
        shards,
        mesh=mesh,
        in_specs=(
            P(("groups", "rows"), None),
            P(None, ("groups", "blocks", "cols")),
            P(("groups", "blocks", "cols")),
            P(("groups", "blocks"), "rows", None),
            P(("groups", "rows")),
            P(("groups", "rows"), "cols"),
            P(("groups", "blocks", "rows"), "cols"),
        ),
        out_specs=(P(("groups", "blocks", "rows"), "cols"), P(("groups", "rows"), "cols")),
        check_vma=False,
    )
```

```python
import functools

import jax
import jax.numpy as jnp
from jax import lax
from jax.experimental import pallas as pl
from jax.experimental.pallas import tpu as pltpu
from jax.sharding import PartitionSpec as P

DAMPING = 0.5
F32, BF16 = jnp.float32, jnp.bfloat16
LANES = 128

SINE_TERMS = (
    6.283185280127733, -41.341680582549685, 81.60247253767959, -76.5810396203459, 39.75848375303386
)
TURNS = 0.15915494309189535


def cosine(angles, phases):
    turns = angles * TURNS + phases.astype(F32) * TURNS
    quarter = 0.25 - jnp.abs(turns - jnp.round(turns))
    square = quarter * quarter
    result = square * SINE_TERMS[-1] + SINE_TERMS[-2]
    for term in SINE_TERMS[-3::-1]:
        result = result * square + term
    return result * quarter


def dot(a, b):
    return jnp.dot(a, b, preferred_element_type=F32)


def dot_nt(a, b):
    return lax.dot_general(a, b, (((1,), (1,)), ((), ())), preferred_element_type=F32)


def call(kernel, out_shapes, place, args, name, vmem_mib, scratch=(), in_place=None, out_place=pltpu.VMEM, aliases={}):
    spaces = in_place or (pltpu.VMEM,) * len(args)
    vmem = pl.BlockSpec(memory_space=out_place)
    single = isinstance(out_shapes, jax.ShapeDtypeStruct)
    return pl.pallas_call(
        kernel,
        out_shape=out_shapes,
        in_specs=[pl.BlockSpec(memory_space=m) for m in (pltpu.SMEM, *spaces)],
        out_specs=vmem if single else (vmem,) * len(out_shapes),
        scratch_shapes=scratch,
        input_output_aliases=aliases,
        compiler_params=pltpu.CompilerParams(vmem_limit_bytes=vmem_mib << 20),
        name=name,
    )(place, *args)


def like(shape, dtype=BF16):
    return jax.ShapeDtypeStruct(tuple(shape), dtype)


def lanes(index, size):
    return pl.ds(pl.multiple_of(index * size, size), size)


def prepare_kernel(place, inputs, labels, predictions, rows, own, given, wide, tags, sems):
    width = predictions.shape[0]
    part = own.shape[1] // 2
    copies = []
    for j in (0, 1):
        block = 2 * place[1] + (place[2] ^ j)
        at, there = lanes(block, part), slice(j * part, (j + 1) * part)
        copies += [
            pltpu.make_async_copy(predictions.at[:, at], wide.at[:, there], sems.at[3 * j]),
            pltpu.make_async_copy(labels.at[:, at], tags.at[:, there], sems.at[3 * j + 1]),
            pltpu.make_async_copy(inputs.at[at], rows.at[there], sems.at[3 * j + 2]),
        ]
    for copy in copies:
        copy.start()
    tail = own.shape[0] - width
    own[width:], given[width:] = (jnp.zeros((tail, 2 * part), BF16),) * 2
    for j in (0, 1):
        copies[3 * j].wait()
        copies[3 * j + 1].wait()
        there = slice(j * part, (j + 1) * part)
        classes = lax.broadcasted_iota(jnp.int32, (width, part), 0) + place[2] * width
        residual = ((classes == tags[:, there]).astype(F32) - wide[:, there]).astype(BF16)
        own[:width, there] = residual
        given[:width, (1 - j) * part:(2 - j) * part] = residual
    for j in (0, 1):
        copies[3 * j + 2].wait()


def high_low(x):
    high = x.astype(BF16)
    return high, (x - high.astype(F32)).astype(BF16)


def split_kernel(place, x, high, low):
    high[...], low[...] = high_low(x[...])


TILE = 512


def block_kernel(place, rows, w_own, w_other, p_own, p_other, high, low, out, own_slice, feats):
    inputs = rows[:feats.shape[0]]
    half, depth = w_own.shape[1], high.shape[0]
    total = None
    for i, (weights, phases) in enumerate(((w_own, p_own), (w_other, p_other))):
        for k in range(0, half, TILE):
            at = pl.ds(pl.multiple_of((place[2] ^ i) * half + k, TILE), TILE)
            tile = cosine(dot(inputs, weights[:, k:k + TILE]), phases[:, k:k + TILE]).astype(BF16)
            feats[:, at] = tile
            product = dot_nt(tile, high[:, at]) + dot_nt(tile, low[:, at])
            total = product if total is None else total + product
    out[:, :depth], out[:, depth:] = high_low(total)
    own_slice[...] = feats[:, lanes(place[0], depth)]


def product_of(refs, classes):
    total, short = None, None
    for residual, q in zip(refs[::2], refs[1::2]):
        left, right = residual[:classes], q[...]
        if right.shape[0] < 256:
            if short is None:
                short = left[:, :right.shape[0]], right
                continue
            at = slice(0, right.shape[0]) if left.shape[1] == right.shape[0] else slice(right.shape[0], None)
            left = jnp.concatenate([short[0], left[:, at]], axis=1)
            right = jnp.concatenate([short[1], right], axis=0)
            short = None
        product = dot(left, right)
        depth = product.shape[1] // 2
        product = product[:, :depth] + product[:, depth:]
        total = product if total is None else total + product
    return total


def begin_kernel(earlier, place, *refs):
    *pieces, out = refs
    total = product_of(pieces[earlier:], out.shape[0])
    out[...] = pieces[0][...] + total if earlier else total


def update_kernel(place, begun, *refs):
    *pieces, update, sent = refs
    total = DAMPING * (begun[...] + product_of(pieces, begun.shape[0]))
    update[...] = total
    sent[...] = total.astype(BF16)


def far_kernel(place, sent, sent_other, feats, out):
    size = sent.shape[0]
    for i, update in enumerate((sent, sent_other)):
        out[i * size:(i + 1) * size] = dot_nt(update[...], feats[...]).astype(BF16)


def change_kernel(n_feats, place, *refs):
    count = (len(refs) - n_feats) // 2
    feats, updates, outs = refs[:n_feats], refs[n_feats:n_feats + count], refs[n_feats + count:]
    rows = feats[0][...] if n_feats == 1 else jnp.concatenate([f[...] for f in feats], axis=0)
    for update, out in zip(updates, outs):
        out[...] = dot_nt(update[...], rows)


def hop_kernel(half, place, change, came, out):
    size, there = came.shape[1], slice(half * out.shape[0], (half + 1) * out.shape[0])
    there = there if came.shape[0] > out.shape[0] else slice(None)
    out[:, :size] = (change[:, :size] + came[there].astype(F32)).astype(BF16)
    if size < out.shape[1]:
        out[:, size:] = change[:, size:].astype(BF16)


def last_kernel(place, change, came, given, out):
    part = out.shape[1] // 2
    for i in (0, 1):
        at, there = slice(i * part, (i + 1) * part), slice((1 - i) * part, (2 - i) * part)
        total = change[:, at] + came[:, at].astype(F32) + given[:, there].astype(F32)
        out[:, at] = total.astype(BF16)


def apply_kernel(which, place, predictions, change, *refs):
    new, total, sems = refs[-3:]
    width, part = total.shape[0], total.shape[1] // 2
    copies = []
    for j in (0, 1):
        at, there = lanes(2 * (place[1] ^ which) + (place[2] ^ j), part), slice(j * part, (j + 1) * part)
        total[:, there] = predictions[:, at] + change[:width, there].astype(F32)
        copies.append(pltpu.make_async_copy(total.at[:, there], new.at[:, at], sems.at[j]))
        copies[j].start()
    for copy in copies:
        copy.wait()


def swap(x, axes, pairs):
    return lax.ppermute(x, axes, [p for a, b in pairs for p in ((a, b), (b, a))])


def after(arrays, *others):
    return lax.optimization_barrier((*arrays, *others))[:len(arrays)]


def ring_shards(n_rows, inputs, projection, phases, inverse_blocks, labels, predictions, coefficients):
    ring = [2 * z for z in range(n_rows)] + [2 * z + 1 for z in reversed(range(n_rows))]
    size = len(ring)
    even = [(ring[i], ring[i + 1]) for i in range(0, size, 2)]
    odd = [(ring[i], ring[(i + 1) % size]) for i in range(1, size, 2)]
    ways = [[(2 * a + c, 2 * b + c) for c, pairs in enumerate(way) for a, b in pairs]
            for way in ((even, odd), (odd, even))]
    S = lambda x: swap(x, ("rows", "blocks", "cols"), ways[0])
    T = lambda x: swap(x, ("rows", "blocks", "cols"), ways[1])
    C = lambda x: swap(x, "cols", [(0, 1)])

    place = jnp.stack([lax.axis_index(a) for a in ("rows", "blocks", "cols")]).astype(jnp.int32)
    local_rows, width = predictions.shape
    part = local_rows // 4
    padded = -(-width // LANES) * LANES
    predictions, coefficients = predictions.T, coefficients.T
    depth = coefficients.shape[1]

    dma = pltpu.SemaphoreType.DMA
    block_rows = like((2 * part, inputs.shape[1]))
    x0, own, given = call(
        prepare_kernel, (block_rows, *(like((padded, 2 * part)),) * 2), place,
        tuple(pltpu.with_memory_space_constraint(a, pltpu.HBM) for a in (inputs, labels[None, :], predictions)),
        "prepare", 6,
        (pltpu.VMEM((width, 2 * part), F32), pltpu.VMEM((1, 2 * part), jnp.int32), dma((6,))), (pltpu.HBM,) * 3,
    )
    given = C(given)
    (x0,) = after((x0,), given)
    r0 = jnp.concatenate([own, given], axis=0)
    weights = (projection, C(projection))
    phases = phases[None, :]
    phases = (phases, C(phases))
    inverse = call(
        split_kernel, (like(inverse_blocks.shape[1:]),) * 2, place, (inverse_blocks[0],), "split", 14
    )

    def block(rows, size):
        scratch = (pltpu.VMEM((size, 2 * projection.shape[1]), BF16),)
        return call(
            block_kernel, (like((size, 2 * depth)), like((size, depth))), place,
            (rows, *weights, *phases, *inverse), "block", 16, scratch,
        )

    def begin(pairs, *earlier):
        return call(
            functools.partial(begin_kernel, len(earlier)), like((padded, depth), F32), place,
            (*earlier, *[a for pair in pairs for a in pair]), "begin", 14,
        )

    x1, r1 = S(x0), S(r0)
    q0, f0 = block(x0, part)
    (x1,) = after((x1,), q0)
    x2 = T(x1)
    q1, f1 = block(x1, 2 * part)
    (r1,) = after((r1,), q1)
    r2 = T(r1)
    (x2,) = after((x2,), q1)
    x3 = S(x2)
    q2, f2 = block(x2, 2 * part)
    (r2,) = after((r2,), q2)
    r3 = S(r2)
    theirs = lambda r: C(r[padded:])
    q0_other, f0_other = C(q0), C(f0)
    begun = begin([(r0, q0), (r0, q0_other), (r1, q1), (theirs(r1), C(q1))])
    (x3,) = after((x3,), begun, f0_other)
    x4 = T(x3[:part])
    q3, f3 = block(x3, 2 * part)
    (r3,) = after((r3,), q3)
    r4 = T(r3[:, :part])
    (x4,) = after((x4,), q3)
    q4, f4 = block(x4, part)
    begun = begin([(r2, q2), (theirs(r2), C(q2)), (r3, q3), (theirs(r3), C(q3))], begun)
    update, sent = call(
        update_kernel, (like((padded, depth), F32), like((padded, depth))), place,
        (begun, r4, q4, theirs(r4), C(q4)), "update", 14,
    )

    whole, wide = like((padded, 2 * part)), like((padded, 2 * part), F32)
    sent_other = C(sent)

    def changes(feats, *updates):
        return call(
            functools.partial(change_kernel, len(feats)), (wide,) * len(updates), place,
            (*feats, *updates), "change", 8,
        )

    hop = lambda half, own, came: call(functools.partial(hop_kernel, half), whole, place, (own, came), "hop", 4)
    first = T(call(far_kernel, like((2 * padded, part)), place, (sent, sent_other, f4), "far", 6))
    ahead = changes((f3,), sent, sent_other)
    (first,) = after((first,), *ahead)
    second = first
    for way, feats in ((S, (f2,)), (T, (f1,)), (S, (f0, f0_other))):
        second_sum = hop(1, ahead[1], second)
        (first,) = after((first,), second_sum)
        first_sum = hop(0, ahead[0], first)
        second, first = way(second_sum), way(first_sum)
        updates = after((sent, sent_other), first_sum)
        ahead = changes(feats, *updates[:1 if len(feats) == 2 else 2])
        (second,) = after((second,), first_sum, *ahead)
    own = call(last_kernel, whole, place, (ahead[0], first, C(second)), "last", 4)
    new = None
    for i in (0, 1):
        change = swap(own, "blocks", [(0, 1)]) if i else own
        earlier = (new,) if i else ()
        new = call(
            functools.partial(apply_kernel, i), like(predictions.shape, F32), place,
            (predictions, change, *earlier), "apply", 6, (pltpu.VMEM((width, 2 * part), F32), dma((2,))),
            (pltpu.VMEM, pltpu.VMEM, *(pl.ANY,) * i), pl.ANY, {3: 0} if i else {},
        )
    return (coefficients + update[:width]).T, new.T


def plain_shards(inputs, projection, phases, inverse_blocks, labels, predictions, coefficients):
    out_width = predictions.shape[1]
    classes = lax.axis_index("cols") * out_width + jnp.arange(out_width, dtype=jnp.int32)
    onehot = (labels[:, None] == classes[None, :]).astype(F32)
    residual = (onehot - predictions).astype(BF16)
    angles = dot(inputs, projection) + phases.astype(F32)[None, :]
    half_features = jnp.cos(angles).astype(BF16)
    features_full = lax.all_gather(half_features, "cols", axis=1, tiled=True)
    own_gradient = lax.psum_scatter(
        lax.dot_general(features_full, residual, (((0,), (0,)), ((), ())), preferred_element_type=F32),
        "rows", scatter_dimension=0, tiled=True,
    )
    gradient_full = lax.all_gather(own_gradient, "rows", axis=0, tiled=True)
    update = DAMPING * jnp.dot(inverse_blocks[0], gradient_full, precision=lax.Precision.HIGHEST)
    sent = lax.all_gather(update.astype(BF16), "rows", axis=0, tiled=True)
    summed = lax.psum(dot(features_full, sent), "blocks")
    return coefficients + update, predictions + summed


def solution(mesh):
    n_rows, n_blocks = mesh.shape["rows"], mesh.shape["blocks"]
    small_ring = n_blocks == 2 and n_rows == 4 and mesh.shape["cols"] == 2
    shards = functools.partial(ring_shards, n_rows) if small_ring else plain_shards
    return jax.shard_map(
        shards,
        mesh=mesh,
        in_specs=(
            P(("groups", "rows"), None),
            P(None, ("groups", "blocks", "cols")),
            P(("groups", "blocks", "cols")),
            P(("groups", "blocks"), "rows", None),
            P(("groups", "rows")),
            P(("groups", "rows"), "cols"),
            P(("groups", "blocks", "rows"), "cols"),
        ),
        out_specs=(P(("groups", "blocks", "rows"), "cols"), P(("groups", "rows"), "cols")),
        check_vma=False,
    )
```

```python
import functools

import jax
import jax.numpy as jnp
from jax import lax
from jax.experimental import pallas as pl
from jax.experimental.pallas import tpu as pltpu
from jax.sharding import PartitionSpec as P

DAMPING = 0.5
F32, BF16 = jnp.float32, jnp.bfloat16
LANES = 128

SINE_TERMS = (
    6.283185280127733, -41.341680582549685, 81.60247253767959, -76.5810396203459, 39.75848375303386
)
TURNS = 0.15915494309189535


def cosine(angles, phases):
    turns = angles * TURNS + phases.astype(F32) * TURNS
    quarter = 0.25 - jnp.abs(turns - jnp.round(turns))
    square = quarter * quarter
    result = square * SINE_TERMS[-1] + SINE_TERMS[-2]
    for term in SINE_TERMS[-3::-1]:
        result = result * square + term
    return result * quarter


def dot(a, b):
    return jnp.dot(a, b, preferred_element_type=F32)


def dot_nt(a, b):
    return lax.dot_general(a, b, (((1,), (1,)), ((), ())), preferred_element_type=F32)


def call(kernel, out_shapes, place, args, name, vmem_mib, scratch=(), in_place=None, out_place=pltpu.VMEM, aliases={}):
    spaces = in_place or (pltpu.VMEM,) * len(args)
    vmem = pl.BlockSpec(memory_space=out_place)
    single = isinstance(out_shapes, jax.ShapeDtypeStruct)
    return pl.pallas_call(
        kernel,
        out_shape=out_shapes,
        in_specs=[pl.BlockSpec(memory_space=m) for m in (pltpu.SMEM, *spaces)],
        out_specs=vmem if single else (vmem,) * len(out_shapes),
        scratch_shapes=scratch,
        input_output_aliases=aliases,
        compiler_params=pltpu.CompilerParams(vmem_limit_bytes=vmem_mib << 20),
        name=name,
    )(place, *args)


def like(shape, dtype=BF16):
    return jax.ShapeDtypeStruct(tuple(shape), dtype)


def lanes(index, size):
    return pl.ds(pl.multiple_of(index * size, size), size)


def prepare_kernel(place, inputs, labels, predictions, rows, own, given, wide, tags, sems):
    width = predictions.shape[0]
    part = own.shape[1] // 2
    copies = []
    for j in (0, 1):
        block = 2 * place[1] + (place[2] ^ j)
        at, there = lanes(block, part), slice(j * part, (j + 1) * part)
        copies += [
            pltpu.make_async_copy(predictions.at[:, at], wide.at[:, there], sems.at[3 * j]),
            pltpu.make_async_copy(labels.at[:, at], tags.at[:, there], sems.at[3 * j + 1]),
            pltpu.make_async_copy(inputs.at[at], rows.at[there], sems.at[3 * j + 2]),
        ]
    for copy in copies:
        copy.start()
    tail = own.shape[0] - width
    own[width:], given[width:] = (jnp.zeros((tail, 2 * part), BF16),) * 2
    for j in (0, 1):
        copies[3 * j].wait()
        copies[3 * j + 1].wait()
        there = slice(j * part, (j + 1) * part)
        classes = lax.broadcasted_iota(jnp.int32, (width, part), 0) + place[2] * width
        residual = ((classes == tags[:, there]).astype(F32) - wide[:, there]).astype(BF16)
        own[:width, there] = residual
        given[:width, (1 - j) * part:(2 - j) * part] = residual
    for j in (0, 1):
        copies[3 * j + 2].wait()


def high_low(x):
    high = x.astype(BF16)
    return high, (x - high.astype(F32)).astype(BF16)


def split_kernel(place, x, high, low):
    high[...], low[...] = high_low(x[...])


TILE = 512


def block_kernel(place, rows, w_own, w_other, p_own, p_other, high, low, out, own_slice, feats):
    inputs = rows[:feats.shape[0]]
    half, depth = w_own.shape[1], high.shape[0]
    total = None
    for i, (weights, phases) in enumerate(((w_own, p_own), (w_other, p_other))):
        for k in range(0, half, TILE):
            at = pl.ds(pl.multiple_of((place[2] ^ i) * half + k, TILE), TILE)
            tile = cosine(dot(inputs, weights[:, k:k + TILE]), phases[:, k:k + TILE]).astype(BF16)
            feats[:, at] = tile
            product = dot_nt(tile, high[:, at]) + dot_nt(tile, low[:, at])
            total = product if total is None else total + product
    out[:, :depth], out[:, depth:] = high_low(total)
    own_slice[...] = feats[:, lanes(place[0], depth)]


def product_of(refs, classes):
    total, short = None, None
    for residual, q in zip(refs[::2], refs[1::2]):
        left, right = residual[:classes], q[...]
        if right.shape[0] < 256:
            if short is None:
                short = left[:, :right.shape[0]], right
                continue
            at = slice(0, right.shape[0]) if left.shape[1] == right.shape[0] else slice(right.shape[0], None)
            left = jnp.concatenate([short[0], left[:, at]], axis=1)
            right = jnp.concatenate([short[1], right], axis=0)
            short = None
        product = dot(left, right)
        depth = product.shape[1] // 2
        product = product[:, :depth] + product[:, depth:]
        total = product if total is None else total + product
    return total


def begin_kernel(earlier, place, *refs):
    *pieces, out = refs
    total = product_of(pieces[earlier:], out.shape[0])
    out[...] = pieces[0][...] + total if earlier else total


def update_kernel(place, begun, *refs):
    *pieces, update, sent = refs
    total = DAMPING * (begun[...] + product_of(pieces, begun.shape[0]))
    update[...] = total
    sent[...] = total.astype(BF16)


def start_kernel(n_feats, place, sent, *refs):
    rows = refs[0][...] if n_feats == 1 else jnp.concatenate([f[...] for f in refs[:n_feats]], axis=0)
    refs[-1][...] = dot_nt(sent[...], rows).astype(BF16)


def change_kernel(n_feats, place, sent, *refs):
    rows = refs[0][...] if n_feats == 1 else jnp.concatenate([f[...] for f in refs[:n_feats]], axis=0)
    refs[-1][...] = dot_nt(sent[...], rows)


def hop_kernel(place, change, came, out):
    out[...] = (change[...] + came[...].astype(F32)).astype(BF16)


def last_kernel(place, change, came, given, out):
    part = out.shape[1] // 2
    for i in (0, 1):
        at, there = slice(i * part, (i + 1) * part), slice((1 - i) * part, (2 - i) * part)
        total = change[:, at] + came[:, at].astype(F32) + given[:, there].astype(F32)
        out[:, at] = total.astype(BF16)


def apply_kernel(which, place, predictions, change, *refs):
    new, total, sems = refs[-3:]
    width, part = total.shape[0], total.shape[1] // 2
    copies = []
    for j in (0, 1):
        at, there = lanes(2 * (place[1] ^ which) + (place[2] ^ j), part), slice(j * part, (j + 1) * part)
        total[:, there] = predictions[:, at] + change[:width, there].astype(F32)
        copies.append(pltpu.make_async_copy(total.at[:, there], new.at[:, at], sems.at[j]))
        copies[j].start()
    for copy in copies:
        copy.wait()


def swap(x, axes, pairs):
    return lax.ppermute(x, axes, [p for a, b in pairs for p in ((a, b), (b, a))])


def after(arrays, *others):
    return lax.optimization_barrier((*arrays, *others))[:len(arrays)]


def ring_shards(n_rows, inputs, projection, phases, inverse_blocks, labels, predictions, coefficients):
    ring = [2 * z for z in range(n_rows)] + [2 * z + 1 for z in reversed(range(n_rows))]
    size = len(ring)
    even = [(ring[i], ring[i + 1]) for i in range(0, size, 2)]
    odd = [(ring[i], ring[(i + 1) % size]) for i in range(1, size, 2)]
    ways = [[(2 * a + c, 2 * b + c) for c, pairs in enumerate(way) for a, b in pairs]
            for way in ((even, odd), (odd, even))]
    S = lambda x: swap(x, ("rows", "blocks", "cols"), ways[0])
    T = lambda x: swap(x, ("rows", "blocks", "cols"), ways[1])
    C = lambda x: swap(x, "cols", [(0, 1)])

    place = jnp.stack([lax.axis_index(a) for a in ("rows", "blocks", "cols")]).astype(jnp.int32)
    local_rows, width = predictions.shape
    part = local_rows // 4
    padded = -(-width // LANES) * LANES
    predictions, coefficients = predictions.T, coefficients.T
    depth = coefficients.shape[1]

    dma = pltpu.SemaphoreType.DMA
    block_rows = like((2 * part, inputs.shape[1]))
    x0, own, given = call(
        prepare_kernel, (block_rows, *(like((padded, 2 * part)),) * 2), place,
        tuple(pltpu.with_memory_space_constraint(a, pltpu.HBM) for a in (inputs, labels[None, :], predictions)),
        "prepare", 6,
        (pltpu.VMEM((width, 2 * part), F32), pltpu.VMEM((1, 2 * part), jnp.int32), dma((6,))), (pltpu.HBM,) * 3,
    )
    given = C(given)
    (x0,) = after((x0,), given)
    r0 = jnp.concatenate([own, given], axis=0)
    weights = (projection, C(projection))
    phases = phases[None, :]
    phases = (phases, C(phases))
    inverse = call(
        split_kernel, (like(inverse_blocks.shape[1:]),) * 2, place, (inverse_blocks[0],), "split", 14
    )

    def block(rows, size):
        scratch = (pltpu.VMEM((size, 2 * projection.shape[1]), BF16),)
        return call(
            block_kernel, (like((size, 2 * depth)), like((size, depth))), place,
            (rows, *weights, *phases, *inverse), "block", 16, scratch,
        )

    def begin(pairs, *earlier):
        return call(
            functools.partial(begin_kernel, len(earlier)), like((padded, depth), F32), place,
            (*earlier, *[a for pair in pairs for a in pair]), "begin", 14,
        )

    x1, r1 = S(x0), S(r0)
    q0, f0 = block(x0, part)
    (x1,) = after((x1,), q0)
    x2 = T(x1)
    q1, f1 = block(x1, 2 * part)
    (r1,) = after((r1,), q1)
    r2 = T(r1)
    (x2,) = after((x2,), q1)
    x3 = S(x2)
    q2, f2 = block(x2, 2 * part)
    (r2,) = after((r2,), q2)
    r3 = S(r2)
    theirs = lambda r: C(r[padded:])
    q0_other, f0_other = C(q0), C(f0)
    begun = begin([(r0, q0), (r0, q0_other), (r1, q1), (theirs(r1), C(q1))])
    (x3,) = after((x3,), begun, f0_other)
    x4 = T(x3[:part])
    q3, f3 = block(x3, 2 * part)
    (r3,) = after((r3,), q3)
    r4 = T(r3[:, :part])
    (x4,) = after((x4,), q3)
    q4, f4 = block(x4, part)
    f4_other = C(f4)
    begun = begin([(r2, q2), (theirs(r2), C(q2)), (r3, q3), (theirs(r3), C(q3))], begun)
    (begun,) = after((begun,), f4_other)
    update, sent = call(
        update_kernel, (like((padded, depth), F32), like((padded, depth))), place,
        (begun, r4, q4, theirs(r4), C(q4)), "update", 14,
    )

    whole, wide = like((padded, 2 * part)), like((padded, 2 * part), F32)

    def product(kernel, out, update, *feats):
        kernel = functools.partial(kernel, len(feats))
        return call(kernel, out, place, (update, *feats), "change", 6)

    hop = lambda ahead, came: call(hop_kernel, whole, place, (ahead, came), "hop", 4)
    first = product(start_kernel, whole, sent, f4, f4_other)
    (sent_other,) = after((C(sent),), first)
    first = T(first)
    second = product(start_kernel, whole, sent_other, f3)
    ahead = product(change_kernel, wide, after((sent,), second)[0], f3)
    second = S(second)
    (first,) = after((first,), ahead)
    for way, feats, later in ((S, f2, f2), (T, f1, f1)):
        total = hop(ahead, first)
        first = way(total)
        ahead = product(change_kernel, wide, after((sent_other,), total)[0], feats)
        (second,) = after((second,), ahead)
        total = hop(ahead, second)
        second = (T if way is S else S)(total)
        ahead = product(change_kernel, wide, after((sent,), total)[0], later)
        (first,) = after((first,), ahead)
    total = hop(ahead, first)
    first = S(total)
    ahead = product(change_kernel, wide, after((sent,), total)[0], f0, f0_other)
    given = C(after((second,), ahead)[0])
    (first,) = after((first,), given)
    own = call(last_kernel, whole, place, (ahead, first, given), "last", 4)
    new = None
    for i in (0, 1):
        change = swap(own, "blocks", [(0, 1)]) if i else own
        earlier = (new,) if i else ()
        new = call(
            functools.partial(apply_kernel, i), like(predictions.shape, F32), place,
            (predictions, change, *earlier), "apply", 6, (pltpu.VMEM((width, 2 * part), F32), dma((2,))),
            (pltpu.VMEM, pltpu.VMEM, *(pl.ANY,) * i), pl.ANY, {3: 0} if i else {},
        )
    return (coefficients + update[:width]).T, new.T


def plain_shards(inputs, projection, phases, inverse_blocks, labels, predictions, coefficients):
    out_width = predictions.shape[1]
    classes = lax.axis_index("cols") * out_width + jnp.arange(out_width, dtype=jnp.int32)
    onehot = (labels[:, None] == classes[None, :]).astype(F32)
    residual = (onehot - predictions).astype(BF16)
    angles = dot(inputs, projection) + phases.astype(F32)[None, :]
    half_features = jnp.cos(angles).astype(BF16)
    features_full = lax.all_gather(half_features, "cols", axis=1, tiled=True)
    own_gradient = lax.psum_scatter(
        lax.dot_general(features_full, residual, (((0,), (0,)), ((), ())), preferred_element_type=F32),
        "rows", scatter_dimension=0, tiled=True,
    )
    gradient_full = lax.all_gather(own_gradient, "rows", axis=0, tiled=True)
    update = DAMPING * jnp.dot(inverse_blocks[0], gradient_full, precision=lax.Precision.HIGHEST)
    sent = lax.all_gather(update.astype(BF16), "rows", axis=0, tiled=True)
    summed = lax.psum(dot(features_full, sent), "blocks")
    return coefficients + update, predictions + summed


def solution(mesh):
    n_rows, n_blocks = mesh.shape["rows"], mesh.shape["blocks"]
    small_ring = n_blocks == 2 and n_rows == 4 and mesh.shape["cols"] == 2
    shards = functools.partial(ring_shards, n_rows) if small_ring else plain_shards
    return jax.shard_map(
        shards,
        mesh=mesh,
        in_specs=(
            P(("groups", "rows"), None),
            P(None, ("groups", "blocks", "cols")),
            P(("groups", "blocks", "cols")),
            P(("groups", "blocks"), "rows", None),
            P(("groups", "rows")),
            P(("groups", "rows"), "cols"),
            P(("groups", "blocks", "rows"), "cols"),
        ),
        out_specs=(P(("groups", "blocks", "rows"), "cols"), P(("groups", "rows"), "cols")),
        check_vma=False,
    )
```

```python
import functools

import jax
import jax.numpy as jnp
from jax import lax
from jax.experimental import pallas as pl
from jax.experimental.pallas import tpu as pltpu
from jax.sharding import PartitionSpec as P

DAMPING = 0.5
F32, BF16 = jnp.float32, jnp.bfloat16
LANES = 128

SINE_TERMS = (
    6.283185280127733, -41.341680582549685, 81.60247253767959, -76.5810396203459, 39.75848375303386
)
TURNS = 0.15915494309189535


def cosine(angles, phases):
    turns = angles * TURNS + phases.astype(F32) * TURNS
    quarter = 0.25 - jnp.abs(turns - jnp.round(turns))
    square = quarter * quarter
    result = square * SINE_TERMS[-1] + SINE_TERMS[-2]
    for term in SINE_TERMS[-3::-1]:
        result = result * square + term
    return result * quarter


def dot(a, b):
    return jnp.dot(a, b, preferred_element_type=F32)


def dot_nt(a, b):
    return lax.dot_general(a, b, (((1,), (1,)), ((), ())), preferred_element_type=F32)


def call(kernel, out_shapes, place, args, name, vmem_mib, scratch=(), in_place=None, out_place=pltpu.VMEM, aliases={}):
    spaces = in_place or (pltpu.VMEM,) * len(args)
    vmem = pl.BlockSpec(memory_space=out_place)
    single = isinstance(out_shapes, jax.ShapeDtypeStruct)
    return pl.pallas_call(
        kernel,
        out_shape=out_shapes,
        in_specs=[pl.BlockSpec(memory_space=m) for m in (pltpu.SMEM, *spaces)],
        out_specs=vmem if single else (vmem,) * len(out_shapes),
        scratch_shapes=scratch,
        input_output_aliases=aliases,
        compiler_params=pltpu.CompilerParams(vmem_limit_bytes=vmem_mib << 20),
        name=name,
    )(place, *args)


def like(shape, dtype=BF16):
    return jax.ShapeDtypeStruct(tuple(shape), dtype)


def lanes(index, size):
    return pl.ds(pl.multiple_of(index * size, size), size)


def prepare_kernel(place, inputs, labels, predictions, rows, own, given, wide, tags, sems):
    width = predictions.shape[0]
    part = own.shape[1] // 2
    copies = []
    for j in (0, 1):
        block = 2 * place[1] + (place[2] ^ j)
        at, there = lanes(block, part), slice(j * part, (j + 1) * part)
        copies += [
            pltpu.make_async_copy(predictions.at[:, at], wide.at[:, there], sems.at[3 * j]),
            pltpu.make_async_copy(labels.at[:, at], tags.at[:, there], sems.at[3 * j + 1]),
            pltpu.make_async_copy(inputs.at[at], rows.at[there], sems.at[3 * j + 2]),
        ]
    for copy in copies:
        copy.start()
    tail = own.shape[0] - width
    own[width:], given[width:] = (jnp.zeros((tail, 2 * part), BF16),) * 2
    for j in (0, 1):
        copies[3 * j].wait()
        copies[3 * j + 1].wait()
        there = slice(j * part, (j + 1) * part)
        classes = lax.broadcasted_iota(jnp.int32, (width, part), 0) + place[2] * width
        residual = ((classes == tags[:, there]).astype(F32) - wide[:, there]).astype(BF16)
        own[:width, there] = residual
        given[:width, (1 - j) * part:(2 - j) * part] = residual
    for j in (0, 1):
        copies[3 * j + 2].wait()


def high_low(x):
    high = x.astype(BF16)
    return high, (x - high.astype(F32)).astype(BF16)


def split_kernel(place, x, high, low):
    high[...], low[...] = high_low(x[...])


TILE = 512


def block_kernel(place, rows, w_own, w_other, p_own, p_other, high, low, out, own_slice, feats):
    inputs = rows[:feats.shape[0]]
    half, depth = w_own.shape[1], high.shape[0]
    total = None
    for i, (weights, phases) in enumerate(((w_own, p_own), (w_other, p_other))):
        for k in range(0, half, TILE):
            at = pl.ds(pl.multiple_of((place[2] ^ i) * half + k, TILE), TILE)
            tile = cosine(dot(inputs, weights[:, k:k + TILE]), phases[:, k:k + TILE]).astype(BF16)
            feats[:, at] = tile
            product = dot_nt(tile, high[:, at]) + dot_nt(tile, low[:, at])
            total = product if total is None else total + product
    out[:, :depth], out[:, depth:] = high_low(total)
    own_slice[...] = feats[:, lanes(place[0], depth)]


def product_of(refs, classes):
    total, short = None, None
    for residual, q in zip(refs[::2], refs[1::2]):
        left, right = residual[:classes], q[...]
        if right.shape[0] < 256:
            if short is None:
                short = left[:, :right.shape[0]], right
                continue
            at = slice(0, right.shape[0]) if left.shape[1] == right.shape[0] else slice(right.shape[0], None)
            left = jnp.concatenate([short[0], left[:, at]], axis=1)
            right = jnp.concatenate([short[1], right], axis=0)
            short = None
        product = dot(left, right)
        depth = product.shape[1] // 2
        product = product[:, :depth] + product[:, depth:]
        total = product if total is None else total + product
    return total


def begin_kernel(earlier, place, *refs):
    *pieces, out = refs
    total = product_of(pieces[earlier:], out.shape[0])
    out[...] = pieces[0][...] + total if earlier else total


def update_kernel(place, begun, *refs):
    *pieces, update, sent = refs
    total = DAMPING * (begun[...] + product_of(pieces, begun.shape[0]))
    update[...] = total
    sent[...] = total.astype(BF16)


def change_kernel(counts, place, sent, *refs):
    at = 0
    for count, out in zip(counts, refs[sum(counts):]):
        rows = refs[at][...] if count == 1 else jnp.concatenate([f[...] for f in refs[at:at + count]], axis=0)
        out[...] = dot_nt(sent[...], rows).astype(out.dtype)
        at += count


def hop_kernel(place, change, came, out):
    out[...] = (change[...] + came[...].astype(F32)).astype(BF16)


def last_kernel(place, change, came, given, out):
    part = out.shape[1] // 2
    for i in (0, 1):
        at, there = slice(i * part, (i + 1) * part), slice((1 - i) * part, (2 - i) * part)
        total = change[:, at] + came[:, at].astype(F32) + given[:, there].astype(F32)
        out[:, at] = total.astype(BF16)


def apply_kernel(which, place, predictions, change, *refs):
    new, total, sems = refs[-3:]
    width, part = total.shape[0], total.shape[1] // 2
    copies = []
    for j in (0, 1):
        at, there = lanes(2 * (place[1] ^ which) + (place[2] ^ j), part), slice(j * part, (j + 1) * part)
        total[:, there] = predictions[:, at] + change[:width, there].astype(F32)
        copies.append(pltpu.make_async_copy(total.at[:, there], new.at[:, at], sems.at[j]))
        copies[j].start()
    for copy in copies:
        copy.wait()


def swap(x, axes, pairs):
    return lax.ppermute(x, axes, [p for a, b in pairs for p in ((a, b), (b, a))])


def after(arrays, *others):
    return lax.optimization_barrier((*arrays, *others))[:len(arrays)]


def ring_shards(n_rows, inputs, projection, phases, inverse_blocks, labels, predictions, coefficients):
    ring = [2 * z for z in range(n_rows)] + [2 * z + 1 for z in reversed(range(n_rows))]
    size = len(ring)
    even = [(ring[i], ring[i + 1]) for i in range(0, size, 2)]
    odd = [(ring[i], ring[(i + 1) % size]) for i in range(1, size, 2)]
    ways = [[(2 * a + c, 2 * b + c) for c, pairs in enumerate(way) for a, b in pairs]
            for way in ((even, odd), (odd, even))]
    S = lambda x: swap(x, ("rows", "blocks", "cols"), ways[0])
    T = lambda x: swap(x, ("rows", "blocks", "cols"), ways[1])
    C = lambda x: swap(x, "cols", [(0, 1)])

    place = jnp.stack([lax.axis_index(a) for a in ("rows", "blocks", "cols")]).astype(jnp.int32)
    local_rows, width = predictions.shape
    part = local_rows // 4
    padded = -(-width // LANES) * LANES
    predictions, coefficients = predictions.T, coefficients.T
    depth = coefficients.shape[1]

    dma = pltpu.SemaphoreType.DMA
    block_rows = like((2 * part, inputs.shape[1]))
    x0, own, given = call(
        prepare_kernel, (block_rows, *(like((padded, 2 * part)),) * 2), place,
        tuple(pltpu.with_memory_space_constraint(a, pltpu.HBM) for a in (inputs, labels[None, :], predictions)),
        "prepare", 6,
        (pltpu.VMEM((width, 2 * part), F32), pltpu.VMEM((1, 2 * part), jnp.int32), dma((6,))), (pltpu.HBM,) * 3,
    )
    given = C(given)
    (x0,) = after((x0,), given)
    r0 = jnp.concatenate([own, given], axis=0)
    weights = (projection, C(projection))
    phases = phases[None, :]
    phases = (phases, C(phases))
    inverse = call(
        split_kernel, (like(inverse_blocks.shape[1:]),) * 2, place, (inverse_blocks[0],), "split", 14
    )

    def block(rows, size):
        scratch = (pltpu.VMEM((size, 2 * projection.shape[1]), BF16),)
        return call(
            block_kernel, (like((size, 2 * depth)), like((size, depth))), place,
            (rows, *weights, *phases, *inverse), "block", 16, scratch,
        )

    def begin(pairs, *earlier):
        return call(
            functools.partial(begin_kernel, len(earlier)), like((padded, depth), F32), place,
            (*earlier, *[a for pair in pairs for a in pair]), "begin", 14,
        )

    x1, r1 = S(x0), S(r0)
    q0, f0 = block(x0, part)
    (x1,) = after((x1,), q0)
    x2 = T(x1)
    q1, f1 = block(x1, 2 * part)
    (r1,) = after((r1,), q1)
    r2 = T(r1)
    (x2,) = after((x2,), q1)
    x3 = S(x2)
    q2, f2 = block(x2, 2 * part)
    (r2,) = after((r2,), q2)
    r3 = S(r2)
    theirs = lambda r: C(r[padded:])
    q0_other, f0_other = C(q0), C(f0)
    begun = begin([(r0, q0), (r0, q0_other), (r1, q1), (theirs(r1), C(q1))])
    (x3,) = after((x3,), begun, f0_other)
    x4 = T(x3[:part])
    q3, f3 = block(x3, 2 * part)
    (r3,) = after((r3,), q3)
    r4 = T(r3[:, :part])
    (x4,) = after((x4,), q3)
    q4, f4 = block(x4, part)
    f4_other = C(f4)
    begun = begin([(r2, q2), (theirs(r2), C(q2)), (r3, q3), (theirs(r3), C(q3))], begun)
    (begun,) = after((begun,), f4_other)
    update, sent = call(
        update_kernel, (like((padded, depth), F32), like((padded, depth))), place,
        (begun, r4, q4, theirs(r4), C(q4)), "update", 14,
    )

    whole, wide = like((padded, 2 * part)), like((padded, 2 * part), F32)

    def changes(update, blocks, outs):
        counts = tuple(len(f) for f in blocks)
        return call(
            functools.partial(change_kernel, counts), outs, place, (update, *[f for b in blocks for f in b]), "change", 8
        )

    hop = lambda ahead, came: call(hop_kernel, whole, place, (ahead, came), "hop", 4)
    (first,) = changes(sent, [(f4, f4_other)], (whole,))
    (sent_other,) = after((C(sent),), first)
    ahead = changes(after((sent,), first)[0], [(f3,), (f2,), (f1,), (f0, f0_other)], (wide,) * 4)
    first = T(first)
    (sent_other,) = after((sent_other,), *ahead)
    second, *behind = changes(sent_other, [(f3,), (f2,), (f1,)], (whole, wide, wide))
    (first,) = after((first,), second)
    second = S(second)
    for i, (way, back) in enumerate(((S, T), (T, S), (S, None))):
        total = hop(ahead[i], first)
        first = way(total)
        (second,) = after((second,), total)
        if back:
            total = hop(behind[i], second)
            second = back(total)
            (first,) = after((first,), total)
    given = C(second)
    (first,) = after((first,), given)
    ahead = ahead[3]
    own = call(last_kernel, whole, place, (ahead, first, given), "last", 4)
    new = None
    for i in (0, 1):
        change = swap(own, "blocks", [(0, 1)]) if i else own
        earlier = (new,) if i else ()
        new = call(
            functools.partial(apply_kernel, i), like(predictions.shape, F32), place,
            (predictions, change, *earlier), "apply", 6, (pltpu.VMEM((width, 2 * part), F32), dma((2,))),
            (pltpu.VMEM, pltpu.VMEM, *(pl.ANY,) * i), pl.ANY, {3: 0} if i else {},
        )
    return (coefficients + update[:width]).T, new.T


def plain_shards(inputs, projection, phases, inverse_blocks, labels, predictions, coefficients):
    out_width = predictions.shape[1]
    classes = lax.axis_index("cols") * out_width + jnp.arange(out_width, dtype=jnp.int32)
    onehot = (labels[:, None] == classes[None, :]).astype(F32)
    residual = (onehot - predictions).astype(BF16)
    angles = dot(inputs, projection) + phases.astype(F32)[None, :]
    half_features = jnp.cos(angles).astype(BF16)
    features_full = lax.all_gather(half_features, "cols", axis=1, tiled=True)
    own_gradient = lax.psum_scatter(
        lax.dot_general(features_full, residual, (((0,), (0,)), ((), ())), preferred_element_type=F32),
        "rows", scatter_dimension=0, tiled=True,
    )
    gradient_full = lax.all_gather(own_gradient, "rows", axis=0, tiled=True)
    update = DAMPING * jnp.dot(inverse_blocks[0], gradient_full, precision=lax.Precision.HIGHEST)
    sent = lax.all_gather(update.astype(BF16), "rows", axis=0, tiled=True)
    summed = lax.psum(dot(features_full, sent), "blocks")
    return coefficients + update, predictions + summed


def solution(mesh):
    n_rows, n_blocks = mesh.shape["rows"], mesh.shape["blocks"]
    small_ring = n_blocks == 2 and n_rows == 4 and mesh.shape["cols"] == 2
    shards = functools.partial(ring_shards, n_rows) if small_ring else plain_shards
    return jax.shard_map(
        shards,
        mesh=mesh,
        in_specs=(
            P(("groups", "rows"), None),
            P(None, ("groups", "blocks", "cols")),
            P(("groups", "blocks", "cols")),
            P(("groups", "blocks"), "rows", None),
            P(("groups", "rows")),
            P(("groups", "rows"), "cols"),
            P(("groups", "blocks", "rows"), "cols"),
        ),
        out_specs=(P(("groups", "blocks", "rows"), "cols"), P(("groups", "rows"), "cols")),
        check_vma=False,
    )
```

```python
import functools

import jax
import jax.numpy as jnp
from jax import lax
from jax.experimental import pallas as pl
from jax.experimental.pallas import tpu as pltpu
from jax.sharding import PartitionSpec as P

DAMPING = 0.5
F32, BF16 = jnp.float32, jnp.bfloat16
LANES = 128

SINE_TERMS = (
    6.283185280127733, -41.341680582549685, 81.60247253767959, -76.5810396203459, 39.75848375303386
)
TURNS = 0.15915494309189535


def cosine(angles, phases):
    turns = angles * TURNS + phases.astype(F32) * TURNS
    quarter = 0.25 - jnp.abs(turns - jnp.round(turns))
    square = quarter * quarter
    result = square * SINE_TERMS[-1] + SINE_TERMS[-2]
    for term in SINE_TERMS[-3::-1]:
        result = result * square + term
    return result * quarter


def dot(a, b):
    return jnp.dot(a, b, preferred_element_type=F32)


def dot_nt(a, b):
    return lax.dot_general(a, b, (((1,), (1,)), ((), ())), preferred_element_type=F32)


def call(kernel, out_shapes, place, args, name, vmem_mib, scratch=(), in_place=None, out_place=pltpu.VMEM, aliases={}):
    spaces = in_place or (pltpu.VMEM,) * len(args)
    vmem = pl.BlockSpec(memory_space=out_place)
    single = isinstance(out_shapes, jax.ShapeDtypeStruct)
    return pl.pallas_call(
        kernel,
        out_shape=out_shapes,
        in_specs=[pl.BlockSpec(memory_space=m) for m in (pltpu.SMEM, *spaces)],
        out_specs=vmem if single else (vmem,) * len(out_shapes),
        scratch_shapes=scratch,
        input_output_aliases=aliases,
        compiler_params=pltpu.CompilerParams(vmem_limit_bytes=vmem_mib << 20),
        name=name,
    )(place, *args)


def like(shape, dtype=BF16):
    return jax.ShapeDtypeStruct(tuple(shape), dtype)


def lanes(index, size):
    return pl.ds(pl.multiple_of(index * size, size), size)


def prepare_kernel(place, inputs, labels, predictions, rows, own, given, wide, tags, sems):
    width = predictions.shape[0]
    part = own.shape[1] // 2
    copies = []
    for j in (0, 1):
        block = 2 * place[1] + (place[2] ^ j)
        at, there = lanes(block, part), slice(j * part, (j + 1) * part)
        copies += [
            pltpu.make_async_copy(predictions.at[:, at], wide.at[:, there], sems.at[3 * j]),
            pltpu.make_async_copy(labels.at[:, at], tags.at[:, there], sems.at[3 * j + 1]),
            pltpu.make_async_copy(inputs.at[at], rows.at[there], sems.at[3 * j + 2]),
        ]
    for copy in copies:
        copy.start()
    tail = own.shape[0] - width
    own[width:], given[width:] = (jnp.zeros((tail, 2 * part), BF16),) * 2
    for j in (0, 1):
        copies[3 * j].wait()
        copies[3 * j + 1].wait()
        there = slice(j * part, (j + 1) * part)
        classes = lax.broadcasted_iota(jnp.int32, (width, part), 0) + place[2] * width
        residual = ((classes == tags[:, there]).astype(F32) - wide[:, there]).astype(BF16)
        own[:width, there] = residual
        given[:width, (1 - j) * part:(2 - j) * part] = residual
    for j in (0, 1):
        copies[3 * j + 2].wait()


def high_low(x):
    high = x.astype(BF16)
    return high, (x - high.astype(F32)).astype(BF16)


def split_kernel(place, x, high, low):
    high[...], low[...] = high_low(x[...])


TILE = 512


def block_kernel(place, rows, w_own, w_other, p_own, p_other, high, low, out, own_slice, feats):
    inputs = rows[:feats.shape[0]]
    half, depth = w_own.shape[1], high.shape[0]
    total = None
    for i, (weights, phases) in enumerate(((w_own, p_own), (w_other, p_other))):
        for k in range(0, half, TILE):
            at = pl.ds(pl.multiple_of((place[2] ^ i) * half + k, TILE), TILE)
            tile = cosine(dot(inputs, weights[:, k:k + TILE]), phases[:, k:k + TILE]).astype(BF16)
            feats[:, at] = tile
            product = dot_nt(tile, high[:, at]) + dot_nt(tile, low[:, at])
            total = product if total is None else total + product
    out[:, :depth], out[:, depth:] = high_low(total)
    own_slice[...] = feats[:, lanes(place[0], depth)]


def product_of(refs, classes):
    total, short = None, None
    for residual, q in zip(refs[::2], refs[1::2]):
        left, right = residual[:classes], q[...]
        if right.shape[0] < 256:
            if short is None:
                short = left[:, :right.shape[0]], right
                continue
            at = slice(0, right.shape[0]) if left.shape[1] == right.shape[0] else slice(right.shape[0], None)
            left = jnp.concatenate([short[0], left[:, at]], axis=1)
            right = jnp.concatenate([short[1], right], axis=0)
            short = None
        product = dot(left, right)
        depth = product.shape[1] // 2
        product = product[:, :depth] + product[:, depth:]
        total = product if total is None else total + product
    return total


def begin_kernel(earlier, place, *refs):
    *pieces, out = refs
    total = product_of(pieces[earlier:], out.shape[0])
    out[...] = pieces[0][...] + total if earlier else total


def update_kernel(place, begun, *refs):
    *pieces, update, sent = refs
    total = DAMPING * (begun[...] + product_of(pieces, begun.shape[0]))
    update[...] = total
    sent[...] = total.astype(BF16)


def change_kernel(counts, place, sent, *refs):
    at = 0
    for count, out in zip(counts, refs[sum(counts):]):
        rows = refs[at][...] if count == 1 else jnp.concatenate([f[...] for f in refs[at:at + count]], axis=0)
        out[...] = dot_nt(sent[...], rows).astype(out.dtype)
        at += count


def hop_kernel(place, change, came, out):
    out[...] = (change[...] + came[...].astype(F32)).astype(BF16)


def last_kernel(place, change, came, given, out):
    part = out.shape[1] // 2
    for i in (0, 1):
        at, there = slice(i * part, (i + 1) * part), slice((1 - i) * part, (2 - i) * part)
        total = change[:, at] + came[:, at].astype(F32) + given[:, there].astype(F32)
        out[:, at] = total.astype(BF16)


def apply_kernel(which, place, predictions, change, *refs):
    new, total, sems = refs[-3:]
    width, part = total.shape[0], total.shape[1] // 2
    copies = []
    for j in (0, 1):
        at, there = lanes(2 * (place[1] ^ which) + (place[2] ^ j), part), slice(j * part, (j + 1) * part)
        total[:, there] = predictions[:, at] + change[:width, there].astype(F32)
        copies.append(pltpu.make_async_copy(total.at[:, there], new.at[:, at], sems.at[j]))
        copies[j].start()
    for copy in copies:
        copy.wait()


def swap(x, axes, pairs):
    return lax.ppermute(x, axes, [p for a, b in pairs for p in ((a, b), (b, a))])


def after(arrays, *others):
    return lax.optimization_barrier((*arrays, *others))[:len(arrays)]


def ring_shards(n_rows, inputs, projection, phases, inverse_blocks, labels, predictions, coefficients):
    ring = [2 * z for z in range(n_rows)] + [2 * z + 1 for z in reversed(range(n_rows))]
    size = len(ring)
    even = [(ring[i], ring[i + 1]) for i in range(0, size, 2)]
    odd = [(ring[i], ring[(i + 1) % size]) for i in range(1, size, 2)]
    ways = [[(2 * a + c, 2 * b + c) for c, pairs in enumerate(way) for a, b in pairs]
            for way in ((even, odd), (odd, even))]
    S = lambda x: swap(x, ("rows", "blocks", "cols"), ways[0])
    T = lambda x: swap(x, ("rows", "blocks", "cols"), ways[1])
    C = lambda x: swap(x, "cols", [(0, 1)])

    place = jnp.stack([lax.axis_index(a) for a in ("rows", "blocks", "cols")]).astype(jnp.int32)
    local_rows, width = predictions.shape
    part = local_rows // 4
    padded = -(-width // LANES) * LANES
    predictions, coefficients = predictions.T, coefficients.T
    depth = coefficients.shape[1]

    dma = pltpu.SemaphoreType.DMA
    block_rows = like((2 * part, inputs.shape[1]))
    x0, own, given = call(
        prepare_kernel, (block_rows, *(like((padded, 2 * part)),) * 2), place,
        tuple(pltpu.with_memory_space_constraint(a, pltpu.HBM) for a in (inputs, labels[None, :], predictions)),
        "prepare", 6,
        (pltpu.VMEM((width, 2 * part), F32), pltpu.VMEM((1, 2 * part), jnp.int32), dma((6,))), (pltpu.HBM,) * 3,
    )
    given = C(given)
    (x0,) = after((x0,), given)
    r0 = jnp.concatenate([own, given], axis=0)
    weights = (projection, C(projection))
    phases = phases[None, :]
    phases = (phases, C(phases))
    inverse = call(
        split_kernel, (like(inverse_blocks.shape[1:]),) * 2, place, (inverse_blocks[0],), "split", 14
    )

    def block(rows, size):
        scratch = (pltpu.VMEM((size, 2 * projection.shape[1]), BF16),)
        return call(
            block_kernel, (like((size, 2 * depth)), like((size, depth))), place,
            (rows, *weights, *phases, *inverse), "block", 16, scratch,
        )

    def begin(pairs, *earlier):
        return call(
            functools.partial(begin_kernel, len(earlier)), like((padded, depth), F32), place,
            (*earlier, *[a for pair in pairs for a in pair]), "begin", 14,
        )

    x1, r1 = S(x0), S(r0)
    q0, f0 = block(x0, part)
    (x1,) = after((x1,), q0)
    x2 = T(x1)
    q1, f1 = block(x1, 2 * part)
    (r1,) = after((r1,), q1)
    r2 = T(r1)
    theirs = lambda r: C(r[padded:])
    q0_other, f0_other = C(q0), C(f0)
    (x2,) = after((x2,), q1, q0_other, f0_other)
    x3 = S(x2)
    q2, f2 = block(x2, 2 * part)
    begun = begin([(r0, q0), (r0, q0_other), (r1, q1), (theirs(r1), C(q1))])
    (r2,) = after((r2,), q2, begun)
    r3 = S(r2)
    (x3,) = after((x3,), begun)
    x4 = T(x3[:part])
    q3, f3 = block(x3, 2 * part)
    (r3,) = after((r3,), q3)
    r4 = T(r3[:, :part])
    (x4,) = after((x4,), q3)
    q4, f4 = block(x4, part)
    f4_other = C(f4)
    begun = begin([(r2, q2), (theirs(r2), C(q2)), (r3, q3), (theirs(r3), C(q3))], begun)
    (begun,) = after((begun,), f4_other)
    update, sent = call(
        update_kernel, (like((padded, depth), F32), like((padded, depth))), place,
        (begun, r4, q4, theirs(r4), C(q4)), "update", 14,
    )

    whole, wide = like((padded, 2 * part)), like((padded, 2 * part), F32)

    def changes(update, blocks, outs):
        counts = tuple(len(f) for f in blocks)
        return call(
            functools.partial(change_kernel, counts), outs, place, (update, *[f for b in blocks for f in b]), "change", 8
        )

    hop = lambda ahead, came: call(hop_kernel, whole, place, (ahead, came), "hop", 4)
    (first,) = changes(sent, [(f4, f4_other)], (whole,))
    (sent_other,) = after((C(sent),), first)
    ahead = changes(after((sent,), first)[0], [(f3,), (f2,), (f1,), (f0, f0_other)], (wide,) * 4)
    first = T(first)
    (sent_other,) = after((sent_other,), *ahead)
    second, *behind = changes(sent_other, [(f3,), (f2,), (f1,)], (whole, wide, wide))
    (first,) = after((first,), second)
    second = S(second)
    for i, (way, back) in enumerate(((S, T), (T, S), (S, None))):
        total = hop(ahead[i], first)
        first = way(total)
        (second,) = after((second,), total)
        if back:
            total = hop(behind[i], second)
            second = back(total)
            (first,) = after((first,), total)
    given = C(second)
    (first,) = after((first,), given)
    ahead = ahead[3]
    own = call(last_kernel, whole, place, (ahead, first, given), "last", 4)
    new = None
    for i in (0, 1):
        change = swap(own, "blocks", [(0, 1)]) if i else own
        earlier = (new,) if i else ()
        new = call(
            functools.partial(apply_kernel, i), like(predictions.shape, F32), place,
            (predictions, change, *earlier), "apply", 6, (pltpu.VMEM((width, 2 * part), F32), dma((2,))),
            (pltpu.VMEM, pltpu.VMEM, *(pl.ANY,) * i), pl.ANY, {3: 0} if i else {},
        )
    return (coefficients + update[:width]).T, new.T


def plain_shards(inputs, projection, phases, inverse_blocks, labels, predictions, coefficients):
    out_width = predictions.shape[1]
    classes = lax.axis_index("cols") * out_width + jnp.arange(out_width, dtype=jnp.int32)
    onehot = (labels[:, None] == classes[None, :]).astype(F32)
    residual = (onehot - predictions).astype(BF16)
    angles = dot(inputs, projection) + phases.astype(F32)[None, :]
    half_features = jnp.cos(angles).astype(BF16)
    features_full = lax.all_gather(half_features, "cols", axis=1, tiled=True)
    own_gradient = lax.psum_scatter(
        lax.dot_general(features_full, residual, (((0,), (0,)), ((), ())), preferred_element_type=F32),
        "rows", scatter_dimension=0, tiled=True,
    )
    gradient_full = lax.all_gather(own_gradient, "rows", axis=0, tiled=True)
    update = DAMPING * jnp.dot(inverse_blocks[0], gradient_full, precision=lax.Precision.HIGHEST)
    sent = lax.all_gather(update.astype(BF16), "rows", axis=0, tiled=True)
    summed = lax.psum(dot(features_full, sent), "blocks")
    return coefficients + update, predictions + summed


def solution(mesh):
    n_rows, n_blocks = mesh.shape["rows"], mesh.shape["blocks"]
    small_ring = n_blocks == 2 and n_rows == 4 and mesh.shape["cols"] == 2
    shards = functools.partial(ring_shards, n_rows) if small_ring else plain_shards
    return jax.shard_map(
        shards,
        mesh=mesh,
        in_specs=(
            P(("groups", "rows"), None),
            P(None, ("groups", "blocks", "cols")),
            P(("groups", "blocks", "cols")),
            P(("groups", "blocks"), "rows", None),
            P(("groups", "rows")),
            P(("groups", "rows"), "cols"),
            P(("groups", "blocks", "rows"), "cols"),
        ),
        out_specs=(P(("groups", "blocks", "rows"), "cols"), P(("groups", "rows"), "cols")),
        check_vma=False,
    )
```

```python
import functools

import jax
import jax.numpy as jnp
from jax import lax
from jax.experimental import pallas as pl
from jax.experimental.pallas import tpu as pltpu
from jax.sharding import PartitionSpec as P

DAMPING = 0.5
F32, BF16 = jnp.float32, jnp.bfloat16
LANES = 128

SINE_TERMS = (
    6.283185280127733, -41.341680582549685, 81.60247253767959, -76.5810396203459, 39.75848375303386
)
TURNS = 0.15915494309189535


def cosine(angles, phases):
    turns = angles * TURNS + phases.astype(F32) * TURNS
    quarter = 0.25 - jnp.abs(turns - jnp.round(turns))
    square = quarter * quarter
    result = square * SINE_TERMS[-1] + SINE_TERMS[-2]
    for term in SINE_TERMS[-3::-1]:
        result = result * square + term
    return result * quarter


def dot(a, b):
    return jnp.dot(a, b, preferred_element_type=F32)


def dot_nt(a, b):
    return lax.dot_general(a, b, (((1,), (1,)), ((), ())), preferred_element_type=F32)


def call(kernel, out_shapes, place, args, name, vmem_mib, scratch=(), in_place=None, out_place=pltpu.VMEM, aliases={}):
    spaces = in_place or (pltpu.VMEM,) * len(args)
    vmem = pl.BlockSpec(memory_space=out_place)
    single = isinstance(out_shapes, jax.ShapeDtypeStruct)
    return pl.pallas_call(
        kernel,
        out_shape=out_shapes,
        in_specs=[pl.BlockSpec(memory_space=m) for m in (pltpu.SMEM, *spaces)],
        out_specs=vmem if single else (vmem,) * len(out_shapes),
        scratch_shapes=scratch,
        input_output_aliases=aliases,
        compiler_params=pltpu.CompilerParams(vmem_limit_bytes=vmem_mib << 20),
        name=name,
    )(place, *args)


def like(shape, dtype=BF16):
    return jax.ShapeDtypeStruct(tuple(shape), dtype)


def lanes(index, size):
    return pl.ds(pl.multiple_of(index * size, size), size)


def prepare_kernel(place, inputs, labels, predictions, rows, own, given, wide, tags, sems):
    width = predictions.shape[0]
    part = own.shape[1] // 2
    copies = []
    for j in (0, 1):
        block = 2 * place[1] + (place[2] ^ j)
        at, there = lanes(block, part), slice(j * part, (j + 1) * part)
        copies += [
            pltpu.make_async_copy(predictions.at[:, at], wide.at[:, there], sems.at[3 * j]),
            pltpu.make_async_copy(labels.at[:, at], tags.at[:, there], sems.at[3 * j + 1]),
            pltpu.make_async_copy(inputs.at[at], rows.at[there], sems.at[3 * j + 2]),
        ]
    for copy in copies:
        copy.start()
    tail = own.shape[0] - width
    own[width:], given[width:] = (jnp.zeros((tail, 2 * part), BF16),) * 2
    for j in (0, 1):
        copies[3 * j].wait()
        copies[3 * j + 1].wait()
        there = slice(j * part, (j + 1) * part)
        classes = lax.broadcasted_iota(jnp.int32, (width, part), 0) + place[2] * width
        residual = ((classes == tags[:, there]).astype(F32) - wide[:, there]).astype(BF16)
        own[:width, there] = residual
        given[:width, (1 - j) * part:(2 - j) * part] = residual
    for j in (0, 1):
        copies[3 * j + 2].wait()


def high_low(x):
    high = x.astype(BF16)
    return high, (x - high.astype(F32)).astype(BF16)


def round_kernel(place, x, out):
    out[...] = x[...].astype(BF16)


TILE = 512


def block_kernel(place, rows, w_own, w_other, p_own, p_other, inverse, out, own_slice, feats):
    inputs = rows[:feats.shape[0]]
    half, depth = w_own.shape[1], inverse.shape[0]
    total = None
    for i, (weights, phases) in enumerate(((w_own, p_own), (w_other, p_other))):
        for k in range(0, half, TILE):
            at = pl.ds(pl.multiple_of((place[2] ^ i) * half + k, TILE), TILE)
            tile = cosine(dot(inputs, weights[:, k:k + TILE]), phases[:, k:k + TILE]).astype(BF16)
            feats[:, at] = tile
            product = dot_nt(tile, inverse[:, at])
            total = product if total is None else total + product
    out[:, :depth], out[:, depth:] = high_low(total)
    own_slice[...] = feats[:, lanes(place[0], depth)]


def product_of(refs, classes):
    total, short = None, None
    for residual, q in zip(refs[::2], refs[1::2]):
        left, right = residual[:classes], q[...]
        if right.shape[0] < 256:
            if short is None:
                short = left[:, :right.shape[0]], right
                continue
            at = slice(0, right.shape[0]) if left.shape[1] == right.shape[0] else slice(right.shape[0], None)
            left = jnp.concatenate([short[0], left[:, at]], axis=1)
            right = jnp.concatenate([short[1], right], axis=0)
            short = None
        product = dot(left, right)
        depth = product.shape[1] // 2
        product = product[:, :depth] + product[:, depth:]
        total = product if total is None else total + product
    return total


def begin_kernel(earlier, place, *refs):
    *pieces, out = refs
    total = product_of(pieces[earlier:], out.shape[0])
    out[...] = pieces[0][...] + total if earlier else total


def update_kernel(place, begun, *refs):
    *pieces, update, sent = refs
    total = DAMPING * (begun[...] + product_of(pieces, begun.shape[0]))
    update[...] = total
    sent[...] = total.astype(BF16)


def change_kernel(counts, place, sent, *refs):
    at = 0
    for count, out in zip(counts, refs[sum(counts):]):
        rows = refs[at][...] if count == 1 else jnp.concatenate([f[...] for f in refs[at:at + count]], axis=0)
        out[...] = dot_nt(sent[...], rows).astype(out.dtype)
        at += count


def hop_kernel(place, change, came, out):
    out[...] = (change[...] + came[...].astype(F32)).astype(BF16)


def last_kernel(place, change, came, given, out):
    part = out.shape[1] // 2
    for i in (0, 1):
        at, there = slice(i * part, (i + 1) * part), slice((1 - i) * part, (2 - i) * part)
        total = change[:, at] + came[:, at].astype(F32) + given[:, there].astype(F32)
        out[:, at] = total.astype(BF16)


def apply_kernel(which, place, predictions, change, *refs):
    new, total, sems = refs[-3:]
    width, part = total.shape[0], total.shape[1] // 2
    copies = []
    for j in (0, 1):
        at, there = lanes(2 * (place[1] ^ which) + (place[2] ^ j), part), slice(j * part, (j + 1) * part)
        total[:, there] = predictions[:, at] + change[:width, there].astype(F32)
        copies.append(pltpu.make_async_copy(total.at[:, there], new.at[:, at], sems.at[j]))
        copies[j].start()
    for copy in copies:
        copy.wait()


def swap(x, axes, pairs):
    return lax.ppermute(x, axes, [p for a, b in pairs for p in ((a, b), (b, a))])


def after(arrays, *others):
    return lax.optimization_barrier((*arrays, *others))[:len(arrays)]


def ring_shards(n_rows, inputs, projection, phases, inverse_blocks, labels, predictions, coefficients):
    ring = [2 * z for z in range(n_rows)] + [2 * z + 1 for z in reversed(range(n_rows))]
    size = len(ring)
    even = [(ring[i], ring[i + 1]) for i in range(0, size, 2)]
    odd = [(ring[i], ring[(i + 1) % size]) for i in range(1, size, 2)]
    ways = [[(2 * a + c, 2 * b + c) for c, pairs in enumerate(way) for a, b in pairs]
            for way in ((even, odd), (odd, even))]
    S = lambda x: swap(x, ("rows", "blocks", "cols"), ways[0])
    T = lambda x: swap(x, ("rows", "blocks", "cols"), ways[1])
    C = lambda x: swap(x, "cols", [(0, 1)])

    place = jnp.stack([lax.axis_index(a) for a in ("rows", "blocks", "cols")]).astype(jnp.int32)
    local_rows, width = predictions.shape
    part = local_rows // 4
    padded = -(-width // LANES) * LANES
    predictions, coefficients = predictions.T, coefficients.T
    depth = coefficients.shape[1]

    dma = pltpu.SemaphoreType.DMA
    block_rows = like((2 * part, inputs.shape[1]))
    x0, own, given = call(
        prepare_kernel, (block_rows, *(like((padded, 2 * part)),) * 2), place,
        tuple(pltpu.with_memory_space_constraint(a, pltpu.HBM) for a in (inputs, labels[None, :], predictions)),
        "prepare", 6,
        (pltpu.VMEM((width, 2 * part), F32), pltpu.VMEM((1, 2 * part), jnp.int32), dma((6,))), (pltpu.HBM,) * 3,
    )
    given = C(given)
    (x0,) = after((x0,), given)
    r0 = jnp.concatenate([own, given], axis=0)
    weights = (projection, C(projection))
    phases = phases[None, :]
    phases = (phases, C(phases))
    inverse = call(round_kernel, like(inverse_blocks.shape[1:]), place, (inverse_blocks[0],), "round", 10)

    def block(rows, size):
        scratch = (pltpu.VMEM((size, 2 * projection.shape[1]), BF16),)
        return call(
            block_kernel, (like((size, 2 * depth)), like((size, depth))), place,
            (rows, *weights, *phases, inverse), "block", 16, scratch,
        )

    def begin(pairs, *earlier):
        return call(
            functools.partial(begin_kernel, len(earlier)), like((padded, depth), F32), place,
            (*earlier, *[a for pair in pairs for a in pair]), "begin", 14,
        )

    x1, r1 = S(x0), S(r0)
    q0, f0 = block(x0, part)
    (x1,) = after((x1,), q0)
    x2 = T(x1)
    q1, f1 = block(x1, 2 * part)
    (r1,) = after((r1,), q1)
    r2 = T(r1)
    theirs = lambda r: C(r[padded:])
    q0_other, f0_other = C(q0), C(f0)
    (x2,) = after((x2,), q1, q0_other, f0_other)
    x3 = S(x2)
    q2, f2 = block(x2, 2 * part)
    begun = begin([(r0, q0), (r0, q0_other), (r1, q1), (theirs(r1), C(q1))])
    (r2,) = after((r2,), q2, begun)
    r3 = S(r2)
    (x3,) = after((x3,), begun)
    x4 = T(x3[:part])
    q3, f3 = block(x3, 2 * part)
    (r3,) = after((r3,), q3)
    r4 = T(r3[:, :part])
    (x4,) = after((x4,), q3)
    q4, f4 = block(x4, part)
    f4_other = C(f4)
    begun = begin([(r2, q2), (theirs(r2), C(q2)), (r3, q3), (theirs(r3), C(q3))], begun)
    (begun,) = after((begun,), f4_other)
    update, sent = call(
        update_kernel, (like((padded, depth), F32), like((padded, depth))), place,
        (begun, r4, q4, theirs(r4), C(q4)), "update", 14,
    )

    whole, wide = like((padded, 2 * part)), like((padded, 2 * part), F32)

    def changes(update, blocks, outs):
        counts = tuple(len(f) for f in blocks)
        return call(
            functools.partial(change_kernel, counts), outs, place, (update, *[f for b in blocks for f in b]), "change", 8
        )

    hop = lambda ahead, came: call(hop_kernel, whole, place, (ahead, came), "hop", 4)
    (first,) = changes(sent, [(f4, f4_other)], (whole,))
    (sent_other,) = after((C(sent),), first)
    ahead = changes(after((sent,), first)[0], [(f3,), (f2,), (f1,), (f0, f0_other)], (wide,) * 4)
    first = T(first)
    (sent_other,) = after((sent_other,), *ahead)
    second, *behind = changes(sent_other, [(f3,), (f2,), (f1,)], (whole, wide, wide))
    (first,) = after((first,), second)
    second = S(second)
    for i, (way, back) in enumerate(((S, T), (T, S), (S, None))):
        total = hop(ahead[i], first)
        first = way(total)
        (second,) = after((second,), total)
        if back:
            total = hop(behind[i], second)
            second = back(total)
            (first,) = after((first,), total)
    given = C(second)
    (first,) = after((first,), given)
    ahead = ahead[3]
    own = call(last_kernel, whole, place, (ahead, first, given), "last", 4)
    new = None
    for i in (0, 1):
        change = swap(own, "blocks", [(0, 1)]) if i else own
        earlier = (new,) if i else ()
        new = call(
            functools.partial(apply_kernel, i), like(predictions.shape, F32), place,
            (predictions, change, *earlier), "apply", 6, (pltpu.VMEM((width, 2 * part), F32), dma((2,))),
            (pltpu.VMEM, pltpu.VMEM, *(pl.ANY,) * i), pl.ANY, {3: 0} if i else {},
        )
    return (coefficients + update[:width]).T, new.T


def plain_shards(inputs, projection, phases, inverse_blocks, labels, predictions, coefficients):
    out_width = predictions.shape[1]
    classes = lax.axis_index("cols") * out_width + jnp.arange(out_width, dtype=jnp.int32)
    onehot = (labels[:, None] == classes[None, :]).astype(F32)
    residual = (onehot - predictions).astype(BF16)
    angles = dot(inputs, projection) + phases.astype(F32)[None, :]
    half_features = jnp.cos(angles).astype(BF16)
    features_full = lax.all_gather(half_features, "cols", axis=1, tiled=True)
    own_gradient = lax.psum_scatter(
        lax.dot_general(features_full, residual, (((0,), (0,)), ((), ())), preferred_element_type=F32),
        "rows", scatter_dimension=0, tiled=True,
    )
    gradient_full = lax.all_gather(own_gradient, "rows", axis=0, tiled=True)
    update = DAMPING * jnp.dot(inverse_blocks[0], gradient_full, precision=lax.Precision.HIGHEST)
    sent = lax.all_gather(update.astype(BF16), "rows", axis=0, tiled=True)
    summed = lax.psum(dot(features_full, sent), "blocks")
    return coefficients + update, predictions + summed


def solution(mesh):
    n_rows, n_blocks = mesh.shape["rows"], mesh.shape["blocks"]
    small_ring = n_blocks == 2 and n_rows == 4 and mesh.shape["cols"] == 2
    shards = functools.partial(ring_shards, n_rows) if small_ring else plain_shards
    return jax.shard_map(
        shards,
        mesh=mesh,
        in_specs=(
            P(("groups", "rows"), None),
            P(None, ("groups", "blocks", "cols")),
            P(("groups", "blocks", "cols")),
            P(("groups", "blocks"), "rows", None),
            P(("groups", "rows")),
            P(("groups", "rows"), "cols"),
            P(("groups", "blocks", "rows"), "cols"),
        ),
        out_specs=(P(("groups", "blocks", "rows"), "cols"), P(("groups", "rows"), "cols")),
        check_vma=False,
    )
```

```python
import functools

import jax
import jax.numpy as jnp
from jax import lax
from jax.experimental import pallas as pl
from jax.experimental.pallas import tpu as pltpu
from jax.sharding import PartitionSpec as P

DAMPING = 0.5
F32, BF16 = jnp.float32, jnp.bfloat16
LANES = 128

SINE_TERMS = (
    6.283185280127733, -41.341680582549685, 81.60247253767959, -76.5810396203459, 39.75848375303386
)
TURNS = 0.15915494309189535


def cosine(angles, phases):
    turns = angles * TURNS + phases.astype(F32) * TURNS
    quarter = 0.25 - jnp.abs(turns - jnp.round(turns))
    square = quarter * quarter
    result = square * SINE_TERMS[-1] + SINE_TERMS[-2]
    for term in SINE_TERMS[-3::-1]:
        result = result * square + term
    return result * quarter


def dot(a, b):
    return jnp.dot(a, b, preferred_element_type=F32)


def dot_nt(a, b):
    return lax.dot_general(a, b, (((1,), (1,)), ((), ())), preferred_element_type=F32)


def call(kernel, out_shapes, place, args, name, vmem_mib, scratch=(), in_place=None, out_place=pltpu.VMEM, aliases={}):
    spaces = in_place or (pltpu.VMEM,) * len(args)
    vmem = pl.BlockSpec(memory_space=out_place)
    single = isinstance(out_shapes, jax.ShapeDtypeStruct)
    return pl.pallas_call(
        kernel,
        out_shape=out_shapes,
        in_specs=[pl.BlockSpec(memory_space=m) for m in (pltpu.SMEM, *spaces)],
        out_specs=vmem if single else (vmem,) * len(out_shapes),
        scratch_shapes=scratch,
        input_output_aliases=aliases,
        compiler_params=pltpu.CompilerParams(vmem_limit_bytes=vmem_mib << 20),
        name=name,
    )(place, *args)


def like(shape, dtype=BF16):
    return jax.ShapeDtypeStruct(tuple(shape), dtype)


def lanes(index, size):
    return pl.ds(pl.multiple_of(index * size, size), size)


def prepare_kernel(place, inputs, labels, predictions, rows, own, given, wide, tags, sems):
    width = predictions.shape[0]
    part = own.shape[1] // 2
    copies = []
    for j in (0, 1):
        block = 2 * place[1] + (place[2] ^ j)
        at, there = lanes(block, part), slice(j * part, (j + 1) * part)
        copies += [
            pltpu.make_async_copy(predictions.at[:, at], wide.at[:, there], sems.at[3 * j]),
            pltpu.make_async_copy(labels.at[:, at], tags.at[:, there], sems.at[3 * j + 1]),
            pltpu.make_async_copy(inputs.at[at], rows.at[there], sems.at[3 * j + 2]),
        ]
    for copy in copies:
        copy.start()
    tail = own.shape[0] - width
    own[width:], given[width:] = (jnp.zeros((tail, 2 * part), BF16),) * 2
    for j in (0, 1):
        copies[3 * j].wait()
        copies[3 * j + 1].wait()
        there = slice(j * part, (j + 1) * part)
        classes = lax.broadcasted_iota(jnp.int32, (width, part), 0) + place[2] * width
        residual = ((classes == tags[:, there]).astype(F32) - wide[:, there]).astype(BF16)
        own[:width, there] = residual
        given[:width, (1 - j) * part:(2 - j) * part] = residual
    for j in (0, 1):
        copies[3 * j + 2].wait()


def high_low(x):
    high = x.astype(BF16)
    return high, (x - high.astype(F32)).astype(BF16)


def round_kernel(place, x, out):
    out[...] = x[...].astype(BF16)


TILE = 512


def block_kernel(place, rows, w_own, w_other, p_own, p_other, inverse, out, own_slice, feats):
    inputs = rows[:feats.shape[0]]
    half, depth = w_own.shape[1], inverse.shape[0]
    total = None
    for i, (weights, phases) in enumerate(((w_own, p_own), (w_other, p_other))):
        for k in range(0, half, TILE):
            at = pl.ds(pl.multiple_of((place[2] ^ i) * half + k, TILE), TILE)
            tile = cosine(dot(inputs, weights[:, k:k + TILE]), phases[:, k:k + TILE]).astype(BF16)
            feats[:, at] = tile
            product = dot_nt(tile, inverse[:, at])
            total = product if total is None else total + product
    out[:, :depth], out[:, depth:] = high_low(total)
    own_slice[...] = feats[:, lanes(place[0], depth)]


def product_of(refs, classes):
    total, short = None, None
    for residual, q in zip(refs[::2], refs[1::2]):
        left, right = residual[:classes], q[...]
        if right.shape[0] < 256:
            if short is None:
                short = left[:, :right.shape[0]], right
                continue
            at = slice(0, right.shape[0]) if left.shape[1] == right.shape[0] else slice(right.shape[0], None)
            left = jnp.concatenate([short[0], left[:, at]], axis=1)
            right = jnp.concatenate([short[1], right], axis=0)
            short = None
        product = dot(left, right)
        depth = product.shape[1] // 2
        product = product[:, :depth] + product[:, depth:]
        total = product if total is None else total + product
    return total


def begin_kernel(earlier, place, *refs):
    *pieces, out = refs
    total = product_of(pieces[earlier:], out.shape[0])
    out[...] = pieces[0][...] + total if earlier else total


def update_kernel(place, begun, *refs):
    *pieces, update, sent = refs
    total = DAMPING * (begun[...] + product_of(pieces, begun.shape[0]))
    update[...] = total
    sent[...] = total.astype(BF16)


def change_kernel(counts, place, sent, *refs):
    at = 0
    for count, out in zip(counts, refs[sum(counts):]):
        rows = refs[at][...] if count == 1 else jnp.concatenate([f[...] for f in refs[at:at + count]], axis=0)
        out[...] = dot_nt(sent[...], rows).astype(out.dtype)
        at += count


def hop_kernel(place, change, came, out):
    out[...] = (change[...] + came[...].astype(F32)).astype(BF16)


def last_kernel(place, change, came, given, out):
    part = out.shape[1] // 2
    for i in (0, 1):
        at, there = slice(i * part, (i + 1) * part), slice((1 - i) * part, (2 - i) * part)
        total = change[:, at] + came[:, at].astype(F32) + given[:, there].astype(F32)
        out[:, at] = total.astype(BF16)


def apply_kernel(which, place, predictions, change, *refs):
    new, total, sems = refs[-3:]
    width, part = total.shape[0], total.shape[1] // 2
    copies = []
    for j in (0, 1):
        at, there = lanes(2 * (place[1] ^ which) + (place[2] ^ j), part), slice(j * part, (j + 1) * part)
        total[:, there] = predictions[:, at] + change[:width, there].astype(F32)
        copies.append(pltpu.make_async_copy(total.at[:, there], new.at[:, at], sems.at[j]))
        copies[j].start()
    for copy in copies:
        copy.wait()


def swap(x, axes, pairs):
    return lax.ppermute(x, axes, [p for a, b in pairs for p in ((a, b), (b, a))])


def after(arrays, *others):
    return lax.optimization_barrier((*arrays, *others))[:len(arrays)]


def ring_shards(n_rows, inputs, projection, phases, inverse_blocks, labels, predictions, coefficients):
    ring = [2 * z for z in range(n_rows)] + [2 * z + 1 for z in reversed(range(n_rows))]
    size = len(ring)
    even = [(ring[i], ring[i + 1]) for i in range(0, size, 2)]
    odd = [(ring[i], ring[(i + 1) % size]) for i in range(1, size, 2)]
    ways = [[(2 * a + c, 2 * b + c) for c, pairs in enumerate(way) for a, b in pairs]
            for way in ((even, odd), (odd, even))]
    S = lambda x: swap(x, ("rows", "blocks", "cols"), ways[0])
    T = lambda x: swap(x, ("rows", "blocks", "cols"), ways[1])
    C = lambda x: swap(x, "cols", [(0, 1)])

    place = jnp.stack([lax.axis_index(a) for a in ("rows", "blocks", "cols")]).astype(jnp.int32)
    local_rows, width = predictions.shape
    part = local_rows // 4
    padded = -(-width // LANES) * LANES
    predictions, coefficients = predictions.T, coefficients.T
    depth = coefficients.shape[1]

    dma = pltpu.SemaphoreType.DMA
    block_rows = like((2 * part, inputs.shape[1]))
    x0, own, given = call(
        prepare_kernel, (block_rows, *(like((padded, 2 * part)),) * 2), place,
        tuple(pltpu.with_memory_space_constraint(a, pltpu.HBM) for a in (inputs, labels[None, :], predictions)),
        "prepare", 6,
        (pltpu.VMEM((width, 2 * part), F32), pltpu.VMEM((1, 2 * part), jnp.int32), dma((6,))), (pltpu.HBM,) * 3,
    )
    given = C(given)
    (x0,) = after((x0,), given)
    r0 = jnp.concatenate([own, given], axis=0)
    weights = (projection, C(projection))
    phases = phases[None, :]
    phases = (phases, C(phases))
    inverse = call(round_kernel, like(inverse_blocks.shape[1:]), place, (inverse_blocks[0],), "round", 10)

    def block(rows, size):
        scratch = (pltpu.VMEM((size, 2 * projection.shape[1]), BF16),)
        return call(
            block_kernel, (like((size, 2 * depth)), like((size, depth))), place,
            (rows, *weights, *phases, inverse), "block", 16, scratch,
        )

    def begin(pairs, *earlier):
        return call(
            functools.partial(begin_kernel, len(earlier)), like((padded, depth), F32), place,
            (*earlier, *[a for pair in pairs for a in pair]), "begin", 14,
        )

    x1, r1 = S(x0), S(r0)
    q0, f0 = block(x0, part)
    (x1,) = after((x1,), q0)
    theirs = lambda r: C(r[padded:])

    def onward(way, rows, residual, size, begun, earlier):
        q, f = block(rows, size)
        (rows,) = after((rows,), q)
        further = way(rows[:part] if way is last else rows)
        q_other = C(q)
        (residual,) = after((residual,), q_other)
        further_residual = way(residual[:, :part] if way is last else residual)
        begun = begin([*earlier, (residual, q), (theirs(residual), q_other)], *begun)
        return q, f, further, further_residual, begun

    last = lambda x: T(x)
    q0_other, f0_other = C(q0), C(f0)
    q1, f1, x2, r2, begun = onward(T, x1, r1, 2 * part, (), [(r0, q0), (r0, q0_other)])
    (x2,) = after((x2,), begun, f0_other)
    q2, f2, x3, r3, begun = onward(S, x2, r2, 2 * part, (begun,), [])
    (x3,) = after((x3,), begun)
    q3, f3, x4, r4, begun = onward(last, x3, r3, 2 * part, (begun,), [])
    q4, f4 = block(x4, part)
    f4_other = C(f4)
    (begun,) = after((begun,), f4_other)
    update, sent = call(
        update_kernel, (like((padded, depth), F32), like((padded, depth))), place,
        (begun, r4, q4, theirs(r4), C(q4)), "update", 14,
    )

    whole, wide = like((padded, 2 * part)), like((padded, 2 * part), F32)

    def changes(update, blocks, outs):
        counts = tuple(len(f) for f in blocks)
        return call(
            functools.partial(change_kernel, counts), outs, place, (update, *[f for b in blocks for f in b]), "change", 8
        )

    hop = lambda ahead, came: call(hop_kernel, whole, place, (ahead, came), "hop", 4)
    (first,) = changes(sent, [(f4, f4_other)], (whole,))
    (sent_other,) = after((C(sent),), first)
    ahead = changes(after((sent,), first)[0], [(f3,), (f2,), (f1,), (f0, f0_other)], (wide,) * 4)
    first = T(first)
    (sent_other,) = after((sent_other,), *ahead)
    second, *behind = changes(sent_other, [(f3,), (f2,), (f1,)], (whole, wide, wide))
    (first,) = after((first,), second)
    second = S(second)
    for i, (way, back) in enumerate(((S, T), (T, S), (S, None))):
        total = hop(ahead[i], first)
        first = way(total)
        (second,) = after((second,), total)
        if back:
            total = hop(behind[i], second)
            second = back(total)
            (first,) = after((first,), total)
    given = C(second)
    (first,) = after((first,), given)
    ahead = ahead[3]
    own = call(last_kernel, whole, place, (ahead, first, given), "last", 4)
    new = None
    for i in (0, 1):
        change = swap(own, "blocks", [(0, 1)]) if i else own
        earlier = (new,) if i else ()
        new = call(
            functools.partial(apply_kernel, i), like(predictions.shape, F32), place,
            (predictions, change, *earlier), "apply", 6, (pltpu.VMEM((width, 2 * part), F32), dma((2,))),
            (pltpu.VMEM, pltpu.VMEM, *(pl.ANY,) * i), pl.ANY, {3: 0} if i else {},
        )
    return (coefficients + update[:width]).T, new.T


def plain_shards(inputs, projection, phases, inverse_blocks, labels, predictions, coefficients):
    out_width = predictions.shape[1]
    classes = lax.axis_index("cols") * out_width + jnp.arange(out_width, dtype=jnp.int32)
    onehot = (labels[:, None] == classes[None, :]).astype(F32)
    residual = (onehot - predictions).astype(BF16)
    angles = dot(inputs, projection) + phases.astype(F32)[None, :]
    half_features = jnp.cos(angles).astype(BF16)
    features_full = lax.all_gather(half_features, "cols", axis=1, tiled=True)
    own_gradient = lax.psum_scatter(
        lax.dot_general(features_full, residual, (((0,), (0,)), ((), ())), preferred_element_type=F32),
        "rows", scatter_dimension=0, tiled=True,
    )
    gradient_full = lax.all_gather(own_gradient, "rows", axis=0, tiled=True)
    update = DAMPING * jnp.dot(inverse_blocks[0], gradient_full, precision=lax.Precision.HIGHEST)
    sent = lax.all_gather(update.astype(BF16), "rows", axis=0, tiled=True)
    summed = lax.psum(dot(features_full, sent), "blocks")
    return coefficients + update, predictions + summed


def solution(mesh):
    n_rows, n_blocks = mesh.shape["rows"], mesh.shape["blocks"]
    small_ring = n_blocks == 2 and n_rows == 4 and mesh.shape["cols"] == 2
    shards = functools.partial(ring_shards, n_rows) if small_ring else plain_shards
    return jax.shard_map(
        shards,
        mesh=mesh,
        in_specs=(
            P(("groups", "rows"), None),
            P(None, ("groups", "blocks", "cols")),
            P(("groups", "blocks", "cols")),
            P(("groups", "blocks"), "rows", None),
            P(("groups", "rows")),
            P(("groups", "rows"), "cols"),
            P(("groups", "blocks", "rows"), "cols"),
        ),
        out_specs=(P(("groups", "blocks", "rows"), "cols"), P(("groups", "rows"), "cols")),
        check_vma=False,
    )
```

```python
import functools

import jax
import jax.numpy as jnp
from jax import lax
from jax.experimental import pallas as pl
from jax.experimental.pallas import tpu as pltpu
from jax.sharding import PartitionSpec as P

DAMPING = 0.5
F32, BF16 = jnp.float32, jnp.bfloat16
LANES = 128

SINE_TERMS = (
    6.283185280127733, -41.341680582549685, 81.60247253767959, -76.5810396203459, 39.75848375303386
)
TURNS = 0.15915494309189535


def cosine(angles, phases):
    turns = angles * TURNS + phases.astype(F32) * TURNS
    quarter = 0.25 - jnp.abs(turns - jnp.round(turns))
    square = quarter * quarter
    result = square * SINE_TERMS[-1] + SINE_TERMS[-2]
    for term in SINE_TERMS[-3::-1]:
        result = result * square + term
    return result * quarter


def dot(a, b):
    return jnp.dot(a, b, preferred_element_type=F32)


def dot_nt(a, b):
    return lax.dot_general(a, b, (((1,), (1,)), ((), ())), preferred_element_type=F32)


def call(kernel, out_shapes, place, args, name, vmem_mib, scratch=(), in_place=None, out_place=pltpu.VMEM, aliases={}):
    spaces = in_place or (pltpu.VMEM,) * len(args)
    vmem = pl.BlockSpec(memory_space=out_place)
    single = isinstance(out_shapes, jax.ShapeDtypeStruct)
    return pl.pallas_call(
        kernel,
        out_shape=out_shapes,
        in_specs=[pl.BlockSpec(memory_space=m) for m in (pltpu.SMEM, *spaces)],
        out_specs=vmem if single else (vmem,) * len(out_shapes),
        scratch_shapes=scratch,
        input_output_aliases=aliases,
        compiler_params=pltpu.CompilerParams(vmem_limit_bytes=vmem_mib << 20),
        name=name,
    )(place, *args)


def like(shape, dtype=BF16):
    return jax.ShapeDtypeStruct(tuple(shape), dtype)


def lanes(index, size):
    return pl.ds(pl.multiple_of(index * size, size), size)


def prepare_kernel(place, inputs, labels, predictions, rows, own, given, wide, tags, sems):
    width = predictions.shape[0]
    part = own.shape[1] // 2
    copies = []
    for j in (0, 1):
        block = 2 * place[1] + (place[2] ^ j)
        at, there = lanes(block, part), slice(j * part, (j + 1) * part)
        copies += [
            pltpu.make_async_copy(predictions.at[:, at], wide.at[:, there], sems.at[3 * j]),
            pltpu.make_async_copy(labels.at[:, at], tags.at[:, there], sems.at[3 * j + 1]),
            pltpu.make_async_copy(inputs.at[at], rows.at[there], sems.at[3 * j + 2]),
        ]
    for copy in copies:
        copy.start()
    tail = own.shape[0] - width
    own[width:], given[width:] = (jnp.zeros((tail, 2 * part), BF16),) * 2
    for j in (0, 1):
        copies[3 * j].wait()
        copies[3 * j + 1].wait()
        there = slice(j * part, (j + 1) * part)
        classes = lax.broadcasted_iota(jnp.int32, (width, part), 0) + place[2] * width
        residual = ((classes == tags[:, there]).astype(F32) - wide[:, there]).astype(BF16)
        own[:width, there] = residual
        given[:width, (1 - j) * part:(2 - j) * part] = residual
    for j in (0, 1):
        copies[3 * j + 2].wait()


def high_low(x):
    high = x.astype(BF16)
    return high, (x - high.astype(F32)).astype(BF16)


def round_kernel(place, x, out):
    out[...] = x[...].astype(BF16)


TILE = 1024


def block_kernel(place, rows, w_own, w_other, p_own, p_other, inverse, out, own_slice, feats):
    inputs = rows[:feats.shape[0]]
    half, depth = w_own.shape[1], inverse.shape[0]
    total = None
    for i, (weights, phases) in enumerate(((w_own, p_own), (w_other, p_other))):
        for k in range(0, half, TILE):
            at = pl.ds(pl.multiple_of((place[2] ^ i) * half + k, TILE), TILE)
            tile = cosine(dot(inputs, weights[:, k:k + TILE]), phases[:, k:k + TILE]).astype(BF16)
            feats[:, at] = tile
            product = dot_nt(tile, inverse[:, at])
            total = product if total is None else total + product
    out[:, :depth], out[:, depth:] = high_low(total)
    own_slice[...] = feats[:, lanes(place[0], depth)]


def product_of(refs, classes):
    total, short = None, None
    for residual, q in zip(refs[::2], refs[1::2]):
        left, right = residual[:classes], q[...]
        if right.shape[0] < 256:
            if short is None:
                short = left[:, :right.shape[0]], right
                continue
            at = slice(0, right.shape[0]) if left.shape[1] == right.shape[0] else slice(right.shape[0], None)
            left = jnp.concatenate([short[0], left[:, at]], axis=1)
            right = jnp.concatenate([short[1], right], axis=0)
            short = None
        product = dot(left, right)
        depth = product.shape[1] // 2
        product = product[:, :depth] + product[:, depth:]
        total = product if total is None else total + product
    return total


def begin_kernel(earlier, place, *refs):
    *pieces, out = refs
    total = product_of(pieces[earlier:], out.shape[0])
    out[...] = pieces[0][...] + total if earlier else total


def update_kernel(place, begun, *refs):
    *pieces, update, sent = refs
    total = DAMPING * (begun[...] + product_of(pieces, begun.shape[0]))
    update[...] = total
    sent[...] = total.astype(BF16)


def change_kernel(counts, place, sent, *refs):
    at = 0
    for count, out in zip(counts, refs[sum(counts):]):
        rows = refs[at][...] if count == 1 else jnp.concatenate([f[...] for f in refs[at:at + count]], axis=0)
        out[...] = dot_nt(sent[...], rows).astype(out.dtype)
        at += count


def hop_kernel(place, change, came, out):
    out[...] = (change[...] + came[...].astype(F32)).astype(BF16)


def last_kernel(place, change, came, given, out):
    part = out.shape[1] // 2
    for i in (0, 1):
        at, there = slice(i * part, (i + 1) * part), slice((1 - i) * part, (2 - i) * part)
        total = change[:, at] + came[:, at].astype(F32) + given[:, there].astype(F32)
        out[:, at] = total.astype(BF16)


def apply_kernel(which, place, predictions, change, *refs):
    new, total, sems = refs[-3:]
    width, part = total.shape[0], total.shape[1] // 2
    copies = []
    for j in (0, 1):
        at, there = lanes(2 * (place[1] ^ which) + (place[2] ^ j), part), slice(j * part, (j + 1) * part)
        total[:, there] = predictions[:, at] + change[:width, there].astype(F32)
        copies.append(pltpu.make_async_copy(total.at[:, there], new.at[:, at], sems.at[j]))
        copies[j].start()
    for copy in copies:
        copy.wait()


def swap(x, axes, pairs):
    return lax.ppermute(x, axes, [p for a, b in pairs for p in ((a, b), (b, a))])


def after(arrays, *others):
    return lax.optimization_barrier((*arrays, *others))[:len(arrays)]


def ring_shards(n_rows, inputs, projection, phases, inverse_blocks, labels, predictions, coefficients):
    ring = [2 * z for z in range(n_rows)] + [2 * z + 1 for z in reversed(range(n_rows))]
    size = len(ring)
    even = [(ring[i], ring[i + 1]) for i in range(0, size, 2)]
    odd = [(ring[i], ring[(i + 1) % size]) for i in range(1, size, 2)]
    ways = [[(2 * a + c, 2 * b + c) for c, pairs in enumerate(way) for a, b in pairs]
            for way in ((even, odd), (odd, even))]
    S = lambda x: swap(x, ("rows", "blocks", "cols"), ways[0])
    T = lambda x: swap(x, ("rows", "blocks", "cols"), ways[1])
    C = lambda x: swap(x, "cols", [(0, 1)])

    place = jnp.stack([lax.axis_index(a) for a in ("rows", "blocks", "cols")]).astype(jnp.int32)
    local_rows, width = predictions.shape
    part = local_rows // 4
    padded = -(-width // LANES) * LANES
    predictions, coefficients = predictions.T, coefficients.T
    depth = coefficients.shape[1]

    dma = pltpu.SemaphoreType.DMA
    block_rows = like((2 * part, inputs.shape[1]))
    x0, own, given = call(
        prepare_kernel, (block_rows, *(like((padded, 2 * part)),) * 2), place,
        tuple(pltpu.with_memory_space_constraint(a, pltpu.HBM) for a in (inputs, labels[None, :], predictions)),
        "prepare", 6,
        (pltpu.VMEM((width, 2 * part), F32), pltpu.VMEM((1, 2 * part), jnp.int32), dma((6,))), (pltpu.HBM,) * 3,
    )
    given = C(given)
    (x0,) = after((x0,), given)
    r0 = jnp.concatenate([own, given], axis=0)
    weights = (projection, C(projection))
    phases = phases[None, :]
    phases = (phases, C(phases))
    inverse = call(round_kernel, like(inverse_blocks.shape[1:]), place, (inverse_blocks[0],), "round", 10)

    def block(rows, size):
        scratch = (pltpu.VMEM((size, 2 * projection.shape[1]), BF16),)
        return call(
            block_kernel, (like((size, 2 * depth)), like((size, depth))), place,
            (rows, *weights, *phases, inverse), "block", 16, scratch,
        )

    def begin(pairs, *earlier):
        return call(
            functools.partial(begin_kernel, len(earlier)), like((padded, depth), F32), place,
            (*earlier, *[a for pair in pairs for a in pair]), "begin", 14,
        )

    x1, r1 = S(x0), S(r0)
    q0, f0 = block(x0, part)
    (x1,) = after((x1,), q0)
    theirs = lambda r: C(r[padded:])

    def onward(way, rows, residual, size, begun, earlier):
        q, f = block(rows, size)
        (rows,) = after((rows,), q)
        further = way(rows[:part] if way is last else rows)
        q_other = C(q)
        (residual,) = after((residual,), q_other)
        further_residual = way(residual[:, :part] if way is last else residual)
        begun = begin([*earlier, (residual, q), (theirs(residual), q_other)], *begun)
        return q, f, further, further_residual, begun

    last = lambda x: T(x)
    q0_other, f0_other = C(q0), C(f0)
    q1, f1, x2, r2, begun = onward(T, x1, r1, 2 * part, (), [(r0, q0), (r0, q0_other)])
    (x2,) = after((x2,), begun, f0_other)
    q2, f2, x3, r3, begun = onward(S, x2, r2, 2 * part, (begun,), [])
    (x3,) = after((x3,), begun)
    q3, f3, x4, r4, begun = onward(last, x3, r3, 2 * part, (begun,), [])
    q4, f4 = block(x4, part)
    f4_other = C(f4)
    (begun,) = after((begun,), f4_other)
    update, sent = call(
        update_kernel, (like((padded, depth), F32), like((padded, depth))), place,
        (begun, r4, q4, theirs(r4), C(q4)), "update", 14,
    )

    whole, wide = like((padded, 2 * part)), like((padded, 2 * part), F32)

    def changes(update, blocks, outs):
        counts = tuple(len(f) for f in blocks)
        return call(
            functools.partial(change_kernel, counts), outs, place, (update, *[f for b in blocks for f in b]), "change", 8
        )

    hop = lambda ahead, came: call(hop_kernel, whole, place, (ahead, came), "hop", 4)
    (first,) = changes(sent, [(f4, f4_other)], (whole,))
    (sent_other,) = after((C(sent),), first)
    ahead = changes(after((sent,), first)[0], [(f3,), (f2,), (f1,), (f0, f0_other)], (wide,) * 4)
    first = T(first)
    (sent_other,) = after((sent_other,), *ahead)
    second, *behind = changes(sent_other, [(f3,), (f2,), (f1,)], (whole, wide, wide))
    (first,) = after((first,), second)
    second = S(second)
    for i, (way, back) in enumerate(((S, T), (T, S), (S, None))):
        total = hop(ahead[i], first)
        first = way(total)
        (second,) = after((second,), total)
        if back:
            total = hop(behind[i], second)
            second = back(total)
            (first,) = after((first,), total)
    given = C(second)
    (first,) = after((first,), given)
    ahead = ahead[3]
    own = call(last_kernel, whole, place, (ahead, first, given), "last", 4)
    new = None
    for i in (0, 1):
        change = swap(own, "blocks", [(0, 1)]) if i else own
        earlier = (new,) if i else ()
        new = call(
            functools.partial(apply_kernel, i), like(predictions.shape, F32), place,
            (predictions, change, *earlier), "apply", 6, (pltpu.VMEM((width, 2 * part), F32), dma((2,))),
            (pltpu.VMEM, pltpu.VMEM, *(pl.ANY,) * i), pl.ANY, {3: 0} if i else {},
        )
    return (coefficients + update[:width]).T, new.T


def plain_shards(inputs, projection, phases, inverse_blocks, labels, predictions, coefficients):
    out_width = predictions.shape[1]
    classes = lax.axis_index("cols") * out_width + jnp.arange(out_width, dtype=jnp.int32)
    onehot = (labels[:, None] == classes[None, :]).astype(F32)
    residual = (onehot - predictions).astype(BF16)
    angles = dot(inputs, projection) + phases.astype(F32)[None, :]
    half_features = jnp.cos(angles).astype(BF16)
    features_full = lax.all_gather(half_features, "cols", axis=1, tiled=True)
    own_gradient = lax.psum_scatter(
        lax.dot_general(features_full, residual, (((0,), (0,)), ((), ())), preferred_element_type=F32),
        "rows", scatter_dimension=0, tiled=True,
    )
    gradient_full = lax.all_gather(own_gradient, "rows", axis=0, tiled=True)
    update = DAMPING * jnp.dot(inverse_blocks[0], gradient_full, precision=lax.Precision.HIGHEST)
    sent = lax.all_gather(update.astype(BF16), "rows", axis=0, tiled=True)
    summed = lax.psum(dot(features_full, sent), "blocks")
    return coefficients + update, predictions + summed


def solution(mesh):
    n_rows, n_blocks = mesh.shape["rows"], mesh.shape["blocks"]
    small_ring = n_blocks == 2 and n_rows == 4 and mesh.shape["cols"] == 2
    shards = functools.partial(ring_shards, n_rows) if small_ring else plain_shards
    return jax.shard_map(
        shards,
        mesh=mesh,
        in_specs=(
            P(("groups", "rows"), None),
            P(None, ("groups", "blocks", "cols")),
            P(("groups", "blocks", "cols")),
            P(("groups", "blocks"), "rows", None),
            P(("groups", "rows")),
            P(("groups", "rows"), "cols"),
            P(("groups", "blocks", "rows"), "cols"),
        ),
        out_specs=(P(("groups", "blocks", "rows"), "cols"), P(("groups", "rows"), "cols")),
        check_vma=False,
    )
```

```python
import functools

import jax
import jax.numpy as jnp
from jax import lax
from jax.experimental import pallas as pl
from jax.experimental.pallas import tpu as pltpu
from jax.sharding import PartitionSpec as P

DAMPING = 0.5
F32, BF16 = jnp.float32, jnp.bfloat16
LANES = 128

SINE_TERMS = (
    6.283185280127733, -41.341680582549685, 81.60247253767959, -76.5810396203459, 39.75848375303386
)
TURNS = 0.15915494309189535


def cosine(angles, phases):
    turns = angles * TURNS + phases.astype(F32) * TURNS
    quarter = 0.25 - jnp.abs(turns - jnp.round(turns))
    square = quarter * quarter
    result = square * SINE_TERMS[-1] + SINE_TERMS[-2]
    for term in SINE_TERMS[-3::-1]:
        result = result * square + term
    return result * quarter


def dot(a, b):
    return jnp.dot(a, b, preferred_element_type=F32)


def dot_nt(a, b):
    return lax.dot_general(a, b, (((1,), (1,)), ((), ())), preferred_element_type=F32)


def call(kernel, out_shapes, place, args, name, vmem_mib, scratch=(), in_place=None, out_place=pltpu.VMEM, aliases={}):
    spaces = in_place or (pltpu.VMEM,) * len(args)
    vmem = pl.BlockSpec(memory_space=out_place)
    single = isinstance(out_shapes, jax.ShapeDtypeStruct)
    return pl.pallas_call(
        kernel,
        out_shape=out_shapes,
        in_specs=[pl.BlockSpec(memory_space=m) for m in (pltpu.SMEM, *spaces)],
        out_specs=vmem if single else (vmem,) * len(out_shapes),
        scratch_shapes=scratch,
        input_output_aliases=aliases,
        compiler_params=pltpu.CompilerParams(vmem_limit_bytes=vmem_mib << 20),
        name=name,
    )(place, *args)


def like(shape, dtype=BF16):
    return jax.ShapeDtypeStruct(tuple(shape), dtype)


def lanes(index, size):
    return pl.ds(pl.multiple_of(index * size, size), size)


def prepare_kernel(place, inputs, labels, predictions, rows, own, given, wide, tags, sems):
    width = predictions.shape[0]
    part = own.shape[1] // 2
    copies = []
    for j in (0, 1):
        block = 2 * place[1] + (place[2] ^ j)
        at, there = lanes(block, part), slice(j * part, (j + 1) * part)
        copies += [
            pltpu.make_async_copy(predictions.at[:, at], wide.at[:, there], sems.at[3 * j]),
            pltpu.make_async_copy(labels.at[:, at], tags.at[:, there], sems.at[3 * j + 1]),
            pltpu.make_async_copy(inputs.at[at], rows.at[there], sems.at[3 * j + 2]),
        ]
    for copy in copies:
        copy.start()
    tail = own.shape[0] - width
    own[width:], given[width:] = (jnp.zeros((tail, 2 * part), BF16),) * 2
    for j in (0, 1):
        copies[3 * j].wait()
        copies[3 * j + 1].wait()
        there = slice(j * part, (j + 1) * part)
        classes = lax.broadcasted_iota(jnp.int32, (width, part), 0) + place[2] * width
        residual = ((classes == tags[:, there]).astype(F32) - wide[:, there]).astype(BF16)
        own[:width, there] = residual
        given[:width, (1 - j) * part:(2 - j) * part] = residual
    for j in (0, 1):
        copies[3 * j + 2].wait()


def high_low(x):
    high = x.astype(BF16)
    return high, (x - high.astype(F32)).astype(BF16)


def round_kernel(place, x, out):
    out[...] = x[...].astype(BF16)


TILE = 512


def block_kernel(place, rows, w_own, w_other, p_own, p_other, inverse, out, own_slice, feats):
    inputs = rows[:feats.shape[0]]
    half, depth = w_own.shape[1], inverse.shape[0]
    total = None
    for i, (weights, phases) in enumerate(((w_own, p_own), (w_other, p_other))):
        for k in range(0, half, TILE):
            at = pl.ds(pl.multiple_of((place[2] ^ i) * half + k, TILE), TILE)
            tile = cosine(dot(inputs, weights[:, k:k + TILE]), phases[:, k:k + TILE]).astype(BF16)
            feats[:, at] = tile
            product = dot_nt(tile, inverse[:, at])
            total = product if total is None else total + product
    out[:, :depth], out[:, depth:] = high_low(total)
    own_slice[...] = feats[:, lanes(place[0], depth)]


def features_kernel(place, rows, w_own, w_other, p_own, p_other, feats, own_slice):
    half = w_own.shape[1]
    for i, (weights, phases) in enumerate(((w_own, p_own), (w_other, p_other))):
        for k in range(0, half, TILE):
            at = pl.ds(pl.multiple_of((place[2] ^ i) * half + k, TILE), TILE)
            feats[:, at] = cosine(dot(rows[...], weights[:, k:k + TILE]), phases[:, k:k + TILE]).astype(BF16)
    own_slice[...] = feats[:, lanes(place[0], own_slice.shape[1])]


def meet_kernel(place, feats, inverse, out):
    depth = inverse.shape[0]
    out[:, :depth], out[:, depth:] = high_low(dot_nt(feats[...], inverse[...]))


def product_of(refs, classes):
    total, short = None, None
    for residual, q in zip(refs[::2], refs[1::2]):
        left, right = residual[:classes], q[...]
        if right.shape[0] < 256:
            if short is None:
                short = left[:, :right.shape[0]], right
                continue
            at = slice(0, right.shape[0]) if left.shape[1] == right.shape[0] else slice(right.shape[0], None)
            left = jnp.concatenate([short[0], left[:, at]], axis=1)
            right = jnp.concatenate([short[1], right], axis=0)
            short = None
        product = dot(left, right)
        depth = product.shape[1] // 2
        product = product[:, :depth] + product[:, depth:]
        total = product if total is None else total + product
    return total


def begin_kernel(earlier, place, *refs):
    *pieces, out = refs
    total = product_of(pieces[earlier:], out.shape[0])
    out[...] = pieces[0][...] + total if earlier else total


def update_kernel(place, begun, *refs):
    *pieces, update, sent = refs
    total = DAMPING * (begun[...] + product_of(pieces, begun.shape[0]))
    update[...] = total
    sent[...] = total.astype(BF16)


def change_kernel(counts, place, sent, *refs):
    at = 0
    for count, out in zip(counts, refs[sum(counts):]):
        rows = refs[at][...] if count == 1 else jnp.concatenate([f[...] for f in refs[at:at + count]], axis=0)
        out[...] = dot_nt(sent[...], rows).astype(out.dtype)
        at += count


def hop_kernel(place, change, came, out):
    out[...] = (change[...] + came[...].astype(F32)).astype(BF16)


def last_kernel(place, change, came, given, out):
    part = out.shape[1] // 2
    for i in (0, 1):
        at, there = slice(i * part, (i + 1) * part), slice((1 - i) * part, (2 - i) * part)
        total = change[:, at] + came[:, at].astype(F32) + given[:, there].astype(F32)
        out[:, at] = total.astype(BF16)


def apply_kernel(which, place, predictions, change, *refs):
    new, total, sems = refs[-3:]
    width, part = total.shape[0], total.shape[1] // 2
    copies = []
    for j in (0, 1):
        at, there = lanes(2 * (place[1] ^ which) + (place[2] ^ j), part), slice(j * part, (j + 1) * part)
        total[:, there] = predictions[:, at] + change[:width, there].astype(F32)
        copies.append(pltpu.make_async_copy(total.at[:, there], new.at[:, at], sems.at[j]))
        copies[j].start()
    for copy in copies:
        copy.wait()


def swap(x, axes, pairs):
    return lax.ppermute(x, axes, [p for a, b in pairs for p in ((a, b), (b, a))])


def after(arrays, *others):
    return lax.optimization_barrier((*arrays, *others))[:len(arrays)]


def ring_shards(n_rows, inputs, projection, phases, inverse_blocks, labels, predictions, coefficients):
    ring = [2 * z for z in range(n_rows)] + [2 * z + 1 for z in reversed(range(n_rows))]
    size = len(ring)
    even = [(ring[i], ring[i + 1]) for i in range(0, size, 2)]
    odd = [(ring[i], ring[(i + 1) % size]) for i in range(1, size, 2)]
    ways = [[(2 * a + c, 2 * b + c) for c, pairs in enumerate(way) for a, b in pairs]
            for way in ((even, odd), (odd, even))]
    S = lambda x: swap(x, ("rows", "blocks", "cols"), ways[0])
    T = lambda x: swap(x, ("rows", "blocks", "cols"), ways[1])
    C = lambda x: swap(x, "cols", [(0, 1)])

    place = jnp.stack([lax.axis_index(a) for a in ("rows", "blocks", "cols")]).astype(jnp.int32)
    local_rows, width = predictions.shape
    part = local_rows // 4
    padded = -(-width // LANES) * LANES
    predictions, coefficients = predictions.T, coefficients.T
    depth = coefficients.shape[1]

    dma = pltpu.SemaphoreType.DMA
    block_rows = like((2 * part, inputs.shape[1]))
    x0, own, given = call(
        prepare_kernel, (block_rows, *(like((padded, 2 * part)),) * 2), place,
        tuple(pltpu.with_memory_space_constraint(a, pltpu.HBM) for a in (inputs, labels[None, :], predictions)),
        "prepare", 6,
        (pltpu.VMEM((width, 2 * part), F32), pltpu.VMEM((1, 2 * part), jnp.int32), dma((6,))), (pltpu.HBM,) * 3,
    )
    given = C(given)
    (x0,) = after((x0,), given)
    r0 = jnp.concatenate([own, given], axis=0)
    weights = (projection, C(projection))
    phases = phases[None, :]
    phases = (phases, C(phases))
    inverse = call(round_kernel, like(inverse_blocks.shape[1:]), place, (inverse_blocks[0],), "round", 10)

    def block(rows, size):
        scratch = (pltpu.VMEM((size, 2 * projection.shape[1]), BF16),)
        return call(
            block_kernel, (like((size, 2 * depth)), like((size, depth))), place,
            (rows, *weights, *phases, inverse), "block", 16, scratch,
        )

    def begin(pairs, *earlier):
        return call(
            functools.partial(begin_kernel, len(earlier)), like((padded, depth), F32), place,
            (*earlier, *[a for pair in pairs for a in pair]), "begin", 14,
        )

    x1, r1 = S(x0), S(r0)
    q0, f0 = block(x0, part)
    (x1,) = after((x1,), q0)
    theirs = lambda r: C(r[padded:])

    def onward(way, rows, residual, size, begun, earlier):
        feats, f = call(
            features_kernel, (like((size, inverse.shape[1])), like((size, depth))), place,
            (rows, *weights, *phases), "features", 14,
        )
        (rows,) = after((rows,), f)
        further = way(rows[:part] if way is last else rows)
        q = call(meet_kernel, like((size, 2 * depth)), place, (feats, inverse), "meet", 14)
        (residual,) = after((residual,), q)
        q_other = C(q)
        further_residual = way(residual[:, :part] if way is last else residual)
        begun = begin([*earlier, (residual, q), (theirs(residual), q_other)], *begun)
        return q, f, further, further_residual, begun

    last = lambda x: T(x)
    q0_other, f0_other = C(q0), C(f0)
    q1, f1, x2, r2, begun = onward(T, x1, r1, 2 * part, (), [(r0, q0), (r0, q0_other)])
    (x2,) = after((x2,), q1, f0_other)
    (r2,) = after((r2,), begun)
    q2, f2, x3, r3, begun = onward(S, x2, r2, 2 * part, (begun,), [])
    (x3,) = after((x3,), q2)
    (r3,) = after((r3,), begun)
    q3, f3, x4, r4, begun = onward(last, x3, r3, 2 * part, (begun,), [])
    (x4,) = after((x4,), q3)
    q4, f4 = block(x4, part)
    f4_other = C(f4)
    (begun,) = after((begun,), f4_other)
    update, sent = call(
        update_kernel, (like((padded, depth), F32), like((padded, depth))), place,
        (begun, r4, q4, theirs(r4), C(q4)), "update", 14,
    )

    whole, wide = like((padded, 2 * part)), like((padded, 2 * part), F32)

    def changes(update, blocks, outs):
        counts = tuple(len(f) for f in blocks)
        return call(
            functools.partial(change_kernel, counts), outs, place, (update, *[f for b in blocks for f in b]), "change", 8
        )

    hop = lambda ahead, came: call(hop_kernel, whole, place, (ahead, came), "hop", 4)
    (first,) = changes(sent, [(f4, f4_other)], (whole,))
    (sent_other,) = after((C(sent),), first)
    ahead = changes(after((sent,), first)[0], [(f3,), (f2,), (f1,), (f0, f0_other)], (wide,) * 4)
    first = T(first)
    (sent_other,) = after((sent_other,), *ahead)
    second, *behind = changes(sent_other, [(f3,), (f2,), (f1,)], (whole, wide, wide))
    (first,) = after((first,), second)
    second = S(second)
    for i, (way, back) in enumerate(((S, T), (T, S), (S, None))):
        total = hop(ahead[i], first)
        first = way(total)
        (second,) = after((second,), total)
        if back:
            total = hop(behind[i], second)
            second = back(total)
            (first,) = after((first,), total)
    given = C(second)
    (first,) = after((first,), given)
    ahead = ahead[3]
    own = call(last_kernel, whole, place, (ahead, first, given), "last", 4)
    new = None
    for i in (0, 1):
        change = swap(own, "blocks", [(0, 1)]) if i else own
        earlier = (new,) if i else ()
        new = call(
            functools.partial(apply_kernel, i), like(predictions.shape, F32), place,
            (predictions, change, *earlier), "apply", 6, (pltpu.VMEM((width, 2 * part), F32), dma((2,))),
            (pltpu.VMEM, pltpu.VMEM, *(pl.ANY,) * i), pl.ANY, {3: 0} if i else {},
        )
    return (coefficients + update[:width]).T, new.T


def plain_shards(inputs, projection, phases, inverse_blocks, labels, predictions, coefficients):
    out_width = predictions.shape[1]
    classes = lax.axis_index("cols") * out_width + jnp.arange(out_width, dtype=jnp.int32)
    onehot = (labels[:, None] == classes[None, :]).astype(F32)
    residual = (onehot - predictions).astype(BF16)
    angles = dot(inputs, projection) + phases.astype(F32)[None, :]
    half_features = jnp.cos(angles).astype(BF16)
    features_full = lax.all_gather(half_features, "cols", axis=1, tiled=True)
    own_gradient = lax.psum_scatter(
        lax.dot_general(features_full, residual, (((0,), (0,)), ((), ())), preferred_element_type=F32),
        "rows", scatter_dimension=0, tiled=True,
    )
    gradient_full = lax.all_gather(own_gradient, "rows", axis=0, tiled=True)
    update = DAMPING * jnp.dot(inverse_blocks[0], gradient_full, precision=lax.Precision.HIGHEST)
    sent = lax.all_gather(update.astype(BF16), "rows", axis=0, tiled=True)
    summed = lax.psum(dot(features_full, sent), "blocks")
    return coefficients + update, predictions + summed


def solution(mesh):
    n_rows, n_blocks = mesh.shape["rows"], mesh.shape["blocks"]
    small_ring = n_blocks == 2 and n_rows == 4 and mesh.shape["cols"] == 2
    shards = functools.partial(ring_shards, n_rows) if small_ring else plain_shards
    return jax.shard_map(
        shards,
        mesh=mesh,
        in_specs=(
            P(("groups", "rows"), None),
            P(None, ("groups", "blocks", "cols")),
            P(("groups", "blocks", "cols")),
            P(("groups", "blocks"), "rows", None),
            P(("groups", "rows")),
            P(("groups", "rows"), "cols"),
            P(("groups", "blocks", "rows"), "cols"),
        ),
        out_specs=(P(("groups", "blocks", "rows"), "cols"), P(("groups", "rows"), "cols")),
        check_vma=False,
    )
```

```python
import functools

import jax
import jax.numpy as jnp
from jax import lax
from jax.experimental import pallas as pl
from jax.experimental.pallas import tpu as pltpu
from jax.sharding import PartitionSpec as P

DAMPING = 0.5
F32, BF16 = jnp.float32, jnp.bfloat16
LANES = 128

SINE_TERMS = (
    6.283185280127733, -41.341680582549685, 81.60247253767959, -76.5810396203459, 39.75848375303386
)
TURNS = 0.15915494309189535


def cosine(angles, phases):
    turns = angles * TURNS + phases.astype(F32) * TURNS
    quarter = 0.25 - jnp.abs(turns - jnp.round(turns))
    square = quarter * quarter
    result = square * SINE_TERMS[-1] + SINE_TERMS[-2]
    for term in SINE_TERMS[-3::-1]:
        result = result * square + term
    return result * quarter


def dot(a, b):
    return jnp.dot(a, b, preferred_element_type=F32)


def dot_nt(a, b):
    return lax.dot_general(a, b, (((1,), (1,)), ((), ())), preferred_element_type=F32)


def call(kernel, out_shapes, place, args, name, vmem_mib, scratch=(), in_place=None, out_place=pltpu.VMEM, aliases={}):
    spaces = in_place or (pltpu.VMEM,) * len(args)
    vmem = pl.BlockSpec(memory_space=out_place)
    single = isinstance(out_shapes, jax.ShapeDtypeStruct)
    return pl.pallas_call(
        kernel,
        out_shape=out_shapes,
        in_specs=[pl.BlockSpec(memory_space=m) for m in (pltpu.SMEM, *spaces)],
        out_specs=vmem if single else (vmem,) * len(out_shapes),
        scratch_shapes=scratch,
        input_output_aliases=aliases,
        compiler_params=pltpu.CompilerParams(vmem_limit_bytes=vmem_mib << 20),
        name=name,
    )(place, *args)


def like(shape, dtype=BF16):
    return jax.ShapeDtypeStruct(tuple(shape), dtype)


def lanes(index, size):
    return pl.ds(pl.multiple_of(index * size, size), size)


def prepare_kernel(place, inputs, labels, predictions, rows, own, given, wide, tags, sems):
    width = predictions.shape[0]
    part = own.shape[1] // 2
    copies = []
    for j in (0, 1):
        block = 2 * place[1] + (place[2] ^ j)
        at, there = lanes(block, part), slice(j * part, (j + 1) * part)
        copies += [
            pltpu.make_async_copy(predictions.at[:, at], wide.at[:, there], sems.at[3 * j]),
            pltpu.make_async_copy(labels.at[:, at], tags.at[:, there], sems.at[3 * j + 1]),
            pltpu.make_async_copy(inputs.at[at], rows.at[there], sems.at[3 * j + 2]),
        ]
    for copy in copies:
        copy.start()
    tail = own.shape[0] - width
    own[width:], given[width:] = (jnp.zeros((tail, 2 * part), BF16),) * 2
    for j in (0, 1):
        copies[3 * j].wait()
        copies[3 * j + 1].wait()
        there = slice(j * part, (j + 1) * part)
        classes = lax.broadcasted_iota(jnp.int32, (width, part), 0) + place[2] * width
        residual = ((classes == tags[:, there]).astype(F32) - wide[:, there]).astype(BF16)
        own[:width, there] = residual
        given[:width, (1 - j) * part:(2 - j) * part] = residual
    for j in (0, 1):
        copies[3 * j + 2].wait()


def high_low(x):
    high = x.astype(BF16)
    return high, (x - high.astype(F32)).astype(BF16)


def round_kernel(place, x, out):
    out[...] = x[...].astype(BF16)


TILE = 512


def block_kernel(place, rows, w_own, w_other, p_own, p_other, inverse, out, own_slice, feats):
    inputs = rows[:feats.shape[0]]
    half, depth = w_own.shape[1], inverse.shape[0]
    total = None
    for i, (weights, phases) in enumerate(((w_own, p_own), (w_other, p_other))):
        for k in range(0, half, TILE):
            at = pl.ds(pl.multiple_of((place[2] ^ i) * half + k, TILE), TILE)
            tile = cosine(dot(inputs, weights[:, k:k + TILE]), phases[:, k:k + TILE]).astype(BF16)
            feats[:, at] = tile
            product = dot_nt(tile, inverse[:, at])
            total = product if total is None else total + product
    out[:, :depth], out[:, depth:] = high_low(total)
    own_slice[...] = feats[:, lanes(place[0], depth)]


def features_kernel(place, rows, w_own, w_other, p_own, p_other, feats, own_slice):
    half = w_own.shape[1]
    for i, (weights, phases) in enumerate(((w_own, p_own), (w_other, p_other))):
        for k in range(0, half, TILE):
            at = pl.ds(pl.multiple_of((place[2] ^ i) * half + k, TILE), TILE)
            feats[:, at] = cosine(dot(rows[...], weights[:, k:k + TILE]), phases[:, k:k + TILE]).astype(BF16)
    own_slice[...] = feats[:, lanes(place[0], own_slice.shape[1])]


def meet_kernel(place, feats, inverse, out):
    depth = inverse.shape[0]
    out[:, :depth], out[:, depth:] = high_low(dot_nt(feats[...], inverse[...]))


def product_of(refs, classes):
    total, short = None, None
    for residual, q in zip(refs[::2], refs[1::2]):
        left, right = residual[:classes], q[...]
        if right.shape[0] < 256:
            if short is None:
                short = left[:, :right.shape[0]], right
                continue
            at = slice(0, right.shape[0]) if left.shape[1] == right.shape[0] else slice(right.shape[0], None)
            left = jnp.concatenate([short[0], left[:, at]], axis=1)
            right = jnp.concatenate([short[1], right], axis=0)
            short = None
        product = dot(left, right)
        depth = product.shape[1] // 2
        product = product[:, :depth] + product[:, depth:]
        total = product if total is None else total + product
    return total


def begin_kernel(earlier, place, *refs):
    *pieces, out = refs
    total = product_of(pieces[earlier:], out.shape[0])
    out[...] = pieces[0][...] + total if earlier else total


def update_kernel(place, begun, *refs):
    *pieces, update, sent = refs
    total = DAMPING * (begun[...] + product_of(pieces, begun.shape[0]))
    update[...] = total
    sent[...] = total.astype(BF16)


def change_kernel(counts, place, sent, *refs):
    at = 0
    for count, out in zip(counts, refs[sum(counts):]):
        rows = refs[at][...] if count == 1 else jnp.concatenate([f[...] for f in refs[at:at + count]], axis=0)
        out[...] = dot_nt(sent[...], rows).astype(out.dtype)
        at += count


def last_kernel(place, change, came, given, out):
    part = out.shape[1] // 2
    for i in (0, 1):
        at, there = slice(i * part, (i + 1) * part), slice((1 - i) * part, (2 - i) * part)
        total = change[:, at] + came[:, at].astype(F32) + given[:, there].astype(F32)
        out[:, at] = total.astype(BF16)


def apply_kernel(which, place, predictions, change, *refs):
    new, total, sems = refs[-3:]
    width, part = total.shape[0], total.shape[1] // 2
    copies = []
    for j in (0, 1):
        at, there = lanes(2 * (place[1] ^ which) + (place[2] ^ j), part), slice(j * part, (j + 1) * part)
        total[:, there] = predictions[:, at] + change[:width, there].astype(F32)
        copies.append(pltpu.make_async_copy(total.at[:, there], new.at[:, at], sems.at[j]))
        copies[j].start()
    for copy in copies:
        copy.wait()


def swap(x, axes, pairs):
    return lax.ppermute(x, axes, [p for a, b in pairs for p in ((a, b), (b, a))])


def after(arrays, *others):
    return lax.optimization_barrier((*arrays, *others))[:len(arrays)]


def ring_shards(n_rows, inputs, projection, phases, inverse_blocks, labels, predictions, coefficients):
    ring = [2 * z for z in range(n_rows)] + [2 * z + 1 for z in reversed(range(n_rows))]
    size = len(ring)
    even = [(ring[i], ring[i + 1]) for i in range(0, size, 2)]
    odd = [(ring[i], ring[(i + 1) % size]) for i in range(1, size, 2)]
    ways = [[(2 * a + c, 2 * b + c) for c, pairs in enumerate(way) for a, b in pairs]
            for way in ((even, odd), (odd, even))]
    S = lambda x: swap(x, ("rows", "blocks", "cols"), ways[0])
    T = lambda x: swap(x, ("rows", "blocks", "cols"), ways[1])
    C = lambda x: swap(x, "cols", [(0, 1)])

    place = jnp.stack([lax.axis_index(a) for a in ("rows", "blocks", "cols")]).astype(jnp.int32)
    local_rows, width = predictions.shape
    part = local_rows // 4
    padded = -(-width // LANES) * LANES
    predictions, coefficients = predictions.T, coefficients.T
    depth = coefficients.shape[1]

    dma = pltpu.SemaphoreType.DMA
    block_rows = like((2 * part, inputs.shape[1]))
    x0, own, given = call(
        prepare_kernel, (block_rows, *(like((padded, 2 * part)),) * 2), place,
        tuple(pltpu.with_memory_space_constraint(a, pltpu.HBM) for a in (inputs, labels[None, :], predictions)),
        "prepare", 6,
        (pltpu.VMEM((width, 2 * part), F32), pltpu.VMEM((1, 2 * part), jnp.int32), dma((6,))), (pltpu.HBM,) * 3,
    )
    given = C(given)
    (x0,) = after((x0,), given)
    r0 = jnp.concatenate([own, given], axis=0)
    weights = (projection, C(projection))
    phases = phases[None, :]
    phases = (phases, C(phases))
    inverse = call(round_kernel, like(inverse_blocks.shape[1:]), place, (inverse_blocks[0],), "round", 10)

    def block(rows, size):
        scratch = (pltpu.VMEM((size, 2 * projection.shape[1]), BF16),)
        return call(
            block_kernel, (like((size, 2 * depth)), like((size, depth))), place,
            (rows, *weights, *phases, inverse), "block", 16, scratch,
        )

    def begin(pairs, *earlier):
        return call(
            functools.partial(begin_kernel, len(earlier)), like((padded, depth), F32), place,
            (*earlier, *[a for pair in pairs for a in pair]), "begin", 14,
        )

    x1, r1 = S(x0), S(r0)
    q0, f0 = block(x0, part)
    (x1,) = after((x1,), q0)
    theirs = lambda r: C(r[padded:])

    def onward(way, rows, residual, size, begun, earlier):
        feats, f = call(
            features_kernel, (like((size, inverse.shape[1])), like((size, depth))), place,
            (rows, *weights, *phases), "features", 14,
        )
        (rows,) = after((rows,), f)
        further = way(rows[:part] if way is last else rows)
        q = call(meet_kernel, like((size, 2 * depth)), place, (feats, inverse), "meet", 14)
        (residual,) = after((residual,), q)
        q_other = C(q)
        further_residual = way(residual[:, :part] if way is last else residual)
        begun = begin([*earlier, (residual, q), (theirs(residual), q_other)], *begun)
        return q, f, further, further_residual, begun

    last = lambda x: T(x)
    q0_other, f0_other = C(q0), C(f0)
    q1, f1, x2, r2, begun = onward(T, x1, r1, 2 * part, (), [(r0, q0), (r0, q0_other)])
    (x2,) = after((x2,), q1, f0_other)
    (r2,) = after((r2,), begun)
    q2, f2, x3, r3, begun = onward(S, x2, r2, 2 * part, (begun,), [])
    (x3,) = after((x3,), q2)
    (r3,) = after((r3,), begun)
    q3, f3, x4, r4, begun = onward(last, x3, r3, 2 * part, (begun,), [])
    (x4,) = after((x4,), q3)
    q4, f4 = block(x4, part)
    f4_other = C(f4)
    (begun,) = after((begun,), f4_other)
    update, sent = call(
        update_kernel, (like((padded, depth), F32), like((padded, depth))), place,
        (begun, r4, q4, theirs(r4), C(q4)), "update", 14,
    )

    whole, wide = like((padded, 2 * part)), like((padded, 2 * part), F32)

    def changes(update, blocks, outs):
        counts = tuple(len(f) for f in blocks)
        return call(
            functools.partial(change_kernel, counts), outs, place, (update, *[f for b in blocks for f in b]), "change", 8
        )

    hop = lambda ahead, came: (ahead + came.astype(F32)).astype(BF16)
    (first,) = changes(sent, [(f4, f4_other)], (whole,))
    (sent_other,) = after((C(sent),), first)
    ahead = changes(after((sent,), first)[0], [(f3,), (f2,), (f1,), (f0, f0_other)], (wide,) * 4)
    first = T(first)
    (sent_other,) = after((sent_other,), *ahead)
    second, *behind = changes(sent_other, [(f3,), (f2,), (f1,)], (whole, wide, wide))
    (first,) = after((first,), second)
    second = S(second)
    for i, (way, back) in enumerate(((S, T), (T, S), (S, None))):
        total = hop(ahead[i], first)
        first = way(total)
        (second,) = after((second,), total)
        if back:
            total = hop(behind[i], second)
            second = back(total)
            (first,) = after((first,), total)
    given = C(second)
    (first,) = after((first,), given)
    ahead = ahead[3]
    own = call(last_kernel, whole, place, (ahead, first, given), "last", 4)
    new = None
    for i in (0, 1):
        change = swap(own, "blocks", [(0, 1)]) if i else own
        earlier = (new,) if i else ()
        new = call(
            functools.partial(apply_kernel, i), like(predictions.shape, F32), place,
            (predictions, change, *earlier), "apply", 6, (pltpu.VMEM((width, 2 * part), F32), dma((2,))),
            (pltpu.VMEM, pltpu.VMEM, *(pl.ANY,) * i), pl.ANY, {3: 0} if i else {},
        )
    return (coefficients + update[:width]).T, new.T


def plain_shards(inputs, projection, phases, inverse_blocks, labels, predictions, coefficients):
    out_width = predictions.shape[1]
    classes = lax.axis_index("cols") * out_width + jnp.arange(out_width, dtype=jnp.int32)
    onehot = (labels[:, None] == classes[None, :]).astype(F32)
    residual = (onehot - predictions).astype(BF16)
    angles = dot(inputs, projection) + phases.astype(F32)[None, :]
    half_features = jnp.cos(angles).astype(BF16)
    features_full = lax.all_gather(half_features, "cols", axis=1, tiled=True)
    own_gradient = lax.psum_scatter(
        lax.dot_general(features_full, residual, (((0,), (0,)), ((), ())), preferred_element_type=F32),
        "rows", scatter_dimension=0, tiled=True,
    )
    gradient_full = lax.all_gather(own_gradient, "rows", axis=0, tiled=True)
    update = DAMPING * jnp.dot(inverse_blocks[0], gradient_full, precision=lax.Precision.HIGHEST)
    sent = lax.all_gather(update.astype(BF16), "rows", axis=0, tiled=True)
    summed = lax.psum(dot(features_full, sent), "blocks")
    return coefficients + update, predictions + summed


def solution(mesh):
    n_rows, n_blocks = mesh.shape["rows"], mesh.shape["blocks"]
    small_ring = n_blocks == 2 and n_rows == 4 and mesh.shape["cols"] == 2
    shards = functools.partial(ring_shards, n_rows) if small_ring else plain_shards
    return jax.shard_map(
        shards,
        mesh=mesh,
        in_specs=(
            P(("groups", "rows"), None),
            P(None, ("groups", "blocks", "cols")),
            P(("groups", "blocks", "cols")),
            P(("groups", "blocks"), "rows", None),
            P(("groups", "rows")),
            P(("groups", "rows"), "cols"),
            P(("groups", "blocks", "rows"), "cols"),
        ),
        out_specs=(P(("groups", "blocks", "rows"), "cols"), P(("groups", "rows"), "cols")),
        check_vma=False,
    )
```

```python
import functools

import jax
import jax.numpy as jnp
from jax import lax
from jax.experimental import pallas as pl
from jax.experimental.pallas import tpu as pltpu
from jax.sharding import PartitionSpec as P

DAMPING = 0.5
F32, BF16 = jnp.float32, jnp.bfloat16
LANES = 128

SINE_TERMS = (
    6.283185280127733, -41.341680582549685, 81.60247253767959, -76.5810396203459, 39.75848375303386
)
TURNS = 0.15915494309189535


def cosine(angles, phases):
    turns = angles * TURNS + phases.astype(F32) * TURNS
    quarter = 0.25 - jnp.abs(turns - jnp.round(turns))
    square = quarter * quarter
    result = square * SINE_TERMS[-1] + SINE_TERMS[-2]
    for term in SINE_TERMS[-3::-1]:
        result = result * square + term
    return result * quarter


def dot(a, b):
    return jnp.dot(a, b, preferred_element_type=F32)


def dot_nt(a, b):
    return lax.dot_general(a, b, (((1,), (1,)), ((), ())), preferred_element_type=F32)


def call(kernel, out_shapes, place, args, name, vmem_mib, scratch=(), in_place=None, out_place=pltpu.VMEM, aliases={}):
    spaces = in_place or (pltpu.VMEM,) * len(args)
    vmem = pl.BlockSpec(memory_space=out_place)
    single = isinstance(out_shapes, jax.ShapeDtypeStruct)
    return pl.pallas_call(
        kernel,
        out_shape=out_shapes,
        in_specs=[pl.BlockSpec(memory_space=m) for m in (pltpu.SMEM, *spaces)],
        out_specs=vmem if single else (vmem,) * len(out_shapes),
        scratch_shapes=scratch,
        input_output_aliases=aliases,
        compiler_params=pltpu.CompilerParams(vmem_limit_bytes=vmem_mib << 20),
        name=name,
    )(place, *args)


def like(shape, dtype=BF16):
    return jax.ShapeDtypeStruct(tuple(shape), dtype)


def lanes(index, size):
    return pl.ds(pl.multiple_of(index * size, size), size)


def prepare_kernel(place, inputs, labels, predictions, rows, own, given, wide, tags, sems):
    width = predictions.shape[0]
    part = own.shape[1] // 2
    copies = []
    for j in (0, 1):
        block = 2 * place[1] + (place[2] ^ j)
        at, there = lanes(block, part), slice(j * part, (j + 1) * part)
        copies += [
            pltpu.make_async_copy(predictions.at[:, at], wide.at[:, there], sems.at[3 * j]),
            pltpu.make_async_copy(labels.at[:, at], tags.at[:, there], sems.at[3 * j + 1]),
            pltpu.make_async_copy(inputs.at[at], rows.at[there], sems.at[3 * j + 2]),
        ]
    for copy in copies:
        copy.start()
    tail = own.shape[0] - width
    own[width:], given[width:] = (jnp.zeros((tail, 2 * part), BF16),) * 2
    for j in (0, 1):
        copies[3 * j].wait()
        copies[3 * j + 1].wait()
        there = slice(j * part, (j + 1) * part)
        classes = lax.broadcasted_iota(jnp.int32, (width, part), 0) + place[2] * width
        residual = ((classes == tags[:, there]).astype(F32) - wide[:, there]).astype(BF16)
        own[:width, there] = residual
        given[:width, (1 - j) * part:(2 - j) * part] = residual
    for j in (0, 1):
        copies[3 * j + 2].wait()


def high_low(x):
    high = x.astype(BF16)
    return high, (x - high.astype(F32)).astype(BF16)


def round_kernel(place, x, out):
    out[...] = x[...].astype(BF16)


TILE = 512


def block_kernel(place, rows, w_own, w_other, p_own, p_other, inverse, out, own_slice, feats):
    inputs = rows[:feats.shape[0]]
    half, depth = w_own.shape[1], inverse.shape[0]
    total = None
    for i, (weights, phases) in enumerate(((w_own, p_own), (w_other, p_other))):
        for k in range(0, half, TILE):
            at = pl.ds(pl.multiple_of((place[2] ^ i) * half + k, TILE), TILE)
            tile = cosine(dot(inputs, weights[:, k:k + TILE]), phases[:, k:k + TILE]).astype(BF16)
            feats[:, at] = tile
            product = dot_nt(tile, inverse[:, at])
            total = product if total is None else total + product
    out[:, :depth], out[:, depth:] = high_low(total)
    own_slice[...] = feats[:, lanes(place[0], depth)]


def features_kernel(place, rows, w_own, w_other, p_own, p_other, feats, own_slice):
    half = w_own.shape[1]
    for i, (weights, phases) in enumerate(((w_own, p_own), (w_other, p_other))):
        for k in range(0, half, TILE):
            at = pl.ds(pl.multiple_of((place[2] ^ i) * half + k, TILE), TILE)
            feats[:, at] = cosine(dot(rows[...], weights[:, k:k + TILE]), phases[:, k:k + TILE]).astype(BF16)
    own_slice[...] = feats[:, lanes(place[0], own_slice.shape[1])]


def meet_kernel(place, feats, inverse, out):
    depth = inverse.shape[0]
    out[:, :depth], out[:, depth:] = high_low(dot_nt(feats[...], inverse[...]))


def product_of(refs, classes):
    total, short = None, None
    for residual, q in zip(refs[::2], refs[1::2]):
        left, right = residual[:classes], q[...]
        if right.shape[0] < 256:
            if short is None:
                short = left[:, :right.shape[0]], right
                continue
            at = slice(0, right.shape[0]) if left.shape[1] == right.shape[0] else slice(right.shape[0], None)
            left = jnp.concatenate([short[0], left[:, at]], axis=1)
            right = jnp.concatenate([short[1], right], axis=0)
            short = None
        product = dot(left, right)
        depth = product.shape[1] // 2
        product = product[:, :depth] + product[:, depth:]
        total = product if total is None else total + product
    return total


def begin_kernel(earlier, place, *refs):
    *pieces, out = refs
    total = product_of(pieces[earlier:], out.shape[0])
    out[...] = pieces[0][...] + total if earlier else total


def update_kernel(place, begun, *refs):
    *pieces, update, sent = refs
    total = DAMPING * (begun[...] + product_of(pieces, begun.shape[0]))
    update[...] = total
    sent[...] = total.astype(BF16)


def change_kernel(counts, turned, place, sent, *refs):
    at = 0
    for count, out in zip(counts, refs[sum(counts):]):
        rows = refs[at][...] if count == 1 else jnp.concatenate([f[...] for f in refs[at:at + count]], axis=0)
        if turned:
            part = rows.shape[0] // 2
            rows = jnp.concatenate([rows[part:], rows[:part]], axis=0)
        out[...] = dot_nt(sent[...], rows).astype(out.dtype)
        at += count


def apply_kernel(which, place, predictions, change, *refs):
    new, total, sems = refs[-3:]
    width, part = total.shape[0], total.shape[1] // 2
    copies = []
    for j in (0, 1):
        at, there = lanes(2 * (place[1] ^ which) + (place[2] ^ j), part), slice(j * part, (j + 1) * part)
        total[:, there] = predictions[:, at] + change[:width, there].astype(F32)
        copies.append(pltpu.make_async_copy(total.at[:, there], new.at[:, at], sems.at[j]))
        copies[j].start()
    for copy in copies:
        copy.wait()


def swap(x, axes, pairs):
    return lax.ppermute(x, axes, [p for a, b in pairs for p in ((a, b), (b, a))])


def after(arrays, *others):
    return lax.optimization_barrier((*arrays, *others))[:len(arrays)]


def ring_shards(n_rows, inputs, projection, phases, inverse_blocks, labels, predictions, coefficients):
    ring = [2 * z for z in range(n_rows)] + [2 * z + 1 for z in reversed(range(n_rows))]
    size = len(ring)
    even = [(ring[i], ring[i + 1]) for i in range(0, size, 2)]
    odd = [(ring[i], ring[(i + 1) % size]) for i in range(1, size, 2)]
    ways = [[(2 * a + c, 2 * b + c) for c, pairs in enumerate(way) for a, b in pairs]
            for way in ((even, odd), (odd, even))]
    S = lambda x: swap(x, ("rows", "blocks", "cols"), ways[0])
    T = lambda x: swap(x, ("rows", "blocks", "cols"), ways[1])
    C = lambda x: swap(x, "cols", [(0, 1)])

    place = jnp.stack([lax.axis_index(a) for a in ("rows", "blocks", "cols")]).astype(jnp.int32)
    local_rows, width = predictions.shape
    part = local_rows // 4
    padded = -(-width // LANES) * LANES
    predictions, coefficients = predictions.T, coefficients.T
    depth = coefficients.shape[1]

    dma = pltpu.SemaphoreType.DMA
    block_rows = like((2 * part, inputs.shape[1]))
    x0, own, given = call(
        prepare_kernel, (block_rows, *(like((padded, 2 * part)),) * 2), place,
        tuple(pltpu.with_memory_space_constraint(a, pltpu.HBM) for a in (inputs, labels[None, :], predictions)),
        "prepare", 6,
        (pltpu.VMEM((width, 2 * part), F32), pltpu.VMEM((1, 2 * part), jnp.int32), dma((6,))), (pltpu.HBM,) * 3,
    )
    given = C(given)
    (x0,) = after((x0,), given)
    r0 = jnp.concatenate([own, given], axis=0)
    weights = (projection, C(projection))
    phases = phases[None, :]
    phases = (phases, C(phases))
    inverse = call(round_kernel, like(inverse_blocks.shape[1:]), place, (inverse_blocks[0],), "round", 10)

    def block(rows, size):
        scratch = (pltpu.VMEM((size, 2 * projection.shape[1]), BF16),)
        return call(
            block_kernel, (like((size, 2 * depth)), like((size, depth))), place,
            (rows, *weights, *phases, inverse), "block", 16, scratch,
        )

    def begin(pairs, *earlier):
        return call(
            functools.partial(begin_kernel, len(earlier)), like((padded, depth), F32), place,
            (*earlier, *[a for pair in pairs for a in pair]), "begin", 14,
        )

    x1, r1 = S(x0), S(r0)
    q0, f0 = block(x0, part)
    (x1,) = after((x1,), q0)
    theirs = lambda r: C(r[padded:])

    def onward(way, rows, residual, size, begun, earlier):
        feats, f = call(
            features_kernel, (like((size, inverse.shape[1])), like((size, depth))), place,
            (rows, *weights, *phases), "features", 14,
        )
        (rows,) = after((rows,), f)
        further = way(rows[:part] if way is last else rows)
        q = call(meet_kernel, like((size, 2 * depth)), place, (feats, inverse), "meet", 14)
        (residual,) = after((residual,), q)
        q_other = C(q)
        further_residual = way(residual[:, :part] if way is last else residual)
        begun = begin([*earlier, (residual, q), (theirs(residual), q_other)], *begun)
        return q, f, further, further_residual, begun

    last = lambda x: T(x)
    q0_other, f0_other = C(q0), C(f0)
    q1, f1, x2, r2, begun = onward(T, x1, r1, 2 * part, (), [(r0, q0), (r0, q0_other)])
    (x2,) = after((x2,), q1, f0_other)
    (r2,) = after((r2,), begun)
    q2, f2, x3, r3, begun = onward(S, x2, r2, 2 * part, (begun,), [])
    (x3,) = after((x3,), q2)
    (r3,) = after((r3,), begun)
    q3, f3, x4, r4, begun = onward(last, x3, r3, 2 * part, (begun,), [])
    (x4,) = after((x4,), q3)
    q4, f4 = block(x4, part)
    f4_other = C(f4)
    (begun,) = after((begun,), f4_other)
    update, sent = call(
        update_kernel, (like((padded, depth), F32), like((padded, depth))), place,
        (begun, r4, q4, theirs(r4), C(q4)), "update", 14,
    )

    whole, wide = like((padded, 2 * part)), like((padded, 2 * part), F32)

    def changes(update, blocks, outs, turned=False):
        counts = tuple(len(f) for f in blocks)
        return call(
            functools.partial(change_kernel, counts, turned), outs, place, (update, *[f for b in blocks for f in b]), "change", 8
        )

    hop = lambda ahead, came: (ahead + came.astype(F32)).astype(BF16)
    (first,) = changes(sent, [(f4, f4_other)], (whole,))
    (sent_other,) = after((C(sent),), first)
    ahead = changes(after((sent,), first)[0], [(f3,), (f2,), (f1,), (f0, f0_other)], (wide,) * 4)
    first = T(first)
    (sent_other,) = after((sent_other,), *ahead)
    second, *behind = changes(sent_other, [(f3,), (f2,), (f1,)], (whole, wide, wide), True)
    (first,) = after((first,), second)
    second = S(second)
    for i, (way, back) in enumerate(((S, T), (T, S), (S, None))):
        total = hop(ahead[i], first)
        first = way(total)
        (second,) = after((second,), total)
        if back:
            total = hop(behind[i], second)
            second = back(total)
            (first,) = after((first,), total)
    given = C(second)
    (first,) = after((first,), given)
    own = (ahead[3] + first.astype(F32) + given.astype(F32)).astype(BF16)
    new = None
    for i in (0, 1):
        change = swap(own, "blocks", [(0, 1)]) if i else own
        earlier = (new,) if i else ()
        new = call(
            functools.partial(apply_kernel, i), like(predictions.shape, F32), place,
            (predictions, change, *earlier), "apply", 6, (pltpu.VMEM((width, 2 * part), F32), dma((2,))),
            (pltpu.VMEM, pltpu.VMEM, *(pl.ANY,) * i), pl.ANY, {3: 0} if i else {},
        )
    return (coefficients + update[:width]).T, new.T


def plain_shards(inputs, projection, phases, inverse_blocks, labels, predictions, coefficients):
    out_width = predictions.shape[1]
    classes = lax.axis_index("cols") * out_width + jnp.arange(out_width, dtype=jnp.int32)
    onehot = (labels[:, None] == classes[None, :]).astype(F32)
    residual = (onehot - predictions).astype(BF16)
    angles = dot(inputs, projection) + phases.astype(F32)[None, :]
    half_features = jnp.cos(angles).astype(BF16)
    features_full = lax.all_gather(half_features, "cols", axis=1, tiled=True)
    own_gradient = lax.psum_scatter(
        lax.dot_general(features_full, residual, (((0,), (0,)), ((), ())), preferred_element_type=F32),
        "rows", scatter_dimension=0, tiled=True,
    )
    gradient_full = lax.all_gather(own_gradient, "rows", axis=0, tiled=True)
    update = DAMPING * jnp.dot(inverse_blocks[0], gradient_full, precision=lax.Precision.HIGHEST)
    sent = lax.all_gather(update.astype(BF16), "rows", axis=0, tiled=True)
    summed = lax.psum(dot(features_full, sent), "blocks")
    return coefficients + update, predictions + summed


def solution(mesh):
    n_rows, n_blocks = mesh.shape["rows"], mesh.shape["blocks"]
    small_ring = n_blocks == 2 and n_rows == 4 and mesh.shape["cols"] == 2
    shards = functools.partial(ring_shards, n_rows) if small_ring else plain_shards
    return jax.shard_map(
        shards,
        mesh=mesh,
        in_specs=(
            P(("groups", "rows"), None),
            P(None, ("groups", "blocks", "cols")),
            P(("groups", "blocks", "cols")),
            P(("groups", "blocks"), "rows", None),
            P(("groups", "rows")),
            P(("groups", "rows"), "cols"),
            P(("groups", "blocks", "rows"), "cols"),
        ),
        out_specs=(P(("groups", "blocks", "rows"), "cols"), P(("groups", "rows"), "cols")),
        check_vma=False,
    )
```

```python
import functools

import jax
import jax.numpy as jnp
from jax import lax
from jax.experimental import pallas as pl
from jax.experimental.pallas import tpu as pltpu
from jax.sharding import PartitionSpec as P

DAMPING = 0.5
F32, BF16 = jnp.float32, jnp.bfloat16
LANES = 128

SINE_TERMS = (
    6.283185280127733, -41.341680582549685, 81.60247253767959, -76.5810396203459, 39.75848375303386
)
TURNS = 0.15915494309189535


def cosine(angles, phases):
    turns = angles * TURNS + phases.astype(F32) * TURNS
    quarter = 0.25 - jnp.abs(turns - jnp.round(turns))
    square = quarter * quarter
    result = square * SINE_TERMS[-1] + SINE_TERMS[-2]
    for term in SINE_TERMS[-3::-1]:
        result = result * square + term
    return result * quarter


def dot(a, b):
    return jnp.dot(a, b, preferred_element_type=F32)


def dot_nt(a, b):
    return lax.dot_general(a, b, (((1,), (1,)), ((), ())), preferred_element_type=F32)


def call(kernel, out_shapes, place, args, name, vmem_mib, scratch=(), in_place=None, out_place=pltpu.VMEM, aliases={}):
    spaces = in_place or (pltpu.VMEM,) * len(args)
    vmem = pl.BlockSpec(memory_space=out_place)
    single = isinstance(out_shapes, jax.ShapeDtypeStruct)
    return pl.pallas_call(
        kernel,
        out_shape=out_shapes,
        in_specs=[pl.BlockSpec(memory_space=m) for m in (pltpu.SMEM, *spaces)],
        out_specs=vmem if single else (vmem,) * len(out_shapes),
        scratch_shapes=scratch,
        input_output_aliases=aliases,
        compiler_params=pltpu.CompilerParams(vmem_limit_bytes=vmem_mib << 20),
        name=name,
    )(place, *args)


def like(shape, dtype=BF16):
    return jax.ShapeDtypeStruct(tuple(shape), dtype)


def lanes(index, size):
    return pl.ds(pl.multiple_of(index * size, size), size)


def prepare_kernel(place, inputs, labels, predictions, rows, own, given, wide, tags, sems):
    width = predictions.shape[0]
    part = own.shape[1] // 2
    copies = []
    for j in (0, 1):
        block = 2 * place[1] + (place[2] ^ j)
        at, there = lanes(block, part), slice(j * part, (j + 1) * part)
        copies += [
            pltpu.make_async_copy(predictions.at[:, at], wide.at[:, there], sems.at[3 * j]),
            pltpu.make_async_copy(labels.at[:, at], tags.at[:, there], sems.at[3 * j + 1]),
            pltpu.make_async_copy(inputs.at[at], rows.at[there], sems.at[3 * j + 2]),
        ]
    for copy in copies:
        copy.start()
    tail = own.shape[0] - width
    own[width:], given[width:] = (jnp.zeros((tail, 2 * part), BF16),) * 2
    for j in (0, 1):
        copies[3 * j].wait()
        copies[3 * j + 1].wait()
        there = slice(j * part, (j + 1) * part)
        classes = lax.broadcasted_iota(jnp.int32, (width, part), 0) + place[2] * width
        residual = ((classes == tags[:, there]).astype(F32) - wide[:, there]).astype(BF16)
        own[:width, there] = residual
        given[:width, (1 - j) * part:(2 - j) * part] = residual
    for j in (0, 1):
        copies[3 * j + 2].wait()


def high_low(x):
    high = x.astype(BF16)
    return high, (x - high.astype(F32)).astype(BF16)


def round_kernel(place, x, out):
    out[...] = x[...].astype(BF16)


TILE = 512


def block_kernel(place, rows, w_own, w_other, p_own, p_other, inverse, out, own_slice, feats):
    inputs = rows[:feats.shape[0]]
    half, depth = w_own.shape[1], inverse.shape[0]
    total = None
    for i, (weights, phases) in enumerate(((w_own, p_own), (w_other, p_other))):
        for k in range(0, half, TILE):
            at = pl.ds(pl.multiple_of((place[2] ^ i) * half + k, TILE), TILE)
            tile = cosine(dot(inputs, weights[:, k:k + TILE]), phases[:, k:k + TILE]).astype(BF16)
            feats[:, at] = tile
            product = dot_nt(tile, inverse[:, at])
            total = product if total is None else total + product
    out[:, :depth], out[:, depth:] = high_low(total)
    own_slice[...] = feats[:, lanes(place[0], depth)]


def features_kernel(place, rows, w_own, w_other, p_own, p_other, feats, own_slice):
    half = w_own.shape[1]
    for i, (weights, phases) in enumerate(((w_own, p_own), (w_other, p_other))):
        for k in range(0, half, TILE):
            at = pl.ds(pl.multiple_of((place[2] ^ i) * half + k, TILE), TILE)
            feats[:, at] = cosine(dot(rows[...], weights[:, k:k + TILE]), phases[:, k:k + TILE]).astype(BF16)
    own_slice[...] = feats[:, lanes(place[0], own_slice.shape[1])]


def meet_kernel(place, feats, inverse, out):
    depth = inverse.shape[0]
    out[:, :depth], out[:, depth:] = high_low(dot_nt(feats[...], inverse[...]))


def product_of(refs, classes):
    total, short = None, None
    for residual, q in zip(refs[::2], refs[1::2]):
        left, right = residual[:classes], q[...]
        if right.shape[0] < 256:
            if short is None:
                short = left[:, :right.shape[0]], right
                continue
            at = slice(0, right.shape[0]) if left.shape[1] == right.shape[0] else slice(right.shape[0], None)
            left = jnp.concatenate([short[0], left[:, at]], axis=1)
            right = jnp.concatenate([short[1], right], axis=0)
            short = None
        product = dot(left, right)
        depth = product.shape[1] // 2
        product = product[:, :depth] + product[:, depth:]
        total = product if total is None else total + product
    return total


def begin_kernel(earlier, place, *refs):
    *pieces, out = refs
    total = product_of(pieces[earlier:], out.shape[0])
    out[...] = pieces[0][...] + total if earlier else total


def update_kernel(place, begun, *refs):
    *pieces, update, sent = refs
    total = DAMPING * (begun[...] + product_of(pieces, begun.shape[0]))
    update[...] = total
    sent[...] = total.astype(BF16)


def change_kernel(counts, turned, place, sent, *refs):
    at = 0
    for count, out in zip(counts, refs[sum(counts):]):
        rows = refs[at][...] if count == 1 else jnp.concatenate([f[...] for f in refs[at:at + count]], axis=0)
        if turned:
            part = rows.shape[0] // 2
            rows = jnp.concatenate([rows[part:], rows[:part]], axis=0)
        out[...] = dot_nt(sent[...], rows).astype(out.dtype)
        at += count


def apply_kernel(which, place, predictions, change, *refs):
    new, total, sems = refs[-3:]
    width, part = total.shape[0], total.shape[1] // 2
    copies = []
    for j in (0, 1):
        at, there = lanes(2 * (place[1] ^ which) + (place[2] ^ j), part), slice(j * part, (j + 1) * part)
        total[:, there] = predictions[:, at] + change[:width, there].astype(F32)
        copies.append(pltpu.make_async_copy(total.at[:, there], new.at[:, at], sems.at[j]))
        copies[j].start()
    for copy in copies:
        copy.wait()


def swap(x, axes, pairs):
    return lax.ppermute(x, axes, [p for a, b in pairs for p in ((a, b), (b, a))])


def after(arrays, *others):
    return lax.optimization_barrier((*arrays, *others))[:len(arrays)]


def ring_shards(n_rows, inputs, projection, phases, inverse_blocks, labels, predictions, coefficients):
    ring = [2 * z for z in range(n_rows)] + [2 * z + 1 for z in reversed(range(n_rows))]
    size = len(ring)
    even = [(ring[i], ring[i + 1]) for i in range(0, size, 2)]
    odd = [(ring[i], ring[(i + 1) % size]) for i in range(1, size, 2)]
    ways = [[(2 * a + c, 2 * b + c) for c, pairs in enumerate(way) for a, b in pairs]
            for way in ((even, odd), (odd, even))]
    S = lambda x: swap(x, ("rows", "blocks", "cols"), ways[0])
    T = lambda x: swap(x, ("rows", "blocks", "cols"), ways[1])
    C = lambda x: swap(x, "cols", [(0, 1)])

    place = jnp.stack([lax.axis_index(a) for a in ("rows", "blocks", "cols")]).astype(jnp.int32)
    local_rows, width = predictions.shape
    part = local_rows // 4
    padded = -(-width // LANES) * LANES
    predictions, coefficients = predictions.T, coefficients.T
    depth = coefficients.shape[1]

    dma = pltpu.SemaphoreType.DMA
    block_rows = like((2 * part, inputs.shape[1]))
    x0, own, given = call(
        prepare_kernel, (block_rows, *(like((padded, 2 * part)),) * 2), place,
        tuple(pltpu.with_memory_space_constraint(a, pltpu.HBM) for a in (inputs, labels[None, :], predictions)),
        "prepare", 6,
        (pltpu.VMEM((width, 2 * part), F32), pltpu.VMEM((1, 2 * part), jnp.int32), dma((6,))), (pltpu.HBM,) * 3,
    )
    given = C(given)
    (x0,) = after((x0,), given)
    r0 = jnp.concatenate([own, given], axis=0)
    weights = (projection, C(projection))
    phases = phases[None, :]
    phases = (phases, C(phases))
    inverse = call(round_kernel, like(inverse_blocks.shape[1:]), place, (inverse_blocks[0],), "round", 10)

    def block(rows, size):
        scratch = (pltpu.VMEM((size, 2 * projection.shape[1]), BF16),)
        return call(
            block_kernel, (like((size, 2 * depth)), like((size, depth))), place,
            (rows, *weights, *phases, inverse), "block", 16, scratch,
        )

    def begin(pairs, *earlier):
        return call(
            functools.partial(begin_kernel, len(earlier)), like((padded, depth), F32), place,
            (*earlier, *[a for pair in pairs for a in pair]), "begin", 14,
        )

    x1, r1 = S(x0), S(r0)
    q0, f0 = block(x0, part)
    (x1,) = after((x1,), q0)
    theirs = lambda r: C(r[padded:])

    def onward(way, rows, residual, size, begun, earlier):
        feats, f = call(
            features_kernel, (like((size, inverse.shape[1])), like((size, depth))), place,
            (rows, *weights, *phases), "features", 14,
        )
        (rows,) = after((rows,), f)
        further = way(rows[:part] if way is last else rows)
        q = call(meet_kernel, like((size, 2 * depth)), place, (feats, inverse), "meet", 14)
        (residual,) = after((residual,), q)
        q_other = C(q)
        further_residual = way(residual[:, :part] if way is last else residual)
        begun = begin([*earlier, (residual, q), (theirs(residual), q_other)], *begun)
        return q, f, further, further_residual, begun

    last = lambda x: T(x)
    q0_other, f0_other = C(q0), C(f0)
    q1, f1, x2, r2, begun = onward(T, x1, r1, 2 * part, (), [(r0, q0), (r0, q0_other)])
    (x2,) = after((x2,), q1, f0_other)
    (r2,) = after((r2,), begun)
    q2, f2, x3, r3, begun = onward(S, x2, r2, 2 * part, (begun,), [])
    (x3,) = after((x3,), q2)
    (r3,) = after((r3,), begun)
    q3, f3, x4, r4, begun = onward(last, x3, r3, 2 * part, (begun,), [])
    (x4,) = after((x4,), q3)
    q4, f4 = block(x4, part)
    f4_other = C(f4)
    (begun,) = after((begun,), f4_other)
    update, sent = call(
        update_kernel, (like((padded, depth), F32), like((padded, depth))), place,
        (begun, r4, q4, theirs(r4), C(q4)), "update", 14,
    )

    whole, wide = like((padded, 2 * part)), like((padded, 2 * part), F32)

    def changes(update, blocks, outs, turned=False):
        counts = tuple(len(f) for f in blocks)
        return call(
            functools.partial(change_kernel, counts, turned), outs, place, (update, *[f for b in blocks for f in b]), "change", 8
        )

    hop = lambda ahead, came: (ahead + came.astype(F32)).astype(BF16)
    first = dot_nt(sent, jnp.concatenate([f4, f4_other], axis=0)).astype(BF16)
    (sent_other,) = after((C(sent),), first)
    ahead = changes(after((sent,), first)[0], [(f3,), (f2,), (f1,), (f0, f0_other)], (wide,) * 4)
    first = T(first)
    (sent_other,) = after((sent_other,), *ahead)
    second, *behind = changes(sent_other, [(f3,), (f2,), (f1,)], (whole, wide, wide), True)
    (first,) = after((first,), second)
    second = S(second)
    for i, (way, back) in enumerate(((S, T), (T, S), (S, None))):
        total = hop(ahead[i], first)
        first = way(total)
        (second,) = after((second,), total)
        if back:
            total = hop(behind[i], second)
            second = back(total)
            (first,) = after((first,), total)
    given = C(second)
    (first,) = after((first,), given)
    own = (ahead[3] + first.astype(F32) + given.astype(F32)).astype(BF16)
    new = None
    for i in (0, 1):
        change = swap(own, "blocks", [(0, 1)]) if i else own
        earlier = (new,) if i else ()
        new = call(
            functools.partial(apply_kernel, i), like(predictions.shape, F32), place,
            (predictions, change, *earlier), "apply", 6, (pltpu.VMEM((width, 2 * part), F32), dma((2,))),
            (pltpu.VMEM, pltpu.VMEM, *(pl.ANY,) * i), pl.ANY, {3: 0} if i else {},
        )
    return (coefficients + update[:width]).T, new.T


def plain_shards(inputs, projection, phases, inverse_blocks, labels, predictions, coefficients):
    out_width = predictions.shape[1]
    classes = lax.axis_index("cols") * out_width + jnp.arange(out_width, dtype=jnp.int32)
    onehot = (labels[:, None] == classes[None, :]).astype(F32)
    residual = (onehot - predictions).astype(BF16)
    angles = dot(inputs, projection) + phases.astype(F32)[None, :]
    half_features = jnp.cos(angles).astype(BF16)
    features_full = lax.all_gather(half_features, "cols", axis=1, tiled=True)
    own_gradient = lax.psum_scatter(
        lax.dot_general(features_full, residual, (((0,), (0,)), ((), ())), preferred_element_type=F32),
        "rows", scatter_dimension=0, tiled=True,
    )
    gradient_full = lax.all_gather(own_gradient, "rows", axis=0, tiled=True)
    update = DAMPING * jnp.dot(inverse_blocks[0], gradient_full, precision=lax.Precision.HIGHEST)
    sent = lax.all_gather(update.astype(BF16), "rows", axis=0, tiled=True)
    summed = lax.psum(dot(features_full, sent), "blocks")
    return coefficients + update, predictions + summed


def solution(mesh):
    n_rows, n_blocks = mesh.shape["rows"], mesh.shape["blocks"]
    small_ring = n_blocks == 2 and n_rows == 4 and mesh.shape["cols"] == 2
    shards = functools.partial(ring_shards, n_rows) if small_ring else plain_shards
    return jax.shard_map(
        shards,
        mesh=mesh,
        in_specs=(
            P(("groups", "rows"), None),
            P(None, ("groups", "blocks", "cols")),
            P(("groups", "blocks", "cols")),
            P(("groups", "blocks"), "rows", None),
            P(("groups", "rows")),
            P(("groups", "rows"), "cols"),
            P(("groups", "blocks", "rows"), "cols"),
        ),
        out_specs=(P(("groups", "blocks", "rows"), "cols"), P(("groups", "rows"), "cols")),
        check_vma=False,
    )
```

```python
import functools

import jax
import jax.numpy as jnp
from jax import lax
from jax.experimental import pallas as pl
from jax.experimental.pallas import tpu as pltpu
from jax.sharding import PartitionSpec as P

DAMPING = 0.5
F32, BF16 = jnp.float32, jnp.bfloat16
LANES = 128

SINE_TERMS = (
    6.283185280127733, -41.341680582549685, 81.60247253767959, -76.5810396203459, 39.75848375303386
)
TURNS = 0.15915494309189535


def cosine(angles, phases):
    turns = angles * TURNS + phases.astype(F32) * TURNS
    quarter = 0.25 - jnp.abs(turns - jnp.round(turns))
    square = quarter * quarter
    result = square * SINE_TERMS[-1] + SINE_TERMS[-2]
    for term in SINE_TERMS[-3::-1]:
        result = result * square + term
    return result * quarter


def dot(a, b):
    return jnp.dot(a, b, preferred_element_type=F32)


def dot_nt(a, b):
    return lax.dot_general(a, b, (((1,), (1,)), ((), ())), preferred_element_type=F32)


def call(kernel, out_shapes, place, args, name, vmem_mib, scratch=(), in_place=None, out_place=pltpu.VMEM, aliases={}):
    spaces = in_place or (pltpu.VMEM,) * len(args)
    vmem = pl.BlockSpec(memory_space=out_place)
    single = isinstance(out_shapes, jax.ShapeDtypeStruct)
    return pl.pallas_call(
        kernel,
        out_shape=out_shapes,
        in_specs=[pl.BlockSpec(memory_space=m) for m in (pltpu.SMEM, *spaces)],
        out_specs=vmem if single else (vmem,) * len(out_shapes),
        scratch_shapes=scratch,
        input_output_aliases=aliases,
        compiler_params=pltpu.CompilerParams(vmem_limit_bytes=vmem_mib << 20),
        name=name,
    )(place, *args)


def like(shape, dtype=BF16):
    return jax.ShapeDtypeStruct(tuple(shape), dtype)


def lanes(index, size):
    return pl.ds(pl.multiple_of(index * size, size), size)


def prepare_kernel(place, inputs, labels, predictions, rows, own, given, wide, tags, sems):
    width = predictions.shape[0]
    part = own.shape[1] // 2
    copies = []
    for j in (0, 1):
        block = 2 * place[1] + (place[2] ^ j)
        at, there = lanes(block, part), slice(j * part, (j + 1) * part)
        copies += [
            pltpu.make_async_copy(predictions.at[:, at], wide.at[:, there], sems.at[3 * j]),
            pltpu.make_async_copy(labels.at[:, at], tags.at[:, there], sems.at[3 * j + 1]),
            pltpu.make_async_copy(inputs.at[at], rows.at[there], sems.at[3 * j + 2]),
        ]
    for copy in copies:
        copy.start()
    tail = own.shape[0] - width
    own[width:], given[width:] = (jnp.zeros((tail, 2 * part), BF16),) * 2
    for j in (0, 1):
        copies[3 * j].wait()
        copies[3 * j + 1].wait()
        there = slice(j * part, (j + 1) * part)
        classes = lax.broadcasted_iota(jnp.int32, (width, part), 0) + place[2] * width
        residual = ((classes == tags[:, there]).astype(F32) - wide[:, there]).astype(BF16)
        own[:width, there] = residual
        given[:width, (1 - j) * part:(2 - j) * part] = residual
    for j in (0, 1):
        copies[3 * j + 2].wait()


def high_low(x):
    high = x.astype(BF16)
    return high, (x - high.astype(F32)).astype(BF16)


def round_kernel(place, x, out):
    out[...] = x[...].astype(BF16)


TILE = 512


def block_kernel(place, rows, w_own, w_other, p_own, p_other, inverse, out, own_slice, feats):
    inputs = rows[:feats.shape[0]]
    half, depth = w_own.shape[1], inverse.shape[0]
    total = None
    for i, (weights, phases) in enumerate(((w_own, p_own), (w_other, p_other))):
        for k in range(0, half, TILE):
            at = pl.ds(pl.multiple_of((place[2] ^ i) * half + k, TILE), TILE)
            tile = cosine(dot(inputs, weights[:, k:k + TILE]), phases[:, k:k + TILE]).astype(BF16)
            feats[:, at] = tile
            product = dot_nt(tile, inverse[:, at])
            total = product if total is None else total + product
    out[:, :depth], out[:, depth:] = high_low(total)
    own_slice[...] = feats[:, lanes(place[0], depth)]


def features_kernel(place, rows, w_own, w_other, p_own, p_other, feats, own_slice):
    half = w_own.shape[1]
    for i, (weights, phases) in enumerate(((w_own, p_own), (w_other, p_other))):
        for k in range(0, half, TILE):
            at = pl.ds(pl.multiple_of((place[2] ^ i) * half + k, TILE), TILE)
            feats[:, at] = cosine(dot(rows[...], weights[:, k:k + TILE]), phases[:, k:k + TILE]).astype(BF16)
    own_slice[...] = feats[:, lanes(place[0], own_slice.shape[1])]


def meet_kernel(place, feats, inverse, out):
    depth = inverse.shape[0]
    out[:, :depth], out[:, depth:] = high_low(dot_nt(feats[...], inverse[...]))


def product_of(refs, classes):
    total, short = None, None
    for residual, q in zip(refs[::2], refs[1::2]):
        left, right = residual[:classes], q[...]
        if right.shape[0] < 256:
            if short is None:
                short = left[:, :right.shape[0]], right
                continue
            at = slice(0, right.shape[0]) if left.shape[1] == right.shape[0] else slice(right.shape[0], None)
            left = jnp.concatenate([short[0], left[:, at]], axis=1)
            right = jnp.concatenate([short[1], right], axis=0)
            short = None
        product = dot(left, right)
        depth = product.shape[1] // 2
        product = product[:, :depth] + product[:, depth:]
        total = product if total is None else total + product
    return total


def begin_kernel(earlier, place, *refs):
    *pieces, out = refs
    total = product_of(pieces[earlier:], out.shape[0])
    out[...] = pieces[0][...] + total if earlier else total


def change_kernel(counts, turned, place, sent, *refs):
    at = 0
    for count, out in zip(counts, refs[sum(counts):]):
        rows = refs[at][...] if count == 1 else jnp.concatenate([f[...] for f in refs[at:at + count]], axis=0)
        if turned:
            part = rows.shape[0] // 2
            rows = jnp.concatenate([rows[part:], rows[:part]], axis=0)
        out[...] = dot_nt(sent[...], rows).astype(out.dtype)
        at += count


def apply_kernel(which, place, predictions, change, *refs):
    new, total, sems = refs[-3:]
    width, part = total.shape[0], total.shape[1] // 2
    copies = []
    for j in (0, 1):
        at, there = lanes(2 * (place[1] ^ which) + (place[2] ^ j), part), slice(j * part, (j + 1) * part)
        total[:, there] = predictions[:, at] + change[:width, there].astype(F32)
        copies.append(pltpu.make_async_copy(total.at[:, there], new.at[:, at], sems.at[j]))
        copies[j].start()
    for copy in copies:
        copy.wait()


def swap(x, axes, pairs):
    return lax.ppermute(x, axes, [p for a, b in pairs for p in ((a, b), (b, a))])


def after(arrays, *others):
    return lax.optimization_barrier((*arrays, *others))[:len(arrays)]


def ring_shards(n_rows, inputs, projection, phases, inverse_blocks, labels, predictions, coefficients):
    ring = [2 * z for z in range(n_rows)] + [2 * z + 1 for z in reversed(range(n_rows))]
    size = len(ring)
    even = [(ring[i], ring[i + 1]) for i in range(0, size, 2)]
    odd = [(ring[i], ring[(i + 1) % size]) for i in range(1, size, 2)]
    ways = [[(2 * a + c, 2 * b + c) for c, pairs in enumerate(way) for a, b in pairs]
            for way in ((even, odd), (odd, even))]
    S = lambda x: swap(x, ("rows", "blocks", "cols"), ways[0])
    T = lambda x: swap(x, ("rows", "blocks", "cols"), ways[1])
    C = lambda x: swap(x, "cols", [(0, 1)])

    place = jnp.stack([lax.axis_index(a) for a in ("rows", "blocks", "cols")]).astype(jnp.int32)
    local_rows, width = predictions.shape
    part = local_rows // 4
    padded = -(-width // LANES) * LANES
    predictions, coefficients = predictions.T, coefficients.T
    depth = coefficients.shape[1]

    dma = pltpu.SemaphoreType.DMA
    block_rows = like((2 * part, inputs.shape[1]))
    x0, own, given = call(
        prepare_kernel, (block_rows, *(like((padded, 2 * part)),) * 2), place,
        tuple(pltpu.with_memory_space_constraint(a, pltpu.HBM) for a in (inputs, labels[None, :], predictions)),
        "prepare", 6,
        (pltpu.VMEM((width, 2 * part), F32), pltpu.VMEM((1, 2 * part), jnp.int32), dma((6,))), (pltpu.HBM,) * 3,
    )
    given = C(given)
    (x0,) = after((x0,), given)
    r0 = jnp.concatenate([own, given], axis=0)
    weights = (projection, C(projection))
    phases = phases[None, :]
    phases = (phases, C(phases))
    inverse = call(round_kernel, like(inverse_blocks.shape[1:]), place, (inverse_blocks[0],), "round", 10)

    def block(rows, size):
        scratch = (pltpu.VMEM((size, 2 * projection.shape[1]), BF16),)
        return call(
            block_kernel, (like((size, 2 * depth)), like((size, depth))), place,
            (rows, *weights, *phases, inverse), "block", 16, scratch,
        )

    def begin(pairs, *earlier):
        return call(
            functools.partial(begin_kernel, len(earlier)), like((padded, depth), F32), place,
            (*earlier, *[a for pair in pairs for a in pair]), "begin", 14,
        )

    x1, r1 = S(x0), S(r0)
    q0, f0 = block(x0, part)
    (x1,) = after((x1,), q0)
    theirs = lambda r: C(r[padded:])

    def onward(way, rows, residual, size, begun, earlier):
        feats, f = call(
            features_kernel, (like((size, inverse.shape[1])), like((size, depth))), place,
            (rows, *weights, *phases), "features", 14,
        )
        (rows,) = after((rows,), f)
        further = way(rows[:part] if way is last else rows)
        q = call(meet_kernel, like((size, 2 * depth)), place, (feats, inverse), "meet", 14)
        (residual,) = after((residual,), q)
        q_other = C(q)
        further_residual = way(residual[:, :part] if way is last else residual)
        begun = begin([*earlier, (residual, q), (theirs(residual), q_other)], *begun)
        return q, f, further, further_residual, begun

    last = lambda x: T(x)
    q0_other, f0_other = C(q0), C(f0)
    q1, f1, x2, r2, begun = onward(T, x1, r1, 2 * part, (), [(r0, q0), (r0, q0_other)])
    (x2,) = after((x2,), q1, f0_other)
    (r2,) = after((r2,), begun)
    q2, f2, x3, r3, begun = onward(S, x2, r2, 2 * part, (begun,), [])
    (x3,) = after((x3,), q2)
    (r3,) = after((r3,), begun)
    q3, f3, x4, r4, begun = onward(last, x3, r3, 2 * part, (begun,), [])
    (x4,) = after((x4,), q3)
    q4, f4 = block(x4, part)
    f4_other = C(f4)
    (begun,) = after((begun,), f4_other)
    ends = [(r4[:padded], q4), (theirs(r4), C(q4))]
    total = dot(*[jnp.concatenate(side, axis=1 - i) for i, side in enumerate(zip(*ends))])
    update = DAMPING * (begun + (total[:, :depth] + total[:, depth:]))
    sent = update.astype(BF16)

    whole, wide = like((padded, 2 * part)), like((padded, 2 * part), F32)

    def changes(update, blocks, outs, turned=False):
        counts = tuple(len(f) for f in blocks)
        return call(
            functools.partial(change_kernel, counts, turned), outs, place, (update, *[f for b in blocks for f in b]), "change", 8
        )

    hop = lambda ahead, came: (ahead + came.astype(F32)).astype(BF16)
    first = dot_nt(sent, jnp.concatenate([f4, f4_other], axis=0)).astype(BF16)
    (sent_other,) = after((C(sent),), first)
    ahead = changes(after((sent,), first)[0], [(f3,), (f2,), (f1,), (f0, f0_other)], (wide,) * 4)
    first = T(first)
    (sent_other,) = after((sent_other,), *ahead)
    second, *behind = changes(sent_other, [(f3,), (f2,), (f1,)], (whole, wide, wide), True)
    (first,) = after((first,), second)
    second = S(second)
    for i, (way, back) in enumerate(((S, T), (T, S), (S, None))):
        total = hop(ahead[i], first)
        first = way(total)
        (second,) = after((second,), total)
        if back:
            total = hop(behind[i], second)
            second = back(total)
            (first,) = after((first,), total)
    given = C(second)
    (first,) = after((first,), given)
    own = (ahead[3] + first.astype(F32) + given.astype(F32)).astype(BF16)
    new = None
    for i in (0, 1):
        change = swap(own, "blocks", [(0, 1)]) if i else own
        earlier = (new,) if i else ()
        new = call(
            functools.partial(apply_kernel, i), like(predictions.shape, F32), place,
            (predictions, change, *earlier), "apply", 6, (pltpu.VMEM((width, 2 * part), F32), dma((2,))),
            (pltpu.VMEM, pltpu.VMEM, *(pl.ANY,) * i), pl.ANY, {3: 0} if i else {},
        )
    return (coefficients + update[:width]).T, new.T


def plain_shards(inputs, projection, phases, inverse_blocks, labels, predictions, coefficients):
    out_width = predictions.shape[1]
    classes = lax.axis_index("cols") * out_width + jnp.arange(out_width, dtype=jnp.int32)
    onehot = (labels[:, None] == classes[None, :]).astype(F32)
    residual = (onehot - predictions).astype(BF16)
    angles = dot(inputs, projection) + phases.astype(F32)[None, :]
    half_features = jnp.cos(angles).astype(BF16)
    features_full = lax.all_gather(half_features, "cols", axis=1, tiled=True)
    own_gradient = lax.psum_scatter(
        lax.dot_general(features_full, residual, (((0,), (0,)), ((), ())), preferred_element_type=F32),
        "rows", scatter_dimension=0, tiled=True,
    )
    gradient_full = lax.all_gather(own_gradient, "rows", axis=0, tiled=True)
    update = DAMPING * jnp.dot(inverse_blocks[0], gradient_full, precision=lax.Precision.HIGHEST)
    sent = lax.all_gather(update.astype(BF16), "rows", axis=0, tiled=True)
    summed = lax.psum(dot(features_full, sent), "blocks")
    return coefficients + update, predictions + summed


def solution(mesh):
    n_rows, n_blocks = mesh.shape["rows"], mesh.shape["blocks"]
    small_ring = n_blocks == 2 and n_rows == 4 and mesh.shape["cols"] == 2
    shards = functools.partial(ring_shards, n_rows) if small_ring else plain_shards
    return jax.shard_map(
        shards,
        mesh=mesh,
        in_specs=(
            P(("groups", "rows"), None),
            P(None, ("groups", "blocks", "cols")),
            P(("groups", "blocks", "cols")),
            P(("groups", "blocks"), "rows", None),
            P(("groups", "rows")),
            P(("groups", "rows"), "cols"),
            P(("groups", "blocks", "rows"), "cols"),
        ),
        out_specs=(P(("groups", "blocks", "rows"), "cols"), P(("groups", "rows"), "cols")),
        check_vma=False,
    )
```
